512 devices in a mesh: gx: 16 (over z_hi, x), gy: 8 (over z_lo, core), gz: 4 (over y).
Axes of the slice: x: 4, y: 4, z: 16 (z_hi: 4, z_lo: 4; z = z_hi * 4 + z_lo), core: 2. Of those that a mesh axis runs over, the one named last changes fastest.
Arguments:
- noise: float32 [128, 256, 512], P('gx', 'gy', 'gz'), may hold values from -6 to 6
- kappa_sq: float32 [128, 256, 512], P('gx', 'gy', 'gz'), may hold values from 0.25 to 2
- cuts: int32 [18], replicated, may hold values from 0 to 96, as said below
- pressure_init: float32 [160, 256, 512], P('gx', 'gy', 'gz'), may hold values from -6 to 6
- source: float32 [160, 256, 512], P('gx', 'gy', 'gz'), may hold values from -24 to 24
Outputs:
- field: float32 [128, 256, 512], P('gx', 'gy', 'gz')
- pressure: float32 [160, 256, 512], P('gx', 'gy', 'gz')
The draws below stay inside these ranges and needn't reach their ends.
Inputs may be any that keep to these rules, and one draw needn't show every extreme that they name: cuts[0] lies within 2 of 16; cuts[1] = 0 and cuts[17] = 96; cuts[i+1] lies within 2 of i * 6; in every draw some flow tile holds exactly 10 inset planes.
All inputs are finite; a program needn't handle non-finite values.
Results may differ from the reference program's by a relative error of at most 0.00002.
Values sent between devices are 32-bit elements; how exact they have to be, the bound alone decides.
No kernel may reach another device: no remote copies, remote signals or barrier semaphores. Data moves between devices by JAX's collectives and lax.ppermute only.
A program may use at most 64 MiB of HBM per device.

```python
import jax
import jax.numpy as jnp
from jax import lax

SWEEPS = 8
JACOBI = 8
NX = 128
NY = 256
NZ = 512
NX_IN = 96
FLOW_MEAN = 6
JITTER = 2
FLOW_MOST = 10
N_GX = 16


def draw_cuts(key, part):
    first_key, second_key, third_key = jax.random.split(jax.random.fold_in(key, 17), 3)
    inner = jax.random.randint(first_key, (N_GX - 1,), -JITTER, JITTER + 1)
    where_most = jax.random.randint(second_key, (), 0, N_GX - 2)
    inner = inner.at[where_most].set(-JITTER)
    inner = inner.at[where_most + 1].set(JITTER)
    middle = jnp.arange(1, N_GX, dtype=jnp.int32) * FLOW_MEAN + inner
    start = jax.random.randint(third_key, (1,), NX // 8 - JITTER, NX // 8 + JITTER + 1)
    return jnp.concatenate([start.astype(jnp.int32), jnp.zeros((1,), jnp.int32), middle.astype(jnp.int32), jnp.full((1,), NX_IN, jnp.int32)])


def level_of(stream_key, shape, shards, least, largest):
    def one(axis_at, blocks):
        heights = jax.random.uniform(jax.random.fold_in(jax.random.fold_in(stream_key, 6), axis_at), (blocks,), jnp.float32, least / len(shards), largest / len(shards))
        return jnp.repeat(jnp.exp(heights), shape[axis_at] // blocks).reshape((-1,) + (1,) * (len(shape) - axis_at - 1))

    level = one(*shards[0])
    for cut in shards[1:]:
        level = level * one(*cut)
    return level


def normal_values(stream_key, shape, width, most, cuts=(), held_as=jnp.bfloat16):
    values = width * jax.random.normal(stream_key, shape, jnp.float32)
    if cuts:
        values = values * level_of(stream_key, shape, cuts, -0.22, 0.18)
    return jnp.clip(values, -most, most).astype(held_as)


def setup_inputs(seed: int = 0) -> dict:
    key_list = jax.random.split(jax.random.key(seed), 6)
    noise = normal_values(key_list[0], (NX, NY, NZ), 1.0, 6.0, ((0, 16), (1, 8), (2, 4)), jnp.float32)
    kappa_sq = jnp.clip(0.25 + 1.75 * jax.random.uniform(key_list[1], (NX, NY, NZ), jnp.float32) ** level_of(key_list[1], (NX, NY, NZ), ((0, 16), (1, 8), (2, 4)), -0.2, 0.2), 0.25, 2.0)
    cuts = draw_cuts(jax.random.fold_in(key_list[5], 71), 0)
    pressure_init = normal_values(key_list[3], (N_GX * FLOW_MOST, NY, NZ), 1.0, 6.0, ((0, 16), (1, 8), (2, 4)), jnp.float32)
    source = normal_values(key_list[4], (N_GX * FLOW_MOST, NY, NZ), 4.0, 24.0, ((0, 16), (1, 8), (2, 4)), jnp.float32)
    return dict(noise=noise, kappa_sq=kappa_sq, cuts=cuts, pressure_init=pressure_init, source=source)


THETA = 7.125
DELTA = 6.875
LOG_GAIN = 2.0


def sweep_weights(count):
    ratio_base = THETA / DELTA
    ratio_now = 1.0 / ratio_base
    weights = []
    for index in range(count):
        ratio_next = 1.0 / (2.0 * ratio_base - ratio_now)
        weights.append((ratio_next * ratio_now, 2.0 * ratio_next / DELTA))
        ratio_now = ratio_next
    return weights


def apply_matern(values, kappa_sq):
    padded = jnp.pad(values, 1)
    beside = padded[2:, 1:-1, 1:-1] + padded[:-2, 1:-1, 1:-1]
    beside = beside + padded[1:-1, 2:, 1:-1] + padded[1:-1, :-2, 1:-1]
    beside = beside + padded[1:-1, 1:-1, 2:] + padded[1:-1, 1:-1, :-2]
    return (kappa_sq + 6.0) * values - beside


def six_sides(padded):
    return (padded[:-2, 1:-1, 1:-1], padded[2:, 1:-1, 1:-1],
            padded[1:-1, :-2, 1:-1], padded[1:-1, 2:, 1:-1],
            padded[1:-1, 1:-1, :-2], padded[1:-1, 1:-1, 2:])


def harmonic(own, other):
    return 2.0 * own * other / (own + other)


def reference(noise, kappa_sq, cuts, pressure_init, source):
    field = jnp.zeros_like(noise)
    resid = noise
    direction = noise / THETA
    for weight in sweep_weights(SWEEPS):
        field = field + direction
        resid = resid - apply_matern(direction, kappa_sq)
        direction = weight[0] * direction + weight[1] * resid
    bounds = cuts[1:]
    inner = lax.dynamic_slice_in_dim(field, cuts[0].astype(jnp.int32), NX_IN, 0)
    perm = jnp.exp(LOG_GAIN * inner)
    planes = jnp.arange(NX_IN, dtype=jnp.int32)
    tiles = jnp.sum((planes[:, None] >= bounds[None, 1:N_GX]).astype(jnp.int32), axis=1)
    rows = (tiles * FLOW_MOST + planes - bounds[tiles]).astype(jnp.int32)
    pressure = pressure_init[rows]
    charge = source[rows]
    perm_sides = six_sides(jnp.pad(perm, 1, mode="edge"))
    coupling = [harmonic(perm, other) for other in perm_sides]
    total = coupling[0] + coupling[1] + coupling[2] + coupling[3] + coupling[4] + coupling[5]
    for sweep in range(JACOBI):
        sides = six_sides(jnp.pad(pressure, 1))
        flux = charge + coupling[0] * sides[0] + coupling[1] * sides[1] + coupling[2] * sides[2]
        flux = flux + coupling[3] * sides[3] + coupling[4] * sides[4] + coupling[5] * sides[5]
        pressure = flux / total
    slots = jnp.arange(N_GX * FLOW_MOST, dtype=jnp.int32)
    owners = slots // FLOW_MOST
    offsets = slots - owners * FLOW_MOST
    counts = bounds[1:] - bounds[:-1]
    valid = offsets < counts[owners]
    plane_of = jnp.clip(bounds[owners] + offsets, 0, NX_IN - 1).astype(jnp.int32)
    flow = jnp.where(valid[:, None, None], pressure[plane_of], 0.0)
    return field, flow
```

```python
import jax
import jax.numpy as jnp
import numpy as np
from jax import lax
from jax.experimental import pallas as pl
from jax.experimental.pallas import tpu as pltpu
from jax.sharding import PartitionSpec as P

SWEEPS = 8
JACOBI = 8
THETA = 7.125
DELTA = 6.875
LOG_GAIN = 2.0

COUNT_X = 16
COUNT_Y = 8
COUNT_Z = 4
CX, CY, CZ = 8, 32, 128
INSET = 96
MOST = 10
MEAN = 6
JIT = 2
DEPTH = 8
WIN = MOST + 2 * DEPTH
NH = SWEEPS - 1
NPL = CX + 2 * NH
KPL = NPL - 2
YN = CY + 32
YP = CY + 16

F32 = jnp.float32


def sweep_weights(count):
    ratio_base = THETA / DELTA
    ratio_now = 1.0 / ratio_base
    weights = []
    for index in range(count):
        ratio_next = 1.0 / (2.0 * ratio_base - ratio_now)
        weights.append((ratio_next * ratio_now, 2.0 * ratio_next / DELTA))
        ratio_now = ratio_next
    return weights


def retile_edges():
    first, last = NXC - JIT, NXC + JIT + INSET - 1
    edges = []
    for tile in range(COUNT_X):
        low = max(first, NXC - JIT + MEAN * tile - JIT - DEPTH)
        high = min(last, NXC + JIT + MEAN * (tile + 1) + JIT - 1 + DEPTH)
        for device in range(low // CX, high // CX + 1):
            if device != tile:
                edges.append((device, tile))
    return edges


NXC = CX * COUNT_X // 8


def coloured(edges):
    out_degree = [sum(e[0] == v for e in edges) for v in range(COUNT_X)]
    in_degree = [sum(e[1] == v for e in edges) for v in range(COUNT_X)]
    colours = max(out_degree + in_degree)
    sends = [[None] * colours for _ in range(COUNT_X)]
    takes = [[None] * colours for _ in range(COUNT_X)]
    for u, v in edges:
        a, b = sends[u].index(None), takes[v].index(None)
        if a != b:
            node, taking, colour, path = v, True, a, []
            while True:
                other = (takes if taking else sends)[node][colour]
                if other is None:
                    break
                path.append((node, taking, colour, other))
                node, taking, colour = other, not taking, b if colour == a else a
            for node, taking, colour, other in path:
                (takes if taking else sends)[node][colour] = None
                (sends if taking else takes)[other][colour] = None
            for node, taking, colour, other in path:
                swapped = b if colour == a else a
                (takes if taking else sends)[node][swapped] = other
                (sends if taking else takes)[other][swapped] = node
        sends[u][a], takes[v][a] = v, u
    pairs = [[(u, sends[u][c]) for u in range(COUNT_X) if sends[u][c] is not None] for c in range(colours)]
    table = np.array([[-1 if takes[v][c] is None else takes[v][c] for c in range(colours)] for v in range(COUNT_X)], np.int32)
    return pairs, table


PAIRS, TABLE = coloured(retile_edges())
COLOURS = len(PAIRS)
CUTS_AT = 3
FROM_AT = CUTS_AT + COUNT_X + 2


def cut(info, tile):
    return info[CUTS_AT + 1 + tile]


def clamp(value, low, high):
    return jnp.minimum(jnp.maximum(value, low), high)


def pick_kernel(info, noise, kappa, press, source, up1, dn1, up2, dn2):
    ix = info[0]
    width = cut(info, ix + 1) - cut(info, ix)
    up1[0:NH] = noise[CX - NH :]
    dn1[0:NH] = noise[:NH]
    up1[NH : 2 * NH - 1] = kappa[CX - NH + 1 :]
    dn1[NH : 2 * NH - 1] = kappa[: NH - 1]
    base = 2 * NH - 1
    for k in range(8):
        up1[base + k] = press[clamp(width - 8, 0, 2) + k]
        dn1[base + k] = press[k]
    for k in range(7):
        up1[base + 8 + k] = source[clamp(width - 7, 0, 3) + k]
        dn1[base + 8 + k] = source[k]
    for k in range(6):
        up2[k] = press[clamp(width - 6, 0, 4) + k]
        dn2[k] = press[k]
    for k in range(5):
        up2[6 + k] = source[clamp(width - 5, 0, 5) + k]
        dn2[6 + k] = source[k]


P1 = 2 * NH - 1 + 15
P2 = 11
YB = 2 * NPL + 2 * KPL + 2 * WIN


def join_x_kernel(info, noise, kappa, press, source, up1, dn1, up2, dn2, n_out, k_out, p_out, s_out, yup, ydn):
    ix = info[0]
    n_out[0:NH] = up1[0:NH]
    n_out[NH : NH + CX] = noise[...]
    n_out[NH + CX :] = dn1[0:NH]
    h = NH - 1
    k_out[0:h] = up1[NH : NH + h]
    k_out[h : h + CX] = kappa[...]
    k_out[h + CX :] = dn1[NH : NH + h]
    p_out[...] = jnp.zeros_like(p_out)
    s_out[...] = jnp.zeros_like(s_out)
    here = cut(info, ix)
    base = 2 * NH - 1

    def put(out, tile, row, value):
        known = (tile >= 0) & (tile < COUNT_X)
        safe = clamp(tile, 0, COUNT_X - 1)
        begin, end = cut(info, safe), cut(info, safe + 1)
        at = begin + row - here + DEPTH
        good = known & (begin + row < end) & (at >= 0) & (at < WIN)
        out[jnp.where(good, at, WIN)] = value

    def wide(tile):
        safe = clamp(tile, 0, COUNT_X - 1)
        return cut(info, safe + 1) - cut(info, safe)

    for k in range(MOST):
        put(p_out, ix, k, press[k])
        put(s_out, ix, k, source[k])
    for k in range(8):
        put(p_out, ix - 1, jnp.maximum(wide(ix - 1) - 8, 0) + k, up1[base + k])
        put(p_out, ix + 1, k, dn1[base + k])
    for k in range(7):
        put(s_out, ix - 1, jnp.maximum(wide(ix - 1) - 7, 0) + k, up1[base + 8 + k])
        put(s_out, ix + 1, k, dn1[base + 8 + k])
    for k in range(6):
        put(p_out, ix - 2, jnp.maximum(wide(ix - 2) - 6, 0) + k, up2[k])
        put(p_out, ix + 2, k, dn2[k])
    for k in range(5):
        put(s_out, ix - 2, jnp.maximum(wide(ix - 2) - 5, 0) + k, up2[6 + k])
        put(s_out, ix + 2, k, dn2[6 + k])
    at = 0
    for out, planes, halves in ((n_out, NPL, 2), (k_out, KPL, 2), (p_out, WIN, 1), (s_out, WIN, 1)):
        rows = 8 * halves
        for x in range(planes):
            for half in range(halves):
                yup[at] = out[x, CY - rows + 8 * half : CY - rows + 8 * half + 8]
                ydn[at] = out[x, 8 * half : 8 * half + 8]
                at += 1


def groups(planes, lanes):
    return -(-planes // (CZ // lanes))


ZPARTS = ((NPL, YN, 16), (KPL, YN, 16), (WIN, YP, 8), (WIN, YP, 8))
ZROWS = sum(groups(planes, lanes) * rows for planes, rows, lanes in ZPARTS)
ZSTART = [sum(groups(planes, lanes) * rows for planes, rows, lanes in ZPARTS[:k]) for k in range(4)]


def join_y_kernel(n_in, k_in, p_in, s_in, yup, ydn, n_out, k_out, p_out, s_out, zup, zdn):
    at = 0
    for src, out, planes, halves in ((n_in, n_out, NPL, 2), (k_in, k_out, KPL, 2), (p_in, p_out, WIN, 1), (s_in, s_out, WIN, 1)):
        rows = 8 * halves
        for x in range(planes):
            out[x, rows : rows + CY] = src[x]
            for half in range(halves):
                out[x, 8 * half : 8 * half + 8] = yup[at]
                out[x, rows + CY + 8 * half : rows + CY + 8 * half + 8] = ydn[at]
                at += 1
    for part, out in enumerate((n_out, k_out, p_out, s_out)):
        planes, rows, lanes = ZPARTS[part]
        each = CZ // lanes
        lane = lax.broadcasted_iota(jnp.int32, (rows, CZ), 1)
        for g in range(groups(planes, lanes)):
            up = jnp.zeros((rows, CZ), F32)
            dn = jnp.zeros((rows, CZ), F32)
            for k in range(each):
                x = g * each + k
                if x >= planes:
                    continue
                value = out[x]
                here = (lane >= lanes * k) & (lane < lanes * (k + 1))
                up = jnp.where(here, pltpu.roll(value, (lanes * k + lanes) % CZ, 1), up)
                turned = value if k == 0 else pltpu.roll(value, lanes * k, 1)
                dn = jnp.where(here, turned, dn)
            begin = ZSTART[part] + g * rows
            zup[begin : begin + rows] = up
            zdn[begin : begin + rows] = dn


def turn(value, shift, axis):
    shift %= value.shape[axis]
    return value if shift == 0 else pltpu.roll(value, shift, axis)


def z_halo(part, x, zup, zdn, lane):
    planes, rows, lanes = ZPARTS[part]
    each = CZ // lanes
    begin = ZSTART[part] + (x // each) * rows
    k = x % each
    above = turn(zdn[begin : begin + rows], -lanes * k, 1)
    below = turn(zup[begin : begin + rows], -lanes * (k + 1), 1)
    return jnp.where(lane < lanes, above, jnp.where(lane >= CZ - lanes, below, 0.0))


def chebyshev_kernel(info, n_in, k_in, zup, zdn, field, permp, resid, kap, da, db, acc):
    ix, iy, iz = info[0], info[1], info[2]
    lane = lax.broadcasted_iota(jnp.int32, (YN, CZ), 1)
    for x in range(NPL):
        resid[x, :, 0:CZ] = n_in[x]
        resid[x, :, CZ:] = z_halo(0, x, zup, zdn, lane)
    for x in range(KPL):
        kap[x, :, 0:CZ] = k_in[x] + 6.0
        kap[x, :, CZ:] = z_halo(1, x, zup, zdn, lane) + 6.0
    row = lax.broadcasted_iota(jnp.int32, (YN, 2 * CZ), 0)
    wide = lax.broadcasted_iota(jnp.int32, (YN, 2 * CZ), 1)
    inside = (row >= jnp.where(iy == 0, 16, 0)) & (row < jnp.where(iy == COUNT_Y - 1, 16 + CY, YN))
    inside &= (wide < jnp.where(iz == COUNT_Z - 1, CZ, CZ + 16)) | (wide >= jnp.where(iz == 0, 2 * CZ, 2 * CZ - 16))
    mask = jnp.where(inside, 1.0, 0.0).astype(F32)

    def first(x, _):
        da[x] = resid[x] / THETA
        return 0

    lax.fori_loop(0, NPL, first, 0)
    for x in range(CX):
        acc[x] = da[NH + x]
    old, new = da, db
    for k, (a, b) in enumerate(sweep_weights(SWEEPS)[: SWEEPS - 1], 1):
        def plane(x, _, old=old, new=new, a=a, b=b):
            d = old[x]
            beside = old[x + 1] + old[x - 1]
            beside = beside + (pltpu.roll(d, YN - 1, 0) + pltpu.roll(d, 1, 0))
            beside = beside + (pltpu.roll(d, 2 * CZ - 1, 1) + pltpu.roll(d, 1, 1))
            r = resid[x] - (kap[x - 1] * d - beside)
            resid[x] = r
            at = ix * CX - NH + x
            scale = jnp.where((at >= 0) & (at < CX * COUNT_X), b, 0.0).astype(F32)
            new[x] = a * d + (scale * mask) * r
            return 0

        lax.fori_loop(k, NPL - k, plane, 0)
        for x in range(CX):
            acc[x] += new[NH + x]
        old, new = new, old
    short = lax.broadcasted_iota(jnp.int32, (YP, CZ), 1)
    sides = jnp.zeros((YP, CZ), F32)
    for x in range(CX):
        field[x] = acc[x, 16 : 16 + CY, 0:CZ]
        permp[x] = jnp.exp(LOG_GAIN * acc[x, 8 : 8 + YP, 0:CZ])
        edge = jnp.exp(LOG_GAIN * acc[x, 8 : 8 + YP, CZ:])
        here = (short >= 16 * x) & (short < 16 * x + 16)
        sides = jnp.where(here, turn(edge, 16 * x + 8, 1), sides)
    permp[CX] = sides


def harmonic(own, other):
    return 2.0 * own * other / (own + other)


def jacobi_kernel(info, p_in, s_in, zup, zdn, mine, *rest):
    moved, out = rest[:COLOURS], rest[COLOURS]
    perm, pa, pb, sc, cxm, cxp, cym, cyp, czm, czp = rest[COLOURS + 1 :]
    ix, iy, iz = info[0], info[1], info[2]
    here = cut(info, ix)
    count = cut(info, ix + 1) - here
    lane = lax.broadcasted_iota(jnp.int32, (YP, CZ), 1)
    edges = (lane < 8) | (lane >= CZ - 8)

    def fill(q, _):
        perm[q] = jnp.ones((YP, 2 * CZ), F32)
        return 0

    lax.fori_loop(0, WIN + 1, fill, 0)
    for c in range(COLOURS + 1):
        block = mine if c == COLOURS else moved[c]
        device = ix if c == COLOURS else info[FROM_AT + c]
        sides = block[CX]
        for x in range(CX):
            g = device * CX + x - info[CUTS_AT]
            q = g - here + DEPTH
            good = (device >= 0) & (g >= 0) & (g < INSET) & (q >= 0) & (q < WIN)
            at = jnp.where(good, q, WIN)
            perm[at, :, 0:CZ] = block[x]
            perm[at, :, CZ:] = jnp.where(edges, turn(sides, -16 * x - 8, 1), 1.0)
    for x in range(WIN):
        pa[x, :, 0:CZ] = p_in[x]
        pa[x, :, CZ:] = z_halo(2, x, zup, zdn, lane)
        sc[x, :, 0:CZ] = s_in[x]
        sc[x, :, CZ:] = z_halo(3, x, zup, zdn, lane)

    row = lax.broadcasted_iota(jnp.int32, (YP, 2 * CZ), 0)
    wide = lax.broadcasted_iota(jnp.int32, (YP, 2 * CZ), 1)
    low_y, high_y = jnp.where(iy == 0, 8, 0), jnp.where(iy == COUNT_Y - 1, 8 + CY, YP)
    left = jnp.where(iz == 0, 2 * CZ, 2 * CZ - 8)
    right = jnp.where(iz == COUNT_Z - 1, CZ, CZ + 8)
    inside = (row >= low_y) & (row < high_y) & ((wide < right) | (wide >= left))
    one, zero = jnp.ones((YP, 2 * CZ), F32), jnp.zeros((YP, 2 * CZ), F32)
    has_ym = row != low_y
    has_yp = row != high_y - 1
    has_zm = wide != jnp.where(iz == 0, 0, 2 * CZ - 8)
    has_zp = wide != right - 1

    def couple(q, _):
        g = here + q - DEPTH
        own = perm[q]
        live = inside & (g >= 0) & (g < INSET)
        txm = jnp.where(g > 0, harmonic(own, perm[q - 1]), own)
        txp = jnp.where(g < INSET - 1, harmonic(own, perm[q + 1]), own)
        ty = harmonic(own, pltpu.roll(own, 1, 0))
        tz = harmonic(own, pltpu.roll(own, 1, 1))
        tym = jnp.where(has_ym, ty, own)
        typ = jnp.where(has_yp, pltpu.roll(ty, YP - 1, 0), own)
        tzm = jnp.where(has_zm, tz, own)
        tzp = jnp.where(has_zp, pltpu.roll(tz, 2 * CZ - 1, 1), own)
        total = txm + txp + tym + typ + tzm + tzp
        inv = jnp.where(live, one / total, zero)
        cxm[q] = jnp.where(g > 0, txm * inv, 0.0)
        cxp[q] = jnp.where(g < INSET - 1, txp * inv, 0.0)
        cym[q] = jnp.where(has_ym, tym * inv, 0.0)
        cyp[q] = jnp.where(has_yp, typ * inv, 0.0)
        czm[q] = jnp.where(has_zm, tzm * inv, 0.0)
        czp[q] = jnp.where(has_zp, tzp * inv, 0.0)
        sc[q] = sc[q] * inv
        return 0

    lax.fori_loop(1, WIN - 1, couple, 0)

    old, new = pa, pb
    for sweep in range(1, JACOBI + 1):
        def plane(q, _, old=old, new=new):
            p = old[q]
            total = sc[q] + cxm[q] * old[q - 1] + cxp[q] * old[q + 1]
            total = total + cym[q] * pltpu.roll(p, 1, 0) + cyp[q] * pltpu.roll(p, YP - 1, 0)
            total = total + czm[q] * pltpu.roll(p, 1, 1) + czp[q] * pltpu.roll(p, 2 * CZ - 1, 1)
            new[q] = total
            return 0

        lax.fori_loop(sweep, WIN - sweep, plane, 0)
        old, new = new, old
    for r in range(MOST):
        out[r] = jnp.where(r < count, old[DEPTH + r, 8 : 8 + CY, 0:CZ], 0.0)


def call(kernel, args, outs, scratch=(), scalars=1):
    smem = pl.BlockSpec(memory_space=pltpu.SMEM)
    vmem = pl.BlockSpec(memory_space=pltpu.VMEM)
    return pl.pallas_call(
        kernel,
        out_shape=[jax.ShapeDtypeStruct(shape, F32) for shape in outs],
        in_specs=[smem] * scalars + [vmem] * (len(args) - scalars),
        out_specs=[vmem] * len(outs),
        scratch_shapes=[pltpu.VMEM(shape, F32) for shape in scratch],
        compiler_params=pltpu.CompilerParams(vmem_limit_bytes=56 << 20),
    )(*args)


def shifted(value, axis, count, by):
    return lax.ppermute(value, axis, [(i, i + by) for i in range(count) if 0 <= i + by < count])


def local(noise, kappa_sq, cuts, pressure_init, source):
    ix = lax.axis_index("gx")
    spots = jnp.stack([ix, lax.axis_index("gy"), lax.axis_index("gz")]).astype(jnp.int32)
    origin = lax.dynamic_index_in_dim(jnp.asarray(TABLE), ix, 0, keepdims=False)
    info = jnp.concatenate([spots, cuts, origin])
    own = (noise, kappa_sq, pressure_init, source)
    one, two = (P1, CY, CZ), (P2, CY, CZ)
    up1, dn1, up2, dn2 = call(pick_kernel, (info, *own), [one, one, two, two])
    up1, dn1 = shifted(up1, "gx", COUNT_X, 1), shifted(dn1, "gx", COUNT_X, -1)
    up2, dn2 = shifted(up2, "gx", COUNT_X, 2), shifted(dn2, "gx", COUNT_X, -2)
    n, k, p, s, yup, ydn = call(
        join_x_kernel,
        (info, *own, up1, dn1, up2, dn2),
        [(NPL, CY, CZ), (KPL, CY, CZ), (WIN + 1, CY, CZ), (WIN + 1, CY, CZ), (YB, 8, CZ), (YB, 8, CZ)],
    )
    yup, ydn = shifted(yup, "gy", COUNT_Y, 1), shifted(ydn, "gy", COUNT_Y, -1)
    n, k, p, s, zup, zdn = call(
        join_y_kernel,
        (n, k, p, s, yup, ydn),
        [(NPL, YN, CZ), (KPL, YN, CZ), (WIN, YP, CZ), (WIN, YP, CZ), (ZROWS, CZ), (ZROWS, CZ)],
        scalars=0,
    )
    zup, zdn = shifted(zup, "gz", COUNT_Z, 1), shifted(zdn, "gz", COUNT_Z, -1)
    big = (NPL, YN, 2 * CZ)
    field, permp = call(
        chebyshev_kernel,
        (info, n, k, zup, zdn),
        [(CX, CY, CZ), (CX + 1, YP, CZ)],
        [big, (KPL, YN, 2 * CZ), big, big, (CX, YN, 2 * CZ)],
    )
    moved = [lax.ppermute(permp, "gx", pairs) for pairs in PAIRS]
    room = (WIN + 1, YP, 2 * CZ)
    (pressure,) = call(
        jacobi_kernel,
        (info, p, s, zup, zdn, permp, *moved),
        [(MOST, CY, CZ)],
        [room] * 10,
    )
    return (field, pressure)


def solution(mesh):
    placed = (P("gx", "gy", "gz"), P("gx", "gy", "gz"), P(), P("gx", "gy", "gz"), P("gx", "gy", "gz"))
    return jax.shard_map(
        local,
        mesh=mesh,
        in_specs=placed,
        out_specs=(P("gx", "gy", "gz"), P("gx", "gy", "gz")),
        check_vma=False,
    )
```

```python
import jax
import jax.numpy as jnp
from jax import lax
from jax.experimental import pallas as pl
from jax.experimental.pallas import tpu as pltpu
from jax.sharding import PartitionSpec as P

SWEEPS = 8
JACOBI = 8
THETA = 7.125
DELTA = 6.875
LOG_GAIN = 2.0

COUNT_X = 16
COUNT_Y = 8
COUNT_Z = 4
CX, CY, CZ = 8, 32, 128
INSET = 96
MOST = 10
DEPTH = 8
WIN = MOST + 2 * DEPTH
NH = SWEEPS - 1
NPL = CX + 2 * NH
KPL = NPL - 2
YE = CY + 16
RING = 4

F32 = jnp.float32


def sweep_weights(count):
    ratio_base = THETA / DELTA
    ratio_now = 1.0 / ratio_base
    weights = []
    for index in range(count):
        ratio_next = 1.0 / (2.0 * ratio_base - ratio_now)
        weights.append((ratio_next * ratio_now, 2.0 * ratio_next / DELTA))
        ratio_now = ratio_next
    return weights


CUTS_AT = 3


def cut(info, tile):
    return info[CUTS_AT + 1 + tile]


def clamp(value, low, high):
    return jnp.minimum(jnp.maximum(value, low), high)


def turn(value, shift, axis):
    shift %= value.shape[axis]
    return value if shift == 0 else pltpu.roll(value, shift, axis)


PN = 2 * NH - 1


def pick_slab_kernel(noise, kappa, up, dn):
    up[0:NH] = noise[CX - NH :]
    dn[0:NH] = noise[:NH]
    up[NH:] = kappa[CX - NH + 1 :]
    dn[NH:] = kappa[: NH - 1]


def pick_tile_kernel(info, press, source, up1, dn1, up2, dn2):
    ix = info[0]
    width = cut(info, ix + 1) - cut(info, ix)
    for k in range(8):
        up1[k] = press[clamp(width - 8, 0, 2) + k]
        dn1[k] = press[k]
    for k in range(7):
        up1[8 + k] = source[clamp(width - 7, 0, 3) + k]
        dn1[8 + k] = source[k]
    for k in range(6):
        up2[k] = press[clamp(width - 6, 0, 4) + k]
        dn2[k] = press[k]
    for k in range(5):
        up2[6 + k] = source[clamp(width - 5, 0, 5) + k]
        dn2[6 + k] = source[k]


def side_rows(parts, yup, ydn):
    at = 0
    for part, planes in parts:
        for x in range(planes):
            yup[at] = part[x, CY - 8 :]
            ydn[at] = part[x, 0:8]
            at += 1


def join_slab_kernel(noise, kappa, up, dn, n_out, k_out, yup, ydn):
    n_out[0:NH] = up[0:NH]
    n_out[NH : NH + CX] = noise[...]
    n_out[NH + CX :] = dn[0:NH]
    h = NH - 1
    k_out[0:h] = up[NH:]
    k_out[h : h + CX] = kappa[...]
    k_out[h + CX :] = dn[NH:]
    side_rows(((n_out, NPL), (k_out, KPL)), yup, ydn)


LANES = 8
EACH = CZ // LANES


def groups(planes):
    return -(-planes // EACH)


def join_y_kernel(plane_counts, *refs):
    count = len(plane_counts)
    sources, (yup, ydn), outs, (zup, zdn) = refs[:count], refs[count : count + 2], refs[count + 2 : -2], refs[-2:]
    lane = lax.broadcasted_iota(jnp.int32, (YE, CZ), 1)
    at, begin = 0, 0
    for source, out, planes in zip(sources, outs, plane_counts):
        for x in range(planes):
            out[x, 0:8] = yup[at]
            out[x, 8 : 8 + CY] = source[x]
            out[x, 8 + CY :] = ydn[at]
            at += 1
        for g in range(groups(planes)):
            up = jnp.zeros((YE, CZ), F32)
            dn = jnp.zeros((YE, CZ), F32)
            for k in range(min(EACH, planes - g * EACH)):
                value = out[g * EACH + k]
                here = (lane >= LANES * k) & (lane < LANES * (k + 1))
                up = jnp.where(here, turn(value, LANES * (k + 1), 1), up)
                dn = jnp.where(here, turn(value, LANES * k, 1), dn)
            zup[begin : begin + YE] = up
            zdn[begin : begin + YE] = dn
            begin += YE


def z_halo(start, x, zup, zdn, lane):
    begin = (start + x // EACH) * YE
    k = x % EACH
    above = turn(zdn[begin : begin + YE], -LANES * k, 1)
    below = turn(zup[begin : begin + YE], -LANES * (k + 1), 1)
    return jnp.where(lane < LANES, above, jnp.where(lane >= CZ - LANES, below, 0.0))


def inside_bounds(iy, iz):
    low_y = jnp.where(iy == 0, 8, 0)
    high_y = jnp.where(iy == COUNT_Y - 1, 8 + CY, YE)
    left = jnp.where(iz == 0, 2 * CZ, 2 * CZ - LANES)
    right = jnp.where(iz == COUNT_Z - 1, CZ, CZ + LANES)
    return low_y, high_y, left, right


def chebyshev_kernel(info, n_in, k_in, zup, zdn, field, perm, resid, kap, da, db, acc):
    ix, iy, iz = info[0], info[1], info[2]
    lane = lax.broadcasted_iota(jnp.int32, (YE, CZ), 1)
    for x in range(NPL):
        resid[x, :, 0:CZ] = n_in[x]
        resid[x, :, CZ:] = z_halo(0, x, zup, zdn, lane)
    for x in range(KPL):
        kap[x, :, 0:CZ] = k_in[x] + 6.0
        kap[x, :, CZ:] = z_halo(groups(NPL), x, zup, zdn, lane) + 6.0
    row = lax.broadcasted_iota(jnp.int32, (YE, 2 * CZ), 0)
    wide = lax.broadcasted_iota(jnp.int32, (YE, 2 * CZ), 1)
    low_y, high_y, left, right = inside_bounds(iy, iz)
    inside = (row >= low_y) & (row < high_y) & ((wide < right) | (wide >= left))
    mask = jnp.where(inside, 1.0, 0.0).astype(F32)

    def first(x, _):
        da[x] = resid[x] / THETA
        return 0

    lax.fori_loop(0, NPL, first, 0)
    for x in range(CX):
        acc[x] = da[NH + x]
    old, new = da, db
    for k, (a, b) in enumerate(sweep_weights(SWEEPS)[: SWEEPS - 1], 1):
        def plane(x, _, old=old, new=new, a=a, b=b):
            d = old[x]
            beside = old[x + 1] + old[x - 1]
            beside = beside + (pltpu.roll(d, YE - 1, 0) + pltpu.roll(d, 1, 0))
            beside = beside + (pltpu.roll(d, 2 * CZ - 1, 1) + pltpu.roll(d, 1, 1))
            r = resid[x] - (kap[x - 1] * d - beside)
            resid[x] = r
            at = ix * CX - NH + x
            scale = jnp.where((at >= 0) & (at < CX * COUNT_X), b, 0.0).astype(F32)
            new[x] = a * d + (scale * mask) * r
            return 0

        lax.fori_loop(k, NPL - k, plane, 0)
        for x in range(CX):
            acc[x] += new[NH + x]
        old, new = new, old
    for x in range(CX):
        value = acc[x, 8 : 8 + CY, 0:CZ]
        field[x] = value
        perm[x] = jnp.exp(LOG_GAIN * value)


def window(info, tile):
    first = info[CUTS_AT]
    return first + cut(info, tile) - DEPTH, first + cut(info, tile + 1) + DEPTH - 1


def ring_plane(info, tile, device, r):
    low, high = window(info, tile)
    above = (device + RING) * CX + r <= high
    below = (device - RING) * CX + r >= low
    return above, below


def ring_kernel(info, own, low, high, *outs):
    ix = info[0]
    place = lax.rem(ix, RING)
    for s, out in enumerate(outs, 1):
        tile = ix - place + lax.rem(place + s, RING)
        for r in range(CX):
            above, below = ring_plane(info, tile, ix, r)
            out[r] = jnp.where(above, high[r], jnp.where(below, low[r], own[r]))


def join_tile_kernel(info, own, low, high, ring1, ring2, ring3, press, source, up1, dn1, up2, dn2, w_out, p_out, s_out, yup, ydn):
    ix = info[0]
    place = lax.rem(ix, RING)
    here = cut(info, ix)
    w_out[...] = jnp.ones_like(w_out)
    p_out[...] = jnp.zeros_like(p_out)
    s_out[...] = jnp.zeros_like(s_out)
    for s, ring in enumerate((own, ring1, ring2, ring3)):
        device = ix - place + lax.rem(place + RING - s, RING)
        for r in range(CX):
            above, below = ring_plane(info, ix, device, r)
            value = jnp.where(above, high[r], jnp.where(below, low[r], own[r])) if s == 0 else ring[r]
            at = device + jnp.where(above, RING, jnp.where(below, -RING, 0))
            g = at * CX + r - info[CUTS_AT]
            q = g - here + DEPTH
            good = (g >= 0) & (g < INSET) & (q >= 0) & (q < WIN)
            w_out[jnp.where(good, q, WIN)] = value

    def put(out, tile, row, value):
        known = (tile >= 0) & (tile < COUNT_X)
        safe = clamp(tile, 0, COUNT_X - 1)
        begin, end = cut(info, safe), cut(info, safe + 1)
        at = begin + row - here + DEPTH
        good = known & (begin + row < end) & (at >= 0) & (at < WIN)
        out[jnp.where(good, at, WIN)] = value

    def skipped(tile, kept):
        safe = clamp(tile, 0, COUNT_X - 1)
        return jnp.maximum(cut(info, safe + 1) - cut(info, safe) - kept, 0)

    for k in range(MOST):
        put(p_out, ix, k, press[k])
        put(s_out, ix, k, source[k])
    for k in range(8):
        put(p_out, ix - 1, skipped(ix - 1, 8) + k, up1[k])
        put(p_out, ix + 1, k, dn1[k])
    for k in range(7):
        put(s_out, ix - 1, skipped(ix - 1, 7) + k, up1[8 + k])
        put(s_out, ix + 1, k, dn1[8 + k])
    for k in range(6):
        put(p_out, ix - 2, skipped(ix - 2, 6) + k, up2[k])
        put(p_out, ix + 2, k, dn2[k])
    for k in range(5):
        put(s_out, ix - 2, skipped(ix - 2, 5) + k, up2[6 + k])
        put(s_out, ix + 2, k, dn2[6 + k])
    side_rows(((w_out, WIN), (p_out, WIN), (s_out, WIN)), yup, ydn)


def harmonic(own, other):
    return 2.0 * own * other / (own + other)


def jacobi_kernel(info, w_in, p_in, s_in, zup, zdn, out, perm, pa, pb, sc, cxm, cxp, cym, cyp, czm, czp):
    ix, iy, iz = info[0], info[1], info[2]
    here = cut(info, ix)
    count = cut(info, ix + 1) - here
    lane = lax.broadcasted_iota(jnp.int32, (YE, CZ), 1)
    for part, (src, dst) in enumerate(((w_in, perm), (p_in, pa), (s_in, sc))):
        for x in range(WIN):
            dst[x, :, 0:CZ] = src[x]
            dst[x, :, CZ:] = z_halo(part * groups(WIN), x, zup, zdn, lane)

    row = lax.broadcasted_iota(jnp.int32, (YE, 2 * CZ), 0)
    wide = lax.broadcasted_iota(jnp.int32, (YE, 2 * CZ), 1)
    low_y, high_y, left, right = inside_bounds(iy, iz)
    inside = (row >= low_y) & (row < high_y) & ((wide < right) | (wide >= left))
    has_ym = row != low_y
    has_yp = row != high_y - 1
    has_zm = wide != jnp.where(iz == 0, 0, 2 * CZ - LANES)
    has_zp = wide != right - 1

    def couple(q, _):
        g = here + q - DEPTH
        own = perm[q]
        live = inside & (g >= 0) & (g < INSET)
        txm = jnp.where(g > 0, harmonic(own, perm[q - 1]), own)
        txp = jnp.where(g < INSET - 1, harmonic(own, perm[q + 1]), own)
        ty = harmonic(own, pltpu.roll(own, 1, 0))
        tz = harmonic(own, pltpu.roll(own, 1, 1))
        tym = jnp.where(has_ym, ty, own)
        typ = jnp.where(has_yp, pltpu.roll(ty, YE - 1, 0), own)
        tzm = jnp.where(has_zm, tz, own)
        tzp = jnp.where(has_zp, pltpu.roll(tz, 2 * CZ - 1, 1), own)
        total = txm + txp + tym + typ + tzm + tzp

        def share(has, part):
            return jnp.where(live & has, part / total, 0.0)

        cxm[q] = share(g > 0, txm)
        cxp[q] = share(g < INSET - 1, txp)
        cym[q] = share(has_ym, tym)
        cyp[q] = share(has_yp, typ)
        czm[q] = share(has_zm, tzm)
        czp[q] = share(has_zp, tzp)
        sc[q] = share(True, sc[q])
        return 0

    lax.fori_loop(1, WIN - 1, couple, 0)

    old, new = pa, pb
    for sweep in range(1, JACOBI + 1):
        def plane(q, _, old=old, new=new):
            p = old[q]
            total = sc[q] + cxm[q] * old[q - 1] + cxp[q] * old[q + 1]
            total = total + cym[q] * pltpu.roll(p, 1, 0) + cyp[q] * pltpu.roll(p, YE - 1, 0)
            total = total + czm[q] * pltpu.roll(p, 1, 1) + czp[q] * pltpu.roll(p, 2 * CZ - 1, 1)
            new[q] = total
            return 0

        lax.fori_loop(sweep, WIN - sweep, plane, 0)
        old, new = new, old
    for r in range(MOST):
        out[r] = jnp.where(r < count, old[DEPTH + r, 8 : 8 + CY, 0:CZ], 0.0)


def call(kernel, args, outs, scratch=(), scalars=1, cost=1 << 20):
    smem = pl.BlockSpec(memory_space=pltpu.SMEM)
    vmem = pl.BlockSpec(memory_space=pltpu.VMEM)
    return pl.pallas_call(
        kernel,
        out_shape=[jax.ShapeDtypeStruct(shape, F32) for shape in outs],
        in_specs=[smem] * scalars + [vmem] * (len(args) - scalars),
        out_specs=[vmem] * len(outs),
        scratch_shapes=[pltpu.VMEM(shape, F32) for shape in scratch],
        compiler_params=pltpu.CompilerParams(vmem_limit_bytes=56 << 20),
        cost_estimate=pl.CostEstimate(flops=64 * cost, transcendentals=0, bytes_accessed=cost),
    )(*args)


def shifted(value, axis, count, by):
    return lax.ppermute(value, axis, [(i, i + by) for i in range(count) if 0 <= i + by < count])


def ringed(value, s):
    return lax.ppermute(value, "gx", [(i, i - i % RING + (i + s) % RING) for i in range(COUNT_X)])


def join_y(plane_counts, parts, yup, ydn, beside=()):
    yup, ydn = shifted(yup, "gy", COUNT_Y, 1), shifted(ydn, "gy", COUNT_Y, -1)
    packed = (sum(groups(planes) for planes in plane_counts) * YE, CZ)

    def join_rows(*refs):
        join_y_kernel(plane_counts, *refs)

    *parts, zup, zdn = call(
        join_rows,
        (*parts, yup, ydn),
        [(planes, YE, CZ) for planes in plane_counts] + [packed, packed],
        scalars=0,
    )
    beside, zup, zdn = lax.optimization_barrier((beside, zup, zdn))
    return (*parts, shifted(zup, "gz", COUNT_Z, 1), shifted(zdn, "gz", COUNT_Z, -1)), beside


def local(noise, kappa_sq, cuts, pressure_init, source):
    spots = jnp.stack([lax.axis_index("gx"), lax.axis_index("gy"), lax.axis_index("gz")]).astype(jnp.int32)
    info = jnp.concatenate([spots, cuts])
    plane = (CY, CZ)
    up, dn = call(pick_slab_kernel, (noise, kappa_sq), [(PN, *plane)] * 2, scalars=0)
    up, dn = shifted(up, "gx", COUNT_X, 1), shifted(dn, "gx", COUNT_X, -1)
    n, k, yup, ydn = call(
        join_slab_kernel,
        (noise, kappa_sq, up, dn),
        [(NPL, *plane), (KPL, *plane), (NPL + KPL, 8, CZ), (NPL + KPL, 8, CZ)],
        scalars=0,
    )
    press, charge, n, k, yup, ydn = lax.optimization_barrier((pressure_init, source, n, k, yup, ydn))
    up1, dn1, up2, dn2 = call(pick_tile_kernel, (info, press, charge), [(15, *plane)] * 2 + [(11, *plane)] * 2)
    (n, k, zup, zdn), tile = join_y((NPL, KPL), (n, k), yup, ydn, (up1, dn1, up2, dn2))
    up1, dn1, up2, dn2 = tile
    up1, dn1 = shifted(up1, "gx", COUNT_X, 1), shifted(dn1, "gx", COUNT_X, -1)
    up2, dn2 = shifted(up2, "gx", COUNT_X, 2), shifted(dn2, "gx", COUNT_X, -2)
    big = (NPL, YE, 2 * CZ)
    field, perm = call(
        chebyshev_kernel,
        (info, n, k, zup, zdn),
        [(CX, *plane), (CX, *plane)],
        [big, (KPL, YE, 2 * CZ), big, big, (CX, YE, 2 * CZ)],
        cost=40 << 20,
    )
    perm, up1, dn1, up2, dn2 = lax.optimization_barrier((perm, up1, dn1, up2, dn2))
    low, high = shifted(perm, "gx", COUNT_X, RING), shifted(perm, "gx", COUNT_X, -RING)
    rings = call(ring_kernel, (info, perm, low, high), [(CX, *plane)] * (RING - 1))
    rings = [ringed(value, s) for s, value in enumerate(rings, 1)]
    rows = (3 * WIN, 8, CZ)
    w, p, s, yup, ydn = call(
        join_tile_kernel,
        (info, perm, low, high, *rings, pressure_init, source, up1, dn1, up2, dn2),
        [(WIN + 1, *plane)] * 3 + [rows, rows],
    )
    (w, p, s, zup, zdn), _ = join_y((WIN, WIN, WIN), (w, p, s), yup, ydn)
    room = (WIN + 1, YE, 2 * CZ)
    (pressure,) = call(jacobi_kernel, (info, w, p, s, zup, zdn), [(MOST, *plane)], [room] * 10)
    return (field, pressure)


def solution(mesh):
    placed = (P("gx", "gy", "gz"), P("gx", "gy", "gz"), P(), P("gx", "gy", "gz"), P("gx", "gy", "gz"))
    return jax.shard_map(
        local,
        mesh=mesh,
        in_specs=placed,
        out_specs=(P("gx", "gy", "gz"), P("gx", "gy", "gz")),
        check_vma=False,
    )
```

```python
import jax
import jax.numpy as jnp
from jax import lax
from jax.experimental import pallas as pl
from jax.experimental.pallas import tpu as pltpu
from jax.sharding import PartitionSpec as P

SWEEPS = 8
JACOBI = 8
THETA = 7.125
DELTA = 6.875
LOG_GAIN = 2.0

COUNT_X = 16
COUNT_Y = 8
COUNT_Z = 4
CX, CY, CZ = 8, 32, 128
INSET = 96
MOST = 10
DEPTH = 8
WIN = MOST + 2 * DEPTH
NH = SWEEPS - 1
NPL = CX + 2 * NH
KPL = NPL - 2
YE = CY + 16
RING = 4

F32 = jnp.float32


def sweep_weights(count):
    ratio_base = THETA / DELTA
    ratio_now = 1.0 / ratio_base
    weights = []
    for index in range(count):
        ratio_next = 1.0 / (2.0 * ratio_base - ratio_now)
        weights.append((ratio_next * ratio_now, 2.0 * ratio_next / DELTA))
        ratio_now = ratio_next
    return weights


CUTS_AT = 3


def cut(info, tile):
    return info[CUTS_AT + 1 + tile]


def clamp(value, low, high):
    return jnp.minimum(jnp.maximum(value, low), high)


def turn(value, shift, axis):
    shift %= value.shape[axis]
    return value if shift == 0 else pltpu.roll(value, shift, axis)


PN = 2 * NH - 1


def pick_slab_kernel(noise, kappa, up, dn):
    up[0:NH] = noise[CX - NH :]
    dn[0:NH] = noise[:NH]
    up[NH:] = kappa[CX - NH + 1 :]
    dn[NH:] = kappa[: NH - 1]


def pick_tile_kernel(info, press, source, up1, dn1, far2, near2):
    ix = info[0]
    width = cut(info, ix + 1) - cut(info, ix)
    late = lax.rem(ix, RING) >= RING // 2
    for k in range(8):
        up1[k] = press[clamp(width - 8, 0, 2) + k]
        dn1[k] = press[k]
    for k in range(7):
        up1[8 + k] = source[clamp(width - 7, 0, 3) + k]
        dn1[8 + k] = source[k]
    for k in range(6):
        last = clamp(width - 6, 0, 4)
        far2[k] = press[jnp.where(late, last, 0) + k]
        near2[k] = press[jnp.where(late, 0, last) + k]
    for k in range(5):
        last = clamp(width - 5, 0, 5)
        far2[6 + k] = source[jnp.where(late, last, 0) + k]
        near2[6 + k] = source[jnp.where(late, 0, last) + k]


def side_rows(parts, yup, ydn):
    at = 0
    for part, planes in parts:
        for x in range(planes):
            yup[at] = part[x, CY - 8 :]
            ydn[at] = part[x, 0:8]
            at += 1


def join_slab_kernel(noise, kappa, up, dn, n_out, k_out, yup, ydn):
    n_out[0:NH] = up[0:NH]
    n_out[NH : NH + CX] = noise[...]
    n_out[NH + CX :] = dn[0:NH]
    h = NH - 1
    k_out[0:h] = up[NH:]
    k_out[h : h + CX] = kappa[...]
    k_out[h + CX :] = dn[NH:]
    side_rows(((n_out, NPL), (k_out, KPL)), yup, ydn)


LANES = 8
EACH = CZ // LANES


def groups(planes):
    return -(-planes // EACH)


def join_y_kernel(plane_counts, *refs):
    count = len(plane_counts)
    sources, (yup, ydn), outs, (zup, zdn) = refs[:count], refs[count : count + 2], refs[count + 2 : -2], refs[-2:]
    lane = lax.broadcasted_iota(jnp.int32, (YE, CZ), 1)
    at, begin = 0, 0
    for source, out, planes in zip(sources, outs, plane_counts):
        for x in range(planes):
            out[x, 0:8] = yup[at]
            out[x, 8 : 8 + CY] = source[x]
            out[x, 8 + CY :] = ydn[at]
            at += 1
        for g in range(groups(planes)):
            up = jnp.zeros((YE, CZ), F32)
            dn = jnp.zeros((YE, CZ), F32)
            for k in range(min(EACH, planes - g * EACH)):
                value = out[g * EACH + k]
                here = (lane >= LANES * k) & (lane < LANES * (k + 1))
                up = jnp.where(here, turn(value, LANES * (k + 1), 1), up)
                dn = jnp.where(here, turn(value, LANES * k, 1), dn)
            zup[begin : begin + YE] = up
            zdn[begin : begin + YE] = dn
            begin += YE


def z_halo(start, x, zup, zdn, lane):
    begin = (start + x // EACH) * YE
    k = x % EACH
    above = turn(zdn[begin : begin + YE], -LANES * k, 1)
    below = turn(zup[begin : begin + YE], -LANES * (k + 1), 1)
    return jnp.where(lane < LANES, above, jnp.where(lane >= CZ - LANES, below, 0.0))


def inside_bounds(iy, iz):
    low_y = jnp.where(iy == 0, 8, 0)
    high_y = jnp.where(iy == COUNT_Y - 1, 8 + CY, YE)
    left = jnp.where(iz == 0, 2 * CZ, 2 * CZ - LANES)
    right = jnp.where(iz == COUNT_Z - 1, CZ, CZ + LANES)
    return low_y, high_y, left, right


def chebyshev_kernel(info, n_in, k_in, zup, zdn, field, perm, resid, kap, da, db, acc):
    ix, iy, iz = info[0], info[1], info[2]
    lane = lax.broadcasted_iota(jnp.int32, (YE, CZ), 1)
    for x in range(NPL):
        resid[x, :, 0:CZ] = n_in[x]
        resid[x, :, CZ:] = z_halo(0, x, zup, zdn, lane)
    for x in range(KPL):
        kap[x, :, 0:CZ] = k_in[x] + 6.0
        kap[x, :, CZ:] = z_halo(groups(NPL), x, zup, zdn, lane) + 6.0
    row = lax.broadcasted_iota(jnp.int32, (YE, 2 * CZ), 0)
    wide = lax.broadcasted_iota(jnp.int32, (YE, 2 * CZ), 1)
    low_y, high_y, left, right = inside_bounds(iy, iz)
    inside = (row >= low_y) & (row < high_y) & ((wide < right) | (wide >= left))
    mask = jnp.where(inside, 1.0, 0.0).astype(F32)

    def first(x, _):
        da[x] = resid[x] / THETA
        return 0

    lax.fori_loop(0, NPL, first, 0)
    for x in range(CX):
        acc[x] = da[NH + x]
    old, new = da, db
    for k, (a, b) in enumerate(sweep_weights(SWEEPS)[: SWEEPS - 1], 1):
        def plane(x, _, old=old, new=new, a=a, b=b):
            d = old[x]
            beside = old[x + 1] + old[x - 1]
            beside = beside + (pltpu.roll(d, YE - 1, 0) + pltpu.roll(d, 1, 0))
            beside = beside + (pltpu.roll(d, 2 * CZ - 1, 1) + pltpu.roll(d, 1, 1))
            r = resid[x] - (kap[x - 1] * d - beside)
            resid[x] = r
            at = ix * CX - NH + x
            scale = jnp.where((at >= 0) & (at < CX * COUNT_X), b, 0.0).astype(F32)
            new[x] = a * d + (scale * mask) * r
            return 0

        lax.fori_loop(k, NPL - k, plane, 0)
        for x in range(CX):
            acc[x] += new[NH + x]
        old, new = new, old
    for x in range(CX):
        value = acc[x, 8 : 8 + CY, 0:CZ]
        field[x] = value
        perm[x] = jnp.exp(LOG_GAIN * value)


def window(info, tile):
    first = info[CUTS_AT]
    return first + cut(info, tile) - DEPTH, first + cut(info, tile + 1) + DEPTH - 1


def ring_plane(info, tile, device, r):
    low, high = window(info, tile)
    above = (device + RING) * CX + r <= high
    below = (device - RING) * CX + r >= low
    return above, below


def ring_kernel(info, own, low, high, *outs):
    ix = info[0]
    place = lax.rem(ix, RING)
    for s, out in enumerate(outs, 1):
        tile = ix - place + lax.rem(place + s, RING)
        for r in range(CX):
            above, below = ring_plane(info, tile, ix, r)
            out[r] = jnp.where(above, high[r], jnp.where(below, low[r], own[r]))


def join_tile_kernel(info, own, low, high, ring1, ring2, ring3, press, source, up1, dn1, far2, near2, w_out, p_out, s_out, yup, ydn):
    ix = info[0]
    place = lax.rem(ix, RING)
    here = cut(info, ix)
    w_out[...] = jnp.ones_like(w_out)
    p_out[...] = jnp.zeros_like(p_out)
    s_out[...] = jnp.zeros_like(s_out)
    for s, ring in enumerate((own, ring1, ring2, ring3)):
        device = ix - place + lax.rem(place + RING - s, RING)
        for r in range(CX):
            above, below = ring_plane(info, ix, device, r)
            value = jnp.where(above, high[r], jnp.where(below, low[r], own[r])) if s == 0 else ring[r]
            at = device + jnp.where(above, RING, jnp.where(below, -RING, 0))
            g = at * CX + r - info[CUTS_AT]
            q = g - here + DEPTH
            good = (g >= 0) & (g < INSET) & (q >= 0) & (q < WIN)
            w_out[jnp.where(good, q, WIN)] = value

    def put(out, tile, row, value):
        known = (tile >= 0) & (tile < COUNT_X)
        safe = clamp(tile, 0, COUNT_X - 1)
        begin, end = cut(info, safe), cut(info, safe + 1)
        at = begin + row - here + DEPTH
        good = known & (begin + row < end) & (at >= 0) & (at < WIN)
        out[jnp.where(good, at, WIN)] = value

    def skipped(tile, kept):
        safe = clamp(tile, 0, COUNT_X - 1)
        return jnp.maximum(cut(info, safe + 1) - cut(info, safe) - kept, 0)

    for k in range(MOST):
        put(p_out, ix, k, press[k])
        put(s_out, ix, k, source[k])
    for k in range(8):
        put(p_out, ix - 1, skipped(ix - 1, 8) + k, up1[k])
        put(p_out, ix + 1, k, dn1[k])
    for k in range(7):
        put(s_out, ix - 1, skipped(ix - 1, 7) + k, up1[8 + k])
        put(s_out, ix + 1, k, dn1[8 + k])
    late = place >= RING // 2
    far, near = jnp.where(late, ix + 2, ix - 2), jnp.where(late, ix - 2, ix + 2)
    for part2, tile, ends in ((far2, far, jnp.logical_not(late)), (near2, near, late)):
        for k in range(6):
            put(p_out, tile, jnp.where(ends, skipped(tile, 6), 0) + k, part2[k])
        for k in range(5):
            put(s_out, tile, jnp.where(ends, skipped(tile, 5), 0) + k, part2[6 + k])
    side_rows(((w_out, WIN), (p_out, WIN), (s_out, WIN)), yup, ydn)


def harmonic(own, other):
    return 2.0 * own * other / (own + other)


def jacobi_kernel(info, w_in, p_in, s_in, zup, zdn, out, perm, pa, pb, sc, cxm, cxp, cym, cyp, czm, czp):
    ix, iy, iz = info[0], info[1], info[2]
    here = cut(info, ix)
    count = cut(info, ix + 1) - here
    lane = lax.broadcasted_iota(jnp.int32, (YE, CZ), 1)
    for part, (src, dst) in enumerate(((w_in, perm), (p_in, pa), (s_in, sc))):
        for x in range(WIN):
            dst[x, :, 0:CZ] = src[x]
            dst[x, :, CZ:] = z_halo(part * groups(WIN), x, zup, zdn, lane)

    row = lax.broadcasted_iota(jnp.int32, (YE, 2 * CZ), 0)
    wide = lax.broadcasted_iota(jnp.int32, (YE, 2 * CZ), 1)
    low_y, high_y, left, right = inside_bounds(iy, iz)
    inside = (row >= low_y) & (row < high_y) & ((wide < right) | (wide >= left))
    has_ym = row != low_y
    has_yp = row != high_y - 1
    has_zm = wide != jnp.where(iz == 0, 0, 2 * CZ - LANES)
    has_zp = wide != right - 1

    def couple(q, _):
        g = here + q - DEPTH
        own = perm[q]
        live = inside & (g >= 0) & (g < INSET)
        txm = jnp.where(g > 0, harmonic(own, perm[q - 1]), own)
        txp = jnp.where(g < INSET - 1, harmonic(own, perm[q + 1]), own)
        ty = harmonic(own, pltpu.roll(own, 1, 0))
        tz = harmonic(own, pltpu.roll(own, 1, 1))
        tym = jnp.where(has_ym, ty, own)
        typ = jnp.where(has_yp, pltpu.roll(ty, YE - 1, 0), own)
        tzm = jnp.where(has_zm, tz, own)
        tzp = jnp.where(has_zp, pltpu.roll(tz, 2 * CZ - 1, 1), own)
        total = txm + txp + tym + typ + tzm + tzp

        def share(has, part):
            return jnp.where(live & has, part / total, 0.0)

        cxm[q] = share(g > 0, txm)
        cxp[q] = share(g < INSET - 1, txp)
        cym[q] = share(has_ym, tym)
        cyp[q] = share(has_yp, typ)
        czm[q] = share(has_zm, tzm)
        czp[q] = share(has_zp, tzp)
        sc[q] = share(True, sc[q])
        return 0

    lax.fori_loop(1, WIN - 1, couple, 0)

    old, new = pa, pb
    for sweep in range(1, JACOBI + 1):
        def plane(q, _, old=old, new=new):
            p = old[q]
            total = sc[q] + cxm[q] * old[q - 1] + cxp[q] * old[q + 1]
            total = total + cym[q] * pltpu.roll(p, 1, 0) + cyp[q] * pltpu.roll(p, YE - 1, 0)
            total = total + czm[q] * pltpu.roll(p, 1, 1) + czp[q] * pltpu.roll(p, 2 * CZ - 1, 1)
            new[q] = total
            return 0

        lax.fori_loop(sweep, WIN - sweep, plane, 0)
        old, new = new, old
    for r in range(MOST):
        out[r] = jnp.where(r < count, old[DEPTH + r, 8 : 8 + CY, 0:CZ], 0.0)


def call(kernel, args, outs, scratch=(), scalars=1, cost=1 << 20):
    smem = pl.BlockSpec(memory_space=pltpu.SMEM)
    vmem = pl.BlockSpec(memory_space=pltpu.VMEM)
    return pl.pallas_call(
        kernel,
        out_shape=[pltpu.VMEM(shape, F32) for shape in outs],
        in_specs=[smem] * scalars + [vmem] * (len(args) - scalars),
        out_specs=[vmem] * len(outs),
        scratch_shapes=[pltpu.VMEM(shape, F32) for shape in scratch],
        compiler_params=pltpu.CompilerParams(vmem_limit_bytes=56 << 20),
        cost_estimate=pl.CostEstimate(flops=64 * cost, transcendentals=0, bytes_accessed=cost),
    )(*args[:scalars], *[pltpu.with_memory_space_constraint(arg, pltpu.VMEM) for arg in args[scalars:]])


def shifted(value, axis, count, by):
    return lax.ppermute(value, axis, [(i, i + by) for i in range(count) if 0 <= i + by < count])


def ringed(value, s):
    return lax.ppermute(value, "gx", [(i, i - i % RING + (i + s) % RING) for i in range(COUNT_X)])


def far_pairs():
    pairs = [(i, i + RING if i % RING >= RING // 2 else i - RING) for i in range(COUNT_X)]
    return [(i, to) for i, to in pairs if 0 <= to < COUNT_X]


def join_y(plane_counts, parts, yup, ydn, beside=()):
    yup, ydn = shifted(yup, "gy", COUNT_Y, 1), shifted(ydn, "gy", COUNT_Y, -1)
    packed = (sum(groups(planes) for planes in plane_counts) * YE, CZ)

    def join_rows(*refs):
        join_y_kernel(plane_counts, *refs)

    *parts, zup, zdn = call(
        join_rows,
        (*parts, yup, ydn),
        [(planes, YE, CZ) for planes in plane_counts] + [packed, packed],
        scalars=0,
    )
    beside, zup, zdn = lax.optimization_barrier((beside, zup, zdn))
    return (*parts, shifted(zup, "gz", COUNT_Z, 1), shifted(zdn, "gz", COUNT_Z, -1)), beside


def local(noise, kappa_sq, cuts, pressure_init, source):
    spots = jnp.stack([lax.axis_index("gx"), lax.axis_index("gy"), lax.axis_index("gz")]).astype(jnp.int32)
    info = jnp.concatenate([spots, cuts])
    plane = (CY, CZ)
    up, dn = call(pick_slab_kernel, (noise, kappa_sq), [(PN, *plane)] * 2, scalars=0)
    up, dn = shifted(up, "gx", COUNT_X, 1), shifted(dn, "gx", COUNT_X, -1)
    n, k, yup, ydn = call(
        join_slab_kernel,
        (noise, kappa_sq, up, dn),
        [(NPL, *plane), (KPL, *plane), (NPL + KPL, 8, CZ), (NPL + KPL, 8, CZ)],
        scalars=0,
    )
    press, charge, n, k, yup, ydn = lax.optimization_barrier((pressure_init, source, n, k, yup, ydn))
    tile = call(pick_tile_kernel, (info, press, charge), [(15, *plane)] * 2 + [(11, *plane)] * 2)
    (n, k, zup, zdn), (up1, dn1, far2, near2) = join_y((NPL, KPL), (n, k), yup, ydn, tile)
    up1, dn1 = shifted(up1, "gx", COUNT_X, 1), shifted(dn1, "gx", COUNT_X, -1)
    far2 = lax.ppermute(far2, "gx", far_pairs())
    near2 = ringed(near2, 2)
    big = (NPL, YE, 2 * CZ)
    field, perm = call(
        chebyshev_kernel,
        (info, n, k, zup, zdn),
        [(CX, *plane), (CX, *plane)],
        [big, (KPL, YE, 2 * CZ), big, big, (CX, YE, 2 * CZ)],
        cost=40 << 20,
    )
    perm, up1, dn1, far2 = lax.optimization_barrier((perm, up1, dn1, far2))
    far2 = ringed(far2, 2)
    low, high = shifted(perm, "gx", COUNT_X, RING), shifted(perm, "gx", COUNT_X, -RING)
    rings = call(ring_kernel, (info, perm, low, high), [(CX, *plane)] * (RING - 1))
    rings = [ringed(value, s) for s, value in enumerate(rings, 1)]
    rows = (3 * WIN, 8, CZ)
    w, p, s, yup, ydn = call(
        join_tile_kernel,
        (info, perm, low, high, *rings, pressure_init, source, up1, dn1, far2, near2),
        [(WIN + 1, *plane)] * 3 + [rows, rows],
    )
    (w, p, s, zup, zdn), _ = join_y((WIN, WIN, WIN), (w, p, s), yup, ydn)
    room = (WIN + 1, YE, 2 * CZ)
    (pressure,) = call(jacobi_kernel, (info, w, p, s, zup, zdn), [(MOST, *plane)], [room] * 10)
    return (field, pressure)


def solution(mesh):
    placed = (P("gx", "gy", "gz"), P("gx", "gy", "gz"), P(), P("gx", "gy", "gz"), P("gx", "gy", "gz"))
    return jax.shard_map(
        local,
        mesh=mesh,
        in_specs=placed,
        out_specs=(P("gx", "gy", "gz"), P("gx", "gy", "gz")),
        check_vma=False,
    )
```

```python
import jax
import jax.numpy as jnp
from jax import lax
from jax.experimental import pallas as pl
from jax.experimental.pallas import tpu as pltpu
from jax.sharding import PartitionSpec as P

SWEEPS = 8
JACOBI = 8
THETA = 7.125
DELTA = 6.875
LOG_GAIN = 2.0

COUNT_X = 16
COUNT_Y = 8
COUNT_Z = 4
CX, CY, CZ = 8, 32, 128
INSET = 96
MOST = 10
DEPTH = 8
WIN = MOST + 2 * DEPTH
NH = SWEEPS - 1
NPL = CX + 2 * NH
KPL = NPL - 2
YE = CY + 16
RING = 4

F32 = jnp.float32


def sweep_weights(count):
    ratio_base = THETA / DELTA
    ratio_now = 1.0 / ratio_base
    weights = []
    for index in range(count):
        ratio_next = 1.0 / (2.0 * ratio_base - ratio_now)
        weights.append((ratio_next * ratio_now, 2.0 * ratio_next / DELTA))
        ratio_now = ratio_next
    return weights


CUTS_AT = 3


def cut(info, tile):
    return info[CUTS_AT + 1 + tile]


def clamp(value, low, high):
    return jnp.minimum(jnp.maximum(value, low), high)


def turn(value, shift, axis):
    shift %= value.shape[axis]
    return value if shift == 0 else pltpu.roll(value, shift, axis)


PN = 2 * NH - 1


def pick_slab_kernel(noise, kappa, up, dn):
    up[0:NH] = noise[CX - NH :]
    dn[0:NH] = noise[:NH]
    up[NH:] = kappa[CX - NH + 1 :]
    dn[NH:] = kappa[: NH - 1]


def pick_tile_kernel(info, press, source, up1, dn1, far2, near2):
    ix = info[0]
    width = cut(info, ix + 1) - cut(info, ix)
    late = lax.rem(ix, RING) >= RING // 2
    for k in range(8):
        up1[k] = press[clamp(width - 8, 0, 2) + k]
        dn1[k] = press[k]
    for k in range(7):
        up1[8 + k] = source[clamp(width - 7, 0, 3) + k]
        dn1[8 + k] = source[k]
    for k in range(6):
        last = clamp(width - 6, 0, 4)
        far2[k] = press[jnp.where(late, last, 0) + k]
        near2[k] = press[jnp.where(late, 0, last) + k]
    for k in range(5):
        last = clamp(width - 5, 0, 5)
        far2[6 + k] = source[jnp.where(late, last, 0) + k]
        near2[6 + k] = source[jnp.where(late, 0, last) + k]


def side_rows(parts, yup, ydn):
    at = 0
    for part, planes in parts:
        for x in range(planes):
            yup[at] = part[x, CY - 8 :]
            ydn[at] = part[x, 0:8]
            at += 1


def join_slab_kernel(noise, kappa, up, dn, n_out, k_out, yup, ydn):
    n_out[0:NH] = up[0:NH]
    n_out[NH : NH + CX] = noise[...]
    n_out[NH + CX :] = dn[0:NH]
    h = NH - 1
    k_out[0:h] = up[NH:]
    k_out[h : h + CX] = kappa[...]
    k_out[h + CX :] = dn[NH:]
    side_rows(((n_out, NPL), (k_out, KPL)), yup, ydn)


LANES = 8
EACH = CZ // LANES


def groups(planes):
    return -(-planes // EACH)


def join_y_kernel(plane_counts, *refs):
    count = len(plane_counts)
    sources, (yup, ydn), outs, (zup, zdn) = refs[:count], refs[count : count + 2], refs[count + 2 : -2], refs[-2:]
    lane = lax.broadcasted_iota(jnp.int32, (YE, CZ), 1)
    at, begin = 0, 0
    for source, out, planes in zip(sources, outs, plane_counts):
        for x in range(planes):
            out[x, 0:8] = yup[at]
            out[x, 8 : 8 + CY] = source[x]
            out[x, 8 + CY :] = ydn[at]
            at += 1
        for g in range(groups(planes)):
            up = jnp.zeros((YE, CZ), F32)
            dn = jnp.zeros((YE, CZ), F32)
            for k in range(min(EACH, planes - g * EACH)):
                value = out[g * EACH + k]
                here = (lane >= LANES * k) & (lane < LANES * (k + 1))
                up = jnp.where(here, turn(value, LANES * (k + 1), 1), up)
                dn = jnp.where(here, turn(value, LANES * k, 1), dn)
            zup[begin : begin + YE] = up
            zdn[begin : begin + YE] = dn
            begin += YE


def z_halo(start, x, zup, zdn, lane):
    begin = (start + x // EACH) * YE
    k = x % EACH
    above = turn(zdn[begin : begin + YE], -LANES * k, 1)
    below = turn(zup[begin : begin + YE], -LANES * (k + 1), 1)
    return jnp.where(lane < LANES, above, jnp.where(lane >= CZ - LANES, below, 0.0))


def inside_bounds(iy, iz):
    low_y = jnp.where(iy == 0, 8, 0)
    high_y = jnp.where(iy == COUNT_Y - 1, 8 + CY, YE)
    left = jnp.where(iz == 0, 2 * CZ, 2 * CZ - LANES)
    right = jnp.where(iz == COUNT_Z - 1, CZ, CZ + LANES)
    return low_y, high_y, left, right


def chebyshev_kernel(info, n_in, k_in, zup, zdn, field, perm, resid, kap, da, db, acc):
    ix, iy, iz = info[0], info[1], info[2]
    lane = lax.broadcasted_iota(jnp.int32, (YE, CZ), 1)
    for x in range(NPL):
        resid[x, :, 0:CZ] = n_in[x]
        resid[x, :, CZ:] = z_halo(0, x, zup, zdn, lane)
    for x in range(KPL):
        kap[x, :, 0:CZ] = k_in[x] + 6.0
        kap[x, :, CZ:] = z_halo(groups(NPL), x, zup, zdn, lane) + 6.0
    row = lax.broadcasted_iota(jnp.int32, (YE, 2 * CZ), 0)
    wide = lax.broadcasted_iota(jnp.int32, (YE, 2 * CZ), 1)
    low_y, high_y, left, right = inside_bounds(iy, iz)
    inside = (row >= low_y) & (row < high_y) & ((wide < right) | (wide >= left))
    mask = jnp.where(inside, 1.0, 0.0).astype(F32)

    def first(x, _):
        da[x] = resid[x] / THETA
        return 0

    for x in range(NPL):
        first(x, 0)
    for x in range(CX):
        acc[x] = da[NH + x]
    old, new = da, db
    for k, (a, b) in enumerate(sweep_weights(SWEEPS)[: SWEEPS - 1], 1):
        def plane(x, _, old=old, new=new, a=a, b=b):
            d = old[x]
            beside = old[x + 1] + old[x - 1]
            beside = beside + (pltpu.roll(d, YE - 1, 0) + pltpu.roll(d, 1, 0))
            beside = beside + (pltpu.roll(d, 2 * CZ - 1, 1) + pltpu.roll(d, 1, 1))
            r = resid[x] - (kap[x - 1] * d - beside)
            resid[x] = r
            at = ix * CX - NH + x
            scale = jnp.where((at >= 0) & (at < CX * COUNT_X), b, 0.0).astype(F32)
            new[x] = a * d + (scale * mask) * r
            return 0

        for x in range(k, NPL - k):
            plane(x, 0)
        for x in range(CX):
            acc[x] += new[NH + x]
        old, new = new, old
    for x in range(CX):
        value = acc[x, 8 : 8 + CY, 0:CZ]
        field[x] = value
        perm[x] = jnp.exp(LOG_GAIN * value)


def window(info, tile):
    first = info[CUTS_AT]
    return first + cut(info, tile) - DEPTH, first + cut(info, tile + 1) + DEPTH - 1


def ring_plane(info, tile, device, r):
    low, high = window(info, tile)
    above = (device + RING) * CX + r <= high
    below = (device - RING) * CX + r >= low
    return above, below


def ring_kernel(info, own, low, high, *outs):
    ix = info[0]
    place = lax.rem(ix, RING)
    for s, out in enumerate(outs, 1):
        tile = ix - place + lax.rem(place + s, RING)
        for r in range(CX):
            above, below = ring_plane(info, tile, ix, r)
            out[r] = jnp.where(above, high[r], jnp.where(below, low[r], own[r]))


def join_tile_kernel(info, own, low, high, ring1, ring2, ring3, press, source, up1, dn1, far2, near2, w_out, p_out, s_out, yup, ydn):
    ix = info[0]
    place = lax.rem(ix, RING)
    here = cut(info, ix)
    w_out[...] = jnp.ones_like(w_out)
    p_out[...] = jnp.zeros_like(p_out)
    s_out[...] = jnp.zeros_like(s_out)
    for s, ring in enumerate((own, ring1, ring2, ring3)):
        device = ix - place + lax.rem(place + RING - s, RING)
        for r in range(CX):
            above, below = ring_plane(info, ix, device, r)
            value = jnp.where(above, high[r], jnp.where(below, low[r], own[r])) if s == 0 else ring[r]
            at = device + jnp.where(above, RING, jnp.where(below, -RING, 0))
            g = at * CX + r - info[CUTS_AT]
            q = g - here + DEPTH
            good = (g >= 0) & (g < INSET) & (q >= 0) & (q < WIN)
            w_out[jnp.where(good, q, WIN)] = value

    def put(out, tile, row, value):
        known = (tile >= 0) & (tile < COUNT_X)
        safe = clamp(tile, 0, COUNT_X - 1)
        begin, end = cut(info, safe), cut(info, safe + 1)
        at = begin + row - here + DEPTH
        good = known & (begin + row < end) & (at >= 0) & (at < WIN)
        out[jnp.where(good, at, WIN)] = value

    def skipped(tile, kept):
        safe = clamp(tile, 0, COUNT_X - 1)
        return jnp.maximum(cut(info, safe + 1) - cut(info, safe) - kept, 0)

    for k in range(MOST):
        put(p_out, ix, k, press[k])
        put(s_out, ix, k, source[k])
    for k in range(8):
        put(p_out, ix - 1, skipped(ix - 1, 8) + k, up1[k])
        put(p_out, ix + 1, k, dn1[k])
    for k in range(7):
        put(s_out, ix - 1, skipped(ix - 1, 7) + k, up1[8 + k])
        put(s_out, ix + 1, k, dn1[8 + k])
    late = place >= RING // 2
    far, near = jnp.where(late, ix + 2, ix - 2), jnp.where(late, ix - 2, ix + 2)
    for part2, tile, ends in ((far2, far, jnp.logical_not(late)), (near2, near, late)):
        for k in range(6):
            put(p_out, tile, jnp.where(ends, skipped(tile, 6), 0) + k, part2[k])
        for k in range(5):
            put(s_out, tile, jnp.where(ends, skipped(tile, 5), 0) + k, part2[6 + k])
    side_rows(((w_out, WIN), (p_out, WIN), (s_out, WIN)), yup, ydn)


def harmonic(own, other):
    return 2.0 * own * other / (own + other)


def jacobi_kernel(info, w_in, p_in, s_in, zup, zdn, out, perm, pa, pb, sc, cxm, cxp, cym, cyp, czm, czp):
    ix, iy, iz = info[0], info[1], info[2]
    here = cut(info, ix)
    count = cut(info, ix + 1) - here
    lane = lax.broadcasted_iota(jnp.int32, (YE, CZ), 1)
    for part, (src, dst) in enumerate(((w_in, perm), (p_in, pa), (s_in, sc))):
        for x in range(WIN):
            dst[x, :, 0:CZ] = src[x]
            dst[x, :, CZ:] = z_halo(part * groups(WIN), x, zup, zdn, lane)

    row = lax.broadcasted_iota(jnp.int32, (YE, 2 * CZ), 0)
    wide = lax.broadcasted_iota(jnp.int32, (YE, 2 * CZ), 1)
    low_y, high_y, left, right = inside_bounds(iy, iz)
    inside = (row >= low_y) & (row < high_y) & ((wide < right) | (wide >= left))
    has_ym = row != low_y
    has_yp = row != high_y - 1
    has_zm = wide != jnp.where(iz == 0, 0, 2 * CZ - LANES)
    has_zp = wide != right - 1

    def couple(q, _):
        g = here + q - DEPTH
        own = perm[q]
        live = inside & (g >= 0) & (g < INSET)
        txm = jnp.where(g > 0, harmonic(own, perm[q - 1]), own)
        txp = jnp.where(g < INSET - 1, harmonic(own, perm[q + 1]), own)
        ty = harmonic(own, pltpu.roll(own, 1, 0))
        tz = harmonic(own, pltpu.roll(own, 1, 1))
        tym = jnp.where(has_ym, ty, own)
        typ = jnp.where(has_yp, pltpu.roll(ty, YE - 1, 0), own)
        tzm = jnp.where(has_zm, tz, own)
        tzp = jnp.where(has_zp, pltpu.roll(tz, 2 * CZ - 1, 1), own)
        total = txm + txp + tym + typ + tzm + tzp

        def share(has, part):
            return jnp.where(live & has, part / total, 0.0)

        cxm[q] = share(g > 0, txm)
        cxp[q] = share(g < INSET - 1, txp)
        cym[q] = share(has_ym, tym)
        cyp[q] = share(has_yp, typ)
        czm[q] = share(has_zm, tzm)
        czp[q] = share(has_zp, tzp)
        sc[q] = share(True, sc[q])
        return 0

    for q in range(1, WIN - 1):
        couple(q, 0)

    old, new = pa, pb
    for sweep in range(1, JACOBI + 1):
        def plane(q, _, old=old, new=new):
            p = old[q]
            total = sc[q] + cxm[q] * old[q - 1] + cxp[q] * old[q + 1]
            total = total + cym[q] * pltpu.roll(p, 1, 0) + cyp[q] * pltpu.roll(p, YE - 1, 0)
            total = total + czm[q] * pltpu.roll(p, 1, 1) + czp[q] * pltpu.roll(p, 2 * CZ - 1, 1)
            new[q] = total
            return 0

        for q in range(sweep, WIN - sweep):
            plane(q, 0)
        old, new = new, old
    for r in range(MOST):
        out[r] = jnp.where(r < count, old[DEPTH + r, 8 : 8 + CY, 0:CZ], 0.0)


def call(kernel, args, outs, scratch=(), scalars=1, cost=1 << 20):
    smem = pl.BlockSpec(memory_space=pltpu.SMEM)
    vmem = pl.BlockSpec(memory_space=pltpu.VMEM)
    return pl.pallas_call(
        kernel,
        out_shape=[pltpu.VMEM(shape, F32) for shape in outs],
        in_specs=[smem] * scalars + [vmem] * (len(args) - scalars),
        out_specs=[vmem] * len(outs),
        scratch_shapes=[pltpu.VMEM(shape, F32) for shape in scratch],
        compiler_params=pltpu.CompilerParams(vmem_limit_bytes=56 << 20),
        cost_estimate=pl.CostEstimate(flops=64 * cost, transcendentals=0, bytes_accessed=cost),
    )(*args[:scalars], *[pltpu.with_memory_space_constraint(arg, pltpu.VMEM) for arg in args[scalars:]])


def shifted(value, axis, count, by):
    return lax.ppermute(value, axis, [(i, i + by) for i in range(count) if 0 <= i + by < count])


def ringed(value, s):
    return lax.ppermute(value, "gx", [(i, i - i % RING + (i + s) % RING) for i in range(COUNT_X)])


def far_pairs():
    pairs = [(i, i + RING if i % RING >= RING // 2 else i - RING) for i in range(COUNT_X)]
    return [(i, to) for i, to in pairs if 0 <= to < COUNT_X]


def join_y(plane_counts, parts, yup, ydn, beside=()):
    yup, ydn = shifted(yup, "gy", COUNT_Y, 1), shifted(ydn, "gy", COUNT_Y, -1)
    packed = (sum(groups(planes) for planes in plane_counts) * YE, CZ)

    def join_rows(*refs):
        join_y_kernel(plane_counts, *refs)

    *parts, zup, zdn = call(
        join_rows,
        (*parts, yup, ydn),
        [(planes, YE, CZ) for planes in plane_counts] + [packed, packed],
        scalars=0,
    )
    beside, zup, zdn = lax.optimization_barrier((beside, zup, zdn))
    return (*parts, shifted(zup, "gz", COUNT_Z, 1), shifted(zdn, "gz", COUNT_Z, -1)), beside


def local(noise, kappa_sq, cuts, pressure_init, source):
    spots = jnp.stack([lax.axis_index("gx"), lax.axis_index("gy"), lax.axis_index("gz")]).astype(jnp.int32)
    info = jnp.concatenate([spots, cuts])
    plane = (CY, CZ)
    up, dn = call(pick_slab_kernel, (noise, kappa_sq), [(PN, *plane)] * 2, scalars=0)
    up, dn = shifted(up, "gx", COUNT_X, 1), shifted(dn, "gx", COUNT_X, -1)
    n, k, yup, ydn = call(
        join_slab_kernel,
        (noise, kappa_sq, up, dn),
        [(NPL, *plane), (KPL, *plane), (NPL + KPL, 8, CZ), (NPL + KPL, 8, CZ)],
        scalars=0,
    )
    press, charge, n, k, yup, ydn = lax.optimization_barrier((pressure_init, source, n, k, yup, ydn))
    tile = call(pick_tile_kernel, (info, press, charge), [(15, *plane)] * 2 + [(11, *plane)] * 2)
    (n, k, zup, zdn), (up1, dn1, far2, near2) = join_y((NPL, KPL), (n, k), yup, ydn, tile)
    up1, dn1 = shifted(up1, "gx", COUNT_X, 1), shifted(dn1, "gx", COUNT_X, -1)
    far2 = lax.ppermute(far2, "gx", far_pairs())
    near2 = ringed(near2, 2)
    big = (NPL, YE, 2 * CZ)
    field, perm = call(
        chebyshev_kernel,
        (info, n, k, zup, zdn),
        [(CX, *plane), (CX, *plane)],
        [big, (KPL, YE, 2 * CZ), big, big, (CX, YE, 2 * CZ)],
        cost=40 << 20,
    )
    perm, up1, dn1, far2 = lax.optimization_barrier((perm, up1, dn1, far2))
    far2 = ringed(far2, 2)
    low, high = shifted(perm, "gx", COUNT_X, RING), shifted(perm, "gx", COUNT_X, -RING)
    rings = call(ring_kernel, (info, perm, low, high), [(CX, *plane)] * (RING - 1))
    rings = [ringed(value, s) for s, value in enumerate(rings, 1)]
    rows = (3 * WIN, 8, CZ)
    w, p, s, yup, ydn = call(
        join_tile_kernel,
        (info, perm, low, high, *rings, pressure_init, source, up1, dn1, far2, near2),
        [(WIN + 1, *plane)] * 3 + [rows, rows],
    )
    (w, p, s, zup, zdn), _ = join_y((WIN, WIN, WIN), (w, p, s), yup, ydn)
    room = (WIN + 1, YE, 2 * CZ)
    (pressure,) = call(jacobi_kernel, (info, w, p, s, zup, zdn), [(MOST, *plane)], [room] * 10)
    return (field, pressure)


def solution(mesh):
    placed = (P("gx", "gy", "gz"), P("gx", "gy", "gz"), P(), P("gx", "gy", "gz"), P("gx", "gy", "gz"))
    return jax.shard_map(
        local,
        mesh=mesh,
        in_specs=placed,
        out_specs=(P("gx", "gy", "gz"), P("gx", "gy", "gz")),
        check_vma=False,
    )
```

```python
import jax
import jax.numpy as jnp
from jax import lax
from jax.experimental import pallas as pl
from jax.experimental.pallas import tpu as pltpu
from jax.sharding import PartitionSpec as P

SWEEPS = 8
JACOBI = 8
THETA = 7.125
DELTA = 6.875
LOG_GAIN = 2.0

COUNT_X = 16
COUNT_Y = 8
COUNT_Z = 4
CX, CY, CZ = 8, 32, 128
INSET = 96
MOST = 10
DEPTH = 8
WIN = MOST + 2 * DEPTH
NH = SWEEPS - 1
NPL = CX + 2 * NH
KPL = NPL - 2
YE = CY + 16
RING = 4

F32 = jnp.float32


def sweep_weights(count):
    ratio_base = THETA / DELTA
    ratio_now = 1.0 / ratio_base
    weights = []
    for index in range(count):
        ratio_next = 1.0 / (2.0 * ratio_base - ratio_now)
        weights.append((ratio_next * ratio_now, 2.0 * ratio_next / DELTA))
        ratio_now = ratio_next
    return weights


CUTS_AT = 3


def cut(info, tile):
    return info[CUTS_AT + 1 + tile]


def clamp(value, low, high):
    return jnp.minimum(jnp.maximum(value, low), high)


def turn(value, shift, axis):
    shift %= value.shape[axis]
    return value if shift == 0 else pltpu.roll(value, shift, axis)


PN = 2 * NH - 1


def pick_slab_kernel(noise, kappa, up, dn):
    up[0:NH] = noise[CX - NH :]
    dn[0:NH] = noise[:NH]
    up[NH:] = kappa[CX - NH + 1 :]
    dn[NH:] = kappa[: NH - 1]


def pick_tile_kernel(info, press, source, up, dn, far, near2):
    ix = info[0]
    width = cut(info, ix + 1) - cut(info, ix)
    late = lax.rem(ix, RING) >= RING // 2
    for k in range(8):
        last = clamp(width - 8, 0, 2)
        up[k] = press[last + k]
        dn[k] = press[k]
        far[k] = press[jnp.where(late, last, 0) + k]
    for k in range(7):
        last = clamp(width - 7, 0, 3)
        up[8 + k] = source[last + k]
        dn[8 + k] = source[k]
        far[8 + k] = source[jnp.where(late, last, 0) + k]
    for k in range(6):
        near2[k] = press[jnp.where(late, 0, clamp(width - 6, 0, 4)) + k]
    for k in range(5):
        near2[6 + k] = source[jnp.where(late, 0, clamp(width - 5, 0, 5)) + k]


def side_rows(parts, yup, ydn):
    at = 0
    for part, planes in parts:
        for x in range(planes):
            yup[at] = part[x, CY - 8 :]
            ydn[at] = part[x, 0:8]
            at += 1


def join_slab_kernel(noise, kappa, up, dn, n_out, k_out, yup, ydn):
    n_out[0:NH] = up[0:NH]
    n_out[NH : NH + CX] = noise[...]
    n_out[NH + CX :] = dn[0:NH]
    h = NH - 1
    k_out[0:h] = up[NH:]
    k_out[h : h + CX] = kappa[...]
    k_out[h + CX :] = dn[NH:]
    side_rows(((n_out, NPL), (k_out, KPL)), yup, ydn)


LANES = 8
EACH = CZ // LANES


def groups(planes):
    return -(-planes // EACH)


def join_y_kernel(plane_counts, *refs):
    count = len(plane_counts)
    sources, (yup, ydn), outs, (zup, zdn) = refs[:count], refs[count : count + 2], refs[count + 2 : -2], refs[-2:]
    lane = lax.broadcasted_iota(jnp.int32, (YE, CZ), 1)
    at, begin = 0, 0
    for source, out, planes in zip(sources, outs, plane_counts):
        for x in range(planes):
            out[x, 0:8] = yup[at]
            out[x, 8 : 8 + CY] = source[x]
            out[x, 8 + CY :] = ydn[at]
            at += 1
        for g in range(groups(planes)):
            up = jnp.zeros((YE, CZ), F32)
            dn = jnp.zeros((YE, CZ), F32)
            for k in range(min(EACH, planes - g * EACH)):
                value = out[g * EACH + k]
                here = (lane >= LANES * k) & (lane < LANES * (k + 1))
                up = jnp.where(here, turn(value, LANES * (k + 1), 1), up)
                dn = jnp.where(here, turn(value, LANES * k, 1), dn)
            zup[begin : begin + YE] = up
            zdn[begin : begin + YE] = dn
            begin += YE


def z_halo(start, x, zup, zdn, lane):
    begin = (start + x // EACH) * YE
    k = x % EACH
    above = turn(zdn[begin : begin + YE], -LANES * k, 1)
    below = turn(zup[begin : begin + YE], -LANES * (k + 1), 1)
    return jnp.where(lane < LANES, above, jnp.where(lane >= CZ - LANES, below, 0.0))


def inside_bounds(iy, iz):
    low_y = jnp.where(iy == 0, 8, 0)
    high_y = jnp.where(iy == COUNT_Y - 1, 8 + CY, YE)
    left = jnp.where(iz == 0, 2 * CZ, 2 * CZ - LANES)
    right = jnp.where(iz == COUNT_Z - 1, CZ, CZ + LANES)
    return low_y, high_y, left, right


def chebyshev_kernel(info, n_in, k_in, zup, zdn, field, perm, extra, resid, kap, da, db, acc):
    ix, iy, iz = info[0], info[1], info[2]
    lane = lax.broadcasted_iota(jnp.int32, (YE, CZ), 1)
    for x in range(NPL):
        resid[x, :, 0:CZ] = n_in[x]
        resid[x, :, CZ:] = z_halo(0, x, zup, zdn, lane)
    for x in range(KPL):
        kap[x, :, 0:CZ] = k_in[x] + 6.0
        kap[x, :, CZ:] = z_halo(groups(NPL), x, zup, zdn, lane) + 6.0
    row = lax.broadcasted_iota(jnp.int32, (YE, 2 * CZ), 0)
    wide = lax.broadcasted_iota(jnp.int32, (YE, 2 * CZ), 1)
    low_y, high_y, left, right = inside_bounds(iy, iz)
    inside = (row >= low_y) & (row < high_y) & ((wide < right) | (wide >= left))
    mask = jnp.where(inside, 1.0, 0.0).astype(F32)

    def first(x, _):
        da[x] = resid[x] / THETA
        return 0

    for x in range(NPL):
        first(x, 0)
    for x in range(CX):
        acc[x] = da[NH + x]
    old, new = da, db
    for k, (a, b) in enumerate(sweep_weights(SWEEPS)[: SWEEPS - 1], 1):
        def plane(x, _, old=old, new=new, a=a, b=b):
            d = old[x]
            beside = old[x + 1] + old[x - 1]
            beside = beside + (pltpu.roll(d, YE - 1, 0) + pltpu.roll(d, 1, 0))
            beside = beside + (pltpu.roll(d, 2 * CZ - 1, 1) + pltpu.roll(d, 1, 1))
            r = resid[x] - (kap[x - 1] * d - beside)
            resid[x] = r
            at = ix * CX - NH + x
            scale = jnp.where((at >= 0) & (at < CX * COUNT_X), b, 0.0).astype(F32)
            new[x] = a * d + (scale * mask) * r
            return 0

        for x in range(k, NPL - k):
            plane(x, 0)
        for x in range(CX):
            acc[x] += new[NH + x]
        old, new = new, old
    for x in range(CX):
        value = acc[x, 8 : 8 + CY, 0:CZ]
        field[x] = value
        perm[x] = jnp.exp(LOG_GAIN * value)
    half = jnp.where(ix == LATE_EXTRA[0], CX // 2, 0)
    for r in range(CX // 2):
        extra[r] = perm[half + r]


ACROSS = [(4, 0), (5, 1), (8, 4), (9, 5), (12, 8), (3, 7), (6, 10), (7, 11), (10, 14), (11, 15)]
EARLY_EXTRA, LATE_EXTRA = (6, 3), (9, 12)


def window(info, tile):
    first = info[CUTS_AT]
    return first + cut(info, tile) - DEPTH, first + cut(info, tile + 1) + DEPTH - 1


def ring_plane(info, tile, device, r):
    low, high = window(info, tile)
    above = (device + RING) * CX + r <= high
    below = (device - RING) * CX + r >= low
    return above, below


def ring_kernel(info, own, moved, *outs):
    ix = info[0]
    place = lax.rem(ix, RING)
    for s, out in enumerate(outs, 1):
        tile = ix - place + lax.rem(place + s, RING)
        for r in range(CX):
            above, below = ring_plane(info, tile, ix, r)
            out[r] = jnp.where(above | below, moved[r], own[r])


def join_tile_kernel(info, own, moved, extra, ring1, ring2, ring3, press, source, up, dn, wrap, far2, near2, w_out, p_out, s_out, yup, ydn):
    ix = info[0]
    place = lax.rem(ix, RING)
    here = cut(info, ix)
    w_out[...] = jnp.ones_like(w_out)
    p_out[...] = jnp.zeros_like(p_out)
    s_out[...] = jnp.zeros_like(s_out)
    for s, ring in enumerate((own, ring1, ring2, ring3)):
        device = ix - place + lax.rem(place + RING - s, RING)
        direct_above = (ix == EARLY_EXTRA[1]) & (device + RING == EARLY_EXTRA[0])
        direct_below = (ix == LATE_EXTRA[1]) & (device - RING == LATE_EXTRA[0])
        for r in range(CX):
            above, below = ring_plane(info, ix, device, r)
            value = ring[r]
            if s == 0:
                value = jnp.where(above | below, moved[r], value)
            direct = (above & direct_above) | (below & direct_below)
            value = jnp.where(direct, extra[r % (CX // 2)], value)
            at = device + jnp.where(above, RING, jnp.where(below, -RING, 0))
            g = at * CX + r - info[CUTS_AT]
            q = g - here + DEPTH
            good = (g >= 0) & (g < INSET) & (q >= 0) & (q < WIN)
            w_out[jnp.where(good, q, WIN)] = value

    def put(out, tile, row, value):
        known = (tile >= 0) & (tile < COUNT_X)
        safe = clamp(tile, 0, COUNT_X - 1)
        begin, end = cut(info, safe), cut(info, safe + 1)
        at = begin + row - here + DEPTH
        good = known & (begin + row < end) & (at >= 0) & (at < WIN)
        out[jnp.where(good, at, WIN)] = value

    def skipped(tile, kept):
        safe = clamp(tile, 0, COUNT_X - 1)
        return jnp.maximum(cut(info, safe + 1) - cut(info, safe) - kept, 0)

    for k in range(MOST):
        put(p_out, ix, k, press[k])
        put(s_out, ix, k, source[k])
    def put_all(part, tile, ends, rows_p, rows_s):
        for k in range(rows_p):
            put(p_out, tile, jnp.where(ends, skipped(tile, rows_p), 0) + k, part[k])
        for k in range(rows_s):
            put(s_out, tile, jnp.where(ends, skipped(tile, rows_s), 0) + k, part[rows_p + k])

    first, final, late = place == 0, place == RING - 1, place >= RING // 2
    put_all(up, jnp.where(first, -1, ix - 1), True, 8, 7)
    put_all(dn, jnp.where(final, -1, ix + 1), False, 8, 7)
    put_all(wrap, jnp.where(first, ix - 1, jnp.where(final, ix + 1, -1)), first, 8, 7)
    put_all(far2, jnp.where(late, ix + 2, ix - 2), jnp.logical_not(late), 8, 7)
    put_all(near2, jnp.where(late, ix - 2, ix + 2), late, 6, 5)
    side_rows(((w_out, WIN), (p_out, WIN), (s_out, WIN)), yup, ydn)


def harmonic(own, other):
    return 2.0 * own * other / (own + other)


def jacobi_kernel(info, w_in, p_in, s_in, zup, zdn, out, perm, pa, pb, sc, cxm, cxp, cym, cyp, czm, czp):
    ix, iy, iz = info[0], info[1], info[2]
    here = cut(info, ix)
    count = cut(info, ix + 1) - here
    lane = lax.broadcasted_iota(jnp.int32, (YE, CZ), 1)
    for part, (src, dst) in enumerate(((w_in, perm), (p_in, pa), (s_in, sc))):
        for x in range(WIN):
            dst[x, :, 0:CZ] = src[x]
            dst[x, :, CZ:] = z_halo(part * groups(WIN), x, zup, zdn, lane)

    row = lax.broadcasted_iota(jnp.int32, (YE, 2 * CZ), 0)
    wide = lax.broadcasted_iota(jnp.int32, (YE, 2 * CZ), 1)
    low_y, high_y, left, right = inside_bounds(iy, iz)
    inside = (row >= low_y) & (row < high_y) & ((wide < right) | (wide >= left))
    has_ym = row != low_y
    has_yp = row != high_y - 1
    has_zm = wide != jnp.where(iz == 0, 0, 2 * CZ - LANES)
    has_zp = wide != right - 1

    def couple(q, _):
        g = here + q - DEPTH
        own = perm[q]
        live = inside & (g >= 0) & (g < INSET)
        txm = jnp.where(g > 0, harmonic(own, perm[q - 1]), own)
        txp = jnp.where(g < INSET - 1, harmonic(own, perm[q + 1]), own)
        ty = harmonic(own, pltpu.roll(own, 1, 0))
        tz = harmonic(own, pltpu.roll(own, 1, 1))
        tym = jnp.where(has_ym, ty, own)
        typ = jnp.where(has_yp, pltpu.roll(ty, YE - 1, 0), own)
        tzm = jnp.where(has_zm, tz, own)
        tzp = jnp.where(has_zp, pltpu.roll(tz, 2 * CZ - 1, 1), own)
        total = txm + txp + tym + typ + tzm + tzp

        def share(has, part):
            return jnp.where(live & has, part / total, 0.0)

        cxm[q] = share(g > 0, txm)
        cxp[q] = share(g < INSET - 1, txp)
        cym[q] = share(has_ym, tym)
        cyp[q] = share(has_yp, typ)
        czm[q] = share(has_zm, tzm)
        czp[q] = share(has_zp, tzp)
        sc[q] = share(True, sc[q])
        return 0

    for q in range(1, WIN - 1):
        couple(q, 0)

    old, new = pa, pb
    for sweep in range(1, JACOBI + 1):
        def plane(q, _, old=old, new=new):
            p = old[q]
            total = sc[q] + cxm[q] * old[q - 1] + cxp[q] * old[q + 1]
            total = total + cym[q] * pltpu.roll(p, 1, 0) + cyp[q] * pltpu.roll(p, YE - 1, 0)
            total = total + czm[q] * pltpu.roll(p, 1, 1) + czp[q] * pltpu.roll(p, 2 * CZ - 1, 1)
            new[q] = total
            return 0

        for q in range(sweep, WIN - sweep):
            plane(q, 0)
        old, new = new, old
    for r in range(MOST):
        out[r] = jnp.where(r < count, old[DEPTH + r, 8 : 8 + CY, 0:CZ], 0.0)


def call(kernel, args, outs, scratch=(), scalars=1, cost=1 << 20):
    smem = pl.BlockSpec(memory_space=pltpu.SMEM)
    vmem = pl.BlockSpec(memory_space=pltpu.VMEM)
    return pl.pallas_call(
        kernel,
        out_shape=[pltpu.VMEM(shape, F32) for shape in outs],
        in_specs=[smem] * scalars + [vmem] * (len(args) - scalars),
        out_specs=[vmem] * len(outs),
        scratch_shapes=[pltpu.VMEM(shape, F32) for shape in scratch],
        compiler_params=pltpu.CompilerParams(vmem_limit_bytes=56 << 20),
        cost_estimate=pl.CostEstimate(flops=64 * cost, transcendentals=0, bytes_accessed=cost),
    )(*args[:scalars], *[pltpu.with_memory_space_constraint(arg, pltpu.VMEM) for arg in args[scalars:]])


def shifted(value, axis, count, by):
    return lax.ppermute(value, axis, [(i, i + by) for i in range(count) if 0 <= i + by < count])


def ringed(value, s):
    return lax.ppermute(value, "gx", [(i, i - i % RING + (i + s) % RING) for i in range(COUNT_X)])


def far_pairs():
    pairs = [(i, i + RING if i % RING >= RING // 2 else i - RING) for i in range(COUNT_X)]
    return [(i, to) for i, to in pairs if 0 <= to < COUNT_X]


def join_y(plane_counts, parts, yup, ydn, beside=()):
    yup, ydn = shifted(yup, "gy", COUNT_Y, 1), shifted(ydn, "gy", COUNT_Y, -1)
    packed = (sum(groups(planes) for planes in plane_counts) * YE, CZ)

    def join_rows(*refs):
        join_y_kernel(plane_counts, *refs)

    *parts, zup, zdn = call(
        join_rows,
        (*parts, yup, ydn),
        [(planes, YE, CZ) for planes in plane_counts] + [packed, packed],
        scalars=0,
    )
    beside, zup, zdn = lax.optimization_barrier((beside, zup, zdn))
    return (*parts, shifted(zup, "gz", COUNT_Z, 1), shifted(zdn, "gz", COUNT_Z, -1)), beside


def local(noise, kappa_sq, cuts, pressure_init, source):
    spots = jnp.stack([lax.axis_index("gx"), lax.axis_index("gy"), lax.axis_index("gz")]).astype(jnp.int32)
    info = jnp.concatenate([spots, cuts])
    plane = (CY, CZ)
    up, dn = call(pick_slab_kernel, (noise, kappa_sq), [(PN, *plane)] * 2, scalars=0)
    press, charge, up, dn = lax.optimization_barrier((pressure_init, source, up, dn))
    halo = (15, *plane)
    t_up, t_dn, far, near2 = call(pick_tile_kernel, (info, press, charge), [halo] * 3 + [(11, *plane)])
    up, dn = shifted(up, "gx", COUNT_X, 1), shifted(dn, "gx", COUNT_X, -1)
    t_up = lax.ppermute(t_up, "gx", [(i, i + 1) for i in range(COUNT_X) if (i + 1) % RING])
    t_dn = lax.ppermute(t_dn, "gx", [(i + 1, i) for i in range(COUNT_X) if (i + 1) % RING])
    far = lax.ppermute(far, "gx", far_pairs())
    n, k, yup, ydn = call(
        join_slab_kernel,
        (noise, kappa_sq, up, dn),
        [(NPL, *plane), (KPL, *plane), (NPL + KPL, 8, CZ), (NPL + KPL, 8, CZ)],
        scalars=0,
    )
    (n, k, zup, zdn), (far, near2) = join_y((NPL, KPL), (n, k), yup, ydn, (far, near2))
    wrap = lax.ppermute(far, "gx", [(i, i + 3 if i % RING == 0 else i - 3) for i in range(COUNT_X) if i % RING in (0, RING - 1)])
    far2, near2 = ringed(far, 2), ringed(near2, 2)
    big = (NPL, YE, 2 * CZ)
    field, perm, extra = call(
        chebyshev_kernel,
        (info, n, k, zup, zdn),
        [(CX, *plane), (CX, *plane), (CX // 2, *plane)],
        [big, (KPL, YE, 2 * CZ), big, big, (CX, YE, 2 * CZ)],
        cost=40 << 20,
    )
    moved = lax.ppermute(perm, "gx", ACROSS)
    extra = lax.ppermute(extra, "gx", [EARLY_EXTRA, LATE_EXTRA])
    moved, extra = lax.optimization_barrier((moved, extra))
    rings = call(ring_kernel, (info, perm, moved), [(CX, *plane)] * (RING - 1))
    rings = [ringed(value, s) for s, value in enumerate(rings, 1)]
    rows = (3 * WIN, 8, CZ)
    w, p, s, yup, ydn = call(
        join_tile_kernel,
        (info, perm, moved, extra, *rings, pressure_init, source, t_up, t_dn, wrap, far2, near2),
        [(WIN + 1, *plane)] * 3 + [rows, rows],
    )
    (w, p, s, zup, zdn), _ = join_y((WIN, WIN, WIN), (w, p, s), yup, ydn)
    room = (WIN + 1, YE, 2 * CZ)
    (pressure,) = call(jacobi_kernel, (info, w, p, s, zup, zdn), [(MOST, *plane)], [room] * 10)
    return (field, pressure)


def solution(mesh):
    placed = (P("gx", "gy", "gz"), P("gx", "gy", "gz"), P(), P("gx", "gy", "gz"), P("gx", "gy", "gz"))
    return jax.shard_map(
        local,
        mesh=mesh,
        in_specs=placed,
        out_specs=(P("gx", "gy", "gz"), P("gx", "gy", "gz")),
        check_vma=False,
    )
```

```python
import jax
import jax.numpy as jnp
from jax import lax
from jax.experimental import pallas as pl
from jax.experimental.pallas import tpu as pltpu
from jax.sharding import PartitionSpec as P

SWEEPS = 8
JACOBI = 8
THETA = 7.125
DELTA = 6.875
LOG_GAIN = 2.0

COUNT_X = 16
COUNT_Y = 8
COUNT_Z = 4
CX, CY, CZ = 8, 32, 128
INSET = 96
MOST = 10
DEPTH = 8
WIN = MOST + 2 * DEPTH
NH = SWEEPS - 1
NPL = CX + 2 * NH
KPL = NPL - 2
YE = CY + 16
RING = 4

F32 = jnp.float32


def sweep_weights(count):
    ratio_base = THETA / DELTA
    ratio_now = 1.0 / ratio_base
    weights = []
    for index in range(count):
        ratio_next = 1.0 / (2.0 * ratio_base - ratio_now)
        weights.append((ratio_next * ratio_now, 2.0 * ratio_next / DELTA))
        ratio_now = ratio_next
    return weights


CUTS_AT = 3


def cut(info, tile):
    return info[CUTS_AT + 1 + tile]


def clamp(value, low, high):
    return jnp.minimum(jnp.maximum(value, low), high)


def turn(value, shift, axis):
    shift %= value.shape[axis]
    return value if shift == 0 else pltpu.roll(value, shift, axis)


PN = 2 * NH - 1


def pick_slab_kernel(spots, noise, kappa, carry, up, dn):
    at = jnp.where(lax.rem(spots[0], RING) == RING - 1, 1, 0)
    up[0:NH] = noise[CX - NH :]
    dn[0:NH] = noise[:NH]
    up[NH:] = kappa[CX - NH + 1 :]
    dn[NH:] = kappa[: NH - 1]
    for k in range(NH):
        carry[k] = noise[k + (CX - NH) * at]
    for k in range(NH - 1):
        carry[NH + k] = kappa[k + (CX - NH + 1) * at]


def pick_tile_kernel(info, press, source, up, dn, far, near2):
    ix = info[0]
    width = cut(info, ix + 1) - cut(info, ix)
    late = lax.rem(ix, RING) >= RING // 2
    for k in range(8):
        last = clamp(width - 8, 0, 2)
        up[k] = press[last + k]
        dn[k] = press[k]
        far[k] = press[jnp.where(late, last, 0) + k]
    for k in range(7):
        last = clamp(width - 7, 0, 3)
        up[8 + k] = source[last + k]
        dn[8 + k] = source[k]
        far[8 + k] = source[jnp.where(late, last, 0) + k]
    for k in range(6):
        near2[k] = press[jnp.where(late, 0, clamp(width - 6, 0, 4)) + k]
    for k in range(5):
        near2[6 + k] = source[jnp.where(late, 0, clamp(width - 5, 0, 5)) + k]


def side_rows(parts, yup, ydn):
    at = 0
    for part, planes in parts:
        for x in range(planes):
            yup[at] = part[x, CY - 8 :]
            ydn[at] = part[x, 0:8]
            at += 1


def join_slab_kernel(spots, noise, kappa, carry, up, dn, n_out, k_out, yup, ydn):
    place = lax.rem(spots[0], RING)
    h = NH - 1
    n_out[NH : NH + CX] = noise[...]
    k_out[h : h + CX] = kappa[...]
    for at_n, at_k, end, inner in ((0, 0, 0, up), (NH + CX, h + CX, RING - 1, dn)):
        @pl.when(place == end)
        def _(at_n=at_n, at_k=at_k):
            n_out[at_n : at_n + NH] = carry[0:NH]
            k_out[at_k : at_k + h] = carry[NH:]

        @pl.when(place != end)
        def _(at_n=at_n, at_k=at_k, inner=inner):
            n_out[at_n : at_n + NH] = inner[0:NH]
            k_out[at_k : at_k + h] = inner[NH:]

    side_rows(((n_out, NPL), (k_out, KPL)), yup, ydn)


LANES = 8
EACH = CZ // LANES


def groups(planes):
    return -(-planes // EACH)


def join_y_kernel(plane_counts, *refs):
    count = len(plane_counts)
    sources, (yup, ydn), outs, (zup, zdn) = refs[:count], refs[count : count + 2], refs[count + 2 : -2], refs[-2:]
    lane = lax.broadcasted_iota(jnp.int32, (YE, CZ), 1)
    at, begin = 0, 0
    for source, out, planes in zip(sources, outs, plane_counts):
        for x in range(planes):
            out[x, 0:8] = yup[at]
            out[x, 8 : 8 + CY] = source[x]
            out[x, 8 + CY :] = ydn[at]
            at += 1
        for g in range(groups(planes)):
            up = jnp.zeros((YE, CZ), F32)
            dn = jnp.zeros((YE, CZ), F32)
            for k in range(min(EACH, planes - g * EACH)):
                value = out[g * EACH + k]
                here = (lane >= LANES * k) & (lane < LANES * (k + 1))
                up = jnp.where(here, turn(value, LANES * (k + 1), 1), up)
                dn = jnp.where(here, turn(value, LANES * k, 1), dn)
            zup[begin : begin + YE] = up
            zdn[begin : begin + YE] = dn
            begin += YE


def z_halo(start, x, zup, zdn, lane):
    begin = (start + x // EACH) * YE
    k = x % EACH
    above = turn(zdn[begin : begin + YE], -LANES * k, 1)
    below = turn(zup[begin : begin + YE], -LANES * (k + 1), 1)
    return jnp.where(lane < LANES, above, jnp.where(lane >= CZ - LANES, below, 0.0))


def inside_bounds(iy, iz):
    low_y = jnp.where(iy == 0, 8, 0)
    high_y = jnp.where(iy == COUNT_Y - 1, 8 + CY, YE)
    left = jnp.where(iz == 0, 2 * CZ, 2 * CZ - LANES)
    right = jnp.where(iz == COUNT_Z - 1, CZ, CZ + LANES)
    return low_y, high_y, left, right


def chebyshev_kernel(info, n_in, k_in, zup, zdn, field, perm, extra, resid, kap, da, db, acc):
    ix, iy, iz = info[0], info[1], info[2]
    lane = lax.broadcasted_iota(jnp.int32, (YE, CZ), 1)
    for x in range(NPL):
        resid[x, :, 0:CZ] = n_in[x]
        resid[x, :, CZ:] = z_halo(0, x, zup, zdn, lane)
    for x in range(KPL):
        kap[x, :, 0:CZ] = k_in[x] + 6.0
        kap[x, :, CZ:] = z_halo(groups(NPL), x, zup, zdn, lane) + 6.0
    row = lax.broadcasted_iota(jnp.int32, (YE, 2 * CZ), 0)
    wide = lax.broadcasted_iota(jnp.int32, (YE, 2 * CZ), 1)
    low_y, high_y, left, right = inside_bounds(iy, iz)
    inside = (row >= low_y) & (row < high_y) & ((wide < right) | (wide >= left))
    mask = jnp.where(inside, 1.0, 0.0).astype(F32)

    def first(x, _):
        da[x] = resid[x] / THETA
        return 0

    for x in range(NPL):
        first(x, 0)
    for x in range(CX):
        acc[x] = da[NH + x]
    old, new = da, db
    for k, (a, b) in enumerate(sweep_weights(SWEEPS)[: SWEEPS - 1], 1):
        def plane(x, _, old=old, new=new, a=a, b=b):
            d = old[x]
            beside = old[x + 1] + old[x - 1]
            beside = beside + (pltpu.roll(d, YE - 1, 0) + pltpu.roll(d, 1, 0))
            beside = beside + (pltpu.roll(d, 2 * CZ - 1, 1) + pltpu.roll(d, 1, 1))
            r = resid[x] - (kap[x - 1] * d - beside)
            resid[x] = r
            at = ix * CX - NH + x
            scale = jnp.where((at >= 0) & (at < CX * COUNT_X), b, 0.0).astype(F32)
            new[x] = a * d + (scale * mask) * r
            return 0

        for x in range(k, NPL - k):
            plane(x, 0)
        for x in range(CX):
            acc[x] += new[NH + x]
        old, new = new, old
    for x in range(CX):
        value = acc[x, 8 : 8 + CY, 0:CZ]
        field[x] = value
        perm[x] = jnp.exp(LOG_GAIN * value)
    half = jnp.where(ix == LATE_EXTRA[0], CX // 2, 0)
    for r in range(CX // 2):
        extra[r] = perm[half + r]


ACROSS = [(4, 0), (5, 1), (8, 4), (9, 5), (12, 8), (3, 7), (6, 10), (7, 11), (10, 14), (11, 15)]
EARLY_EXTRA, LATE_EXTRA = (6, 3), (9, 12)


def window(info, tile):
    first = info[CUTS_AT]
    return first + cut(info, tile) - DEPTH, first + cut(info, tile + 1) + DEPTH - 1


def ring_plane(info, tile, device, r):
    low, high = window(info, tile)
    above = (device + RING) * CX + r <= high
    below = (device - RING) * CX + r >= low
    return above, below


def ring_kernel(info, own, moved, *outs):
    ix = info[0]
    place = lax.rem(ix, RING)
    for s, out in enumerate(outs, 1):
        tile = ix - place + lax.rem(place + s, RING)
        for r in range(CX):
            above, below = ring_plane(info, tile, ix, r)
            out[r] = jnp.where(above | below, moved[r], own[r])


def join_tile_kernel(info, own, moved, extra, ring1, ring2, ring3, press, source, up, dn, across, far2, near2, w_out, p_out, s_out, yup, ydn):
    ix = info[0]
    place = lax.rem(ix, RING)
    here = cut(info, ix)
    w_out[...] = jnp.ones_like(w_out)
    p_out[...] = jnp.zeros_like(p_out)
    s_out[...] = jnp.zeros_like(s_out)
    for s, ring in enumerate((own, ring1, ring2, ring3)):
        device = ix - place + lax.rem(place + RING - s, RING)
        direct_above = (ix == EARLY_EXTRA[1]) & (device + RING == EARLY_EXTRA[0])
        direct_below = (ix == LATE_EXTRA[1]) & (device - RING == LATE_EXTRA[0])
        for r in range(CX):
            above, below = ring_plane(info, ix, device, r)
            value = ring[r]
            if s == 0:
                value = jnp.where(above | below, moved[r], value)
            direct = (above & direct_above) | (below & direct_below)
            value = jnp.where(direct, extra[r % (CX // 2)], value)
            at = device + jnp.where(above, RING, jnp.where(below, -RING, 0))
            g = at * CX + r - info[CUTS_AT]
            q = g - here + DEPTH
            good = (g >= 0) & (g < INSET) & (q >= 0) & (q < WIN)
            w_out[jnp.where(good, q, WIN)] = value

    def put(out, tile, row, value):
        known = (tile >= 0) & (tile < COUNT_X)
        safe = clamp(tile, 0, COUNT_X - 1)
        begin, end = cut(info, safe), cut(info, safe + 1)
        at = begin + row - here + DEPTH
        good = known & (begin + row < end) & (at >= 0) & (at < WIN)
        out[jnp.where(good, at, WIN)] = value

    def skipped(tile, kept):
        safe = clamp(tile, 0, COUNT_X - 1)
        return jnp.maximum(cut(info, safe + 1) - cut(info, safe) - kept, 0)

    for k in range(MOST):
        put(p_out, ix, k, press[k])
        put(s_out, ix, k, source[k])
    def put_all(part, tile, ends, rows_p, rows_s):
        for k in range(rows_p):
            put(p_out, tile, jnp.where(ends, skipped(tile, rows_p), 0) + k, part[k])
        for k in range(rows_s):
            put(s_out, tile, jnp.where(ends, skipped(tile, rows_s), 0) + k, part[rows_p + k])

    first, final, late = place == 0, place == RING - 1, place >= RING // 2
    put_all(up, jnp.where(first, -1, ix - 1), True, 8, 7)
    put_all(dn, jnp.where(final, -1, ix + 1), False, 8, 7)
    put_all(across, jnp.where(first, ix - 1, jnp.where(final, ix + 1, -1)), first, 8, 7)
    put_all(far2, jnp.where(late, ix + 2, ix - 2), jnp.logical_not(late), 8, 7)
    put_all(near2, jnp.where(late, ix - 2, ix + 2), late, 6, 5)
    side_rows(((w_out, WIN), (p_out, WIN), (s_out, WIN)), yup, ydn)


def harmonic(own, other):
    return 2.0 * own * other / (own + other)


def jacobi_kernel(info, w_in, p_in, s_in, zup, zdn, out, perm, pa, pb, sc, cxm, cxp, cym, cyp, czm, czp):
    ix, iy, iz = info[0], info[1], info[2]
    here = cut(info, ix)
    count = cut(info, ix + 1) - here
    lane = lax.broadcasted_iota(jnp.int32, (YE, CZ), 1)
    for part, (src, dst) in enumerate(((w_in, perm), (p_in, pa), (s_in, sc))):
        for x in range(WIN):
            dst[x, :, 0:CZ] = src[x]
            dst[x, :, CZ:] = z_halo(part * groups(WIN), x, zup, zdn, lane)

    row = lax.broadcasted_iota(jnp.int32, (YE, 2 * CZ), 0)
    wide = lax.broadcasted_iota(jnp.int32, (YE, 2 * CZ), 1)
    low_y, high_y, left, right = inside_bounds(iy, iz)
    inside = (row >= low_y) & (row < high_y) & ((wide < right) | (wide >= left))
    has_ym = row != low_y
    has_yp = row != high_y - 1
    has_zm = wide != jnp.where(iz == 0, 0, 2 * CZ - LANES)
    has_zp = wide != right - 1

    def couple(q, _):
        g = here + q - DEPTH
        own = perm[q]
        live = inside & (g >= 0) & (g < INSET)
        txm = jnp.where(g > 0, harmonic(own, perm[q - 1]), own)
        txp = jnp.where(g < INSET - 1, harmonic(own, perm[q + 1]), own)
        ty = harmonic(own, pltpu.roll(own, 1, 0))
        tz = harmonic(own, pltpu.roll(own, 1, 1))
        tym = jnp.where(has_ym, ty, own)
        typ = jnp.where(has_yp, pltpu.roll(ty, YE - 1, 0), own)
        tzm = jnp.where(has_zm, tz, own)
        tzp = jnp.where(has_zp, pltpu.roll(tz, 2 * CZ - 1, 1), own)
        total = txm + txp + tym + typ + tzm + tzp

        def share(has, part):
            return jnp.where(live & has, part / total, 0.0)

        cxm[q] = share(g > 0, txm)
        cxp[q] = share(g < INSET - 1, txp)
        cym[q] = share(has_ym, tym)
        cyp[q] = share(has_yp, typ)
        czm[q] = share(has_zm, tzm)
        czp[q] = share(has_zp, tzp)
        sc[q] = share(True, sc[q])
        return 0

    for q in range(1, WIN - 1):
        couple(q, 0)

    old, new = pa, pb
    for sweep in range(1, JACOBI + 1):
        def plane(q, _, old=old, new=new):
            p = old[q]
            total = sc[q] + cxm[q] * old[q - 1] + cxp[q] * old[q + 1]
            total = total + cym[q] * pltpu.roll(p, 1, 0) + cyp[q] * pltpu.roll(p, YE - 1, 0)
            total = total + czm[q] * pltpu.roll(p, 1, 1) + czp[q] * pltpu.roll(p, 2 * CZ - 1, 1)
            new[q] = total
            return 0

        for q in range(sweep, WIN - sweep):
            plane(q, 0)
        old, new = new, old
    for r in range(MOST):
        out[r] = jnp.where(r < count, old[DEPTH + r, 8 : 8 + CY, 0:CZ], 0.0)


def call(kernel, args, outs, scratch=(), scalars=1, cost=1 << 20):
    smem = pl.BlockSpec(memory_space=pltpu.SMEM)
    vmem = pl.BlockSpec(memory_space=pltpu.VMEM)
    return pl.pallas_call(
        kernel,
        out_shape=[pltpu.VMEM(shape, F32) for shape in outs],
        in_specs=[smem] * scalars + [vmem] * (len(args) - scalars),
        out_specs=[vmem] * len(outs),
        scratch_shapes=[pltpu.VMEM(shape, F32) for shape in scratch],
        compiler_params=pltpu.CompilerParams(vmem_limit_bytes=56 << 20),
        cost_estimate=pl.CostEstimate(flops=64 * cost, transcendentals=0, bytes_accessed=cost),
    )(*args[:scalars], *[pltpu.with_memory_space_constraint(arg, pltpu.VMEM) for arg in args[scalars:]])


def shifted(value, axis, count, by):
    return lax.ppermute(value, axis, [(i, i + by) for i in range(count) if 0 <= i + by < count])


def ringed(value, s):
    return lax.ppermute(value, "gx", [(i, i - i % RING + (i + s) % RING) for i in range(COUNT_X)])


def join_y(plane_counts, parts, yup, ydn, beside=()):
    yup, ydn = shifted(yup, "gy", COUNT_Y, 1), shifted(ydn, "gy", COUNT_Y, -1)
    yup, ydn, beside = lax.optimization_barrier((yup, ydn, beside))
    packed = (sum(groups(planes) for planes in plane_counts) * YE, CZ)

    def join_rows(*refs):
        join_y_kernel(plane_counts, *refs)

    *parts, zup, zdn = call(
        join_rows,
        (*parts, yup, ydn),
        [(planes, YE, CZ) for planes in plane_counts] + [packed, packed],
        scalars=0,
    )
    return beside, (*parts, shifted(zup, "gz", COUNT_Z, 1), shifted(zdn, "gz", COUNT_Z, -1))


def local(noise, kappa_sq, cuts, pressure_init, source):
    spots = jnp.stack([lax.axis_index("gx"), lax.axis_index("gy"), lax.axis_index("gz")]).astype(jnp.int32)
    info = jnp.concatenate([spots, cuts])
    plane = (CY, CZ)
    inner = [(i, i + 1) for i in range(COUNT_X) if (i + 1) % RING]
    outer = [(i, i + 1) for i in range(COUNT_X - 1) if (i + 1) % RING == 0]
    inner_dn, outer_dn = [(j, i) for i, j in inner], [(j, i) for i, j in outer]
    carry, up, dn = call(pick_slab_kernel, (spots, noise, kappa_sq), [(PN, *plane)] * 3)
    press, charge, carry, up, dn = lax.optimization_barrier((pressure_init, source, carry, up, dn))
    halo = (15, *plane)
    t_up, t_dn, far, near2 = call(pick_tile_kernel, (info, press, charge), [halo] * 3 + [(11, *plane)])
    carry = lax.ppermute(carry, "gx", outer + outer_dn)
    up, dn = lax.ppermute(up, "gx", inner), lax.ppermute(dn, "gx", inner_dn)
    t_up, t_dn = lax.ppermute(t_up, "gx", inner), lax.ppermute(t_dn, "gx", inner_dn)
    far = lax.ppermute(far, "gx", [(i, i + (3, 0, 0, -3)[i % RING]) for i in range(COUNT_X)])
    steps = [(i, i + (RING, -RING, RING, -RING)[i % RING]) for i in range(COUNT_X)]
    across = lax.ppermute(far, "gx", [(i, to) for i, to in steps if 0 <= to < COUNT_X])
    n, k, yup, ydn = call(
        join_slab_kernel,
        (spots, noise, kappa_sq, carry, up, dn),
        [(NPL, *plane), (KPL, *plane), (NPL + KPL, 8, CZ), (NPL + KPL, 8, CZ)],
    )
    across, (n, k, zup, zdn) = join_y((NPL, KPL), (n, k), yup, ydn, across)
    near2 = ringed(near2, 2)
    big = (NPL, YE, 2 * CZ)
    field, perm, extra = call(
        chebyshev_kernel,
        (info, n, k, zup, zdn),
        [(CX, *plane), (CX, *plane), (CX // 2, *plane)],
        [big, (KPL, YE, 2 * CZ), big, big, (CX, YE, 2 * CZ)],
        cost=40 << 20,
    )
    perm, extra, across = lax.optimization_barrier((perm, extra, across))
    far2 = lax.ppermute(across, "gx", [(i, i + (1, 2, -2, -1)[i % RING]) for i in range(COUNT_X)])
    moved = lax.ppermute(perm, "gx", ACROSS)
    extra = lax.ppermute(extra, "gx", [EARLY_EXTRA, LATE_EXTRA])
    moved, extra = lax.optimization_barrier((moved, extra))
    rings = call(ring_kernel, (info, perm, moved), [(CX, *plane)] * (RING - 1))
    rings = [ringed(value, s) for s, value in enumerate(rings, 1)]
    rows = (3 * WIN, 8, CZ)
    w, p, s, yup, ydn = call(
        join_tile_kernel,
        (info, perm, moved, extra, *rings, pressure_init, source, t_up, t_dn, across, far2, near2),
        [(WIN + 1, *plane)] * 3 + [rows, rows],
    )
    _, (w, p, s, zup, zdn) = join_y((WIN, WIN, WIN), (w, p, s), yup, ydn)
    room = (WIN + 1, YE, 2 * CZ)
    (pressure,) = call(jacobi_kernel, (info, w, p, s, zup, zdn), [(MOST, *plane)], [room] * 10)
    return (field, pressure)


def solution(mesh):
    placed = (P("gx", "gy", "gz"), P("gx", "gy", "gz"), P(), P("gx", "gy", "gz"), P("gx", "gy", "gz"))
    return jax.shard_map(
        local,
        mesh=mesh,
        in_specs=placed,
        out_specs=(P("gx", "gy", "gz"), P("gx", "gy", "gz")),
        check_vma=False,
    )
```

```python
import jax
import jax.numpy as jnp
from jax import lax
from jax.experimental import pallas as pl
from jax.experimental.pallas import tpu as pltpu
from jax.sharding import PartitionSpec as P

SWEEPS = 8
JACOBI = 8
THETA = 7.125
DELTA = 6.875
LOG_GAIN = 2.0

COUNT_X = 16
COUNT_Y = 8
COUNT_Z = 4
CX, CY, CZ = 8, 32, 128
INSET = 96
MOST = 10
DEPTH = 8
WIN = MOST + 2 * DEPTH
NH = SWEEPS - 1
NPL = CX + 2 * NH
KPL = NPL - 2
YE = CY + 16
RING = 4

F32 = jnp.float32


def sweep_weights(count):
    ratio_base = THETA / DELTA
    ratio_now = 1.0 / ratio_base
    weights = []
    for index in range(count):
        ratio_next = 1.0 / (2.0 * ratio_base - ratio_now)
        weights.append((ratio_next * ratio_now, 2.0 * ratio_next / DELTA))
        ratio_now = ratio_next
    return weights


CUTS_AT = 3


def cut(info, tile):
    return info[CUTS_AT + 1 + tile]


def clamp(value, low, high):
    return jnp.minimum(jnp.maximum(value, low), high)


def turn(value, shift, axis):
    shift %= value.shape[axis]
    return value if shift == 0 else pltpu.roll(value, shift, axis)


PN = 2 * NH - 1


def pick_slab_kernel(spots, noise, kappa, carry, up, dn):
    at = jnp.where(lax.rem(spots[0], RING) == RING - 1, 1, 0)
    up[0:NH] = noise[CX - NH :]
    dn[0:NH] = noise[:NH]
    up[NH:] = kappa[CX - NH + 1 :]
    dn[NH:] = kappa[: NH - 1]
    for k in range(NH):
        carry[k] = noise[k + (CX - NH) * at]
    for k in range(NH - 1):
        carry[NH + k] = kappa[k + (CX - NH + 1) * at]


def pick_tile_kernel(info, press, source, up, dn, far, near2):
    ix = info[0]
    width = cut(info, ix + 1) - cut(info, ix)
    late = lax.rem(ix, RING) >= RING // 2
    for k in range(8):
        last = clamp(width - 8, 0, 2)
        up[k] = press[last + k]
        dn[k] = press[k]
        far[k] = press[jnp.where(late, last, 0) + k]
    for k in range(7):
        last = clamp(width - 7, 0, 3)
        up[8 + k] = source[last + k]
        dn[8 + k] = source[k]
        far[8 + k] = source[jnp.where(late, last, 0) + k]
    for k in range(6):
        near2[k] = press[jnp.where(late, 0, clamp(width - 6, 0, 4)) + k]
    for k in range(5):
        near2[6 + k] = source[jnp.where(late, 0, clamp(width - 5, 0, 5)) + k]


def side_rows(parts, yup, ydn):
    at = 0
    for part, planes in parts:
        for x in range(planes):
            yup[at] = part[x, CY - 8 :]
            ydn[at] = part[x, 0:8]
            at += 1


def join_slab_kernel(spots, noise, kappa, carry, up, dn, n_out, k_out, yup, ydn):
    place = lax.rem(spots[0], RING)
    h = NH - 1
    n_out[NH : NH + CX] = noise[...]
    k_out[h : h + CX] = kappa[...]
    for at_n, at_k, end, inner in ((0, 0, 0, up), (NH + CX, h + CX, RING - 1, dn)):
        @pl.when(place == end)
        def _(at_n=at_n, at_k=at_k):
            n_out[at_n : at_n + NH] = carry[0:NH]
            k_out[at_k : at_k + h] = carry[NH:]

        @pl.when(place != end)
        def _(at_n=at_n, at_k=at_k, inner=inner):
            n_out[at_n : at_n + NH] = inner[0:NH]
            k_out[at_k : at_k + h] = inner[NH:]

    side_rows(((n_out, NPL), (k_out, KPL)), yup, ydn)


LANES = 8
EACH = CZ // LANES


def groups(planes):
    return -(-planes // EACH)


def join_y_kernel(plane_counts, *refs):
    count = len(plane_counts)
    sources, (yup, ydn), outs, (zup, zdn) = refs[:count], refs[count : count + 2], refs[count + 2 : -2], refs[-2:]
    lane = lax.broadcasted_iota(jnp.int32, (YE, CZ), 1)
    at, begin = 0, 0
    for source, out, planes in zip(sources, outs, plane_counts):
        for x in range(planes):
            out[x, 0:8] = yup[at]
            out[x, 8 : 8 + CY] = source[x]
            out[x, 8 + CY :] = ydn[at]
            at += 1
        for g in range(groups(planes)):
            up = jnp.zeros((YE, CZ), F32)
            dn = jnp.zeros((YE, CZ), F32)
            for k in range(min(EACH, planes - g * EACH)):
                value = out[g * EACH + k]
                here = (lane >= LANES * k) & (lane < LANES * (k + 1))
                up = jnp.where(here, turn(value, LANES * (k + 1), 1), up)
                dn = jnp.where(here, turn(value, LANES * k, 1), dn)
            zup[begin : begin + YE] = up
            zdn[begin : begin + YE] = dn
            begin += YE


def z_halo(start, x, zup, zdn, lane):
    begin = (start + x // EACH) * YE
    k = x % EACH
    above = turn(zdn[begin : begin + YE], -LANES * k, 1)
    below = turn(zup[begin : begin + YE], -LANES * (k + 1), 1)
    return jnp.where(lane < LANES, above, jnp.where(lane >= CZ - LANES, below, 0.0))


def inside_bounds(iy, iz):
    low_y = jnp.where(iy == 0, 8, 0)
    high_y = jnp.where(iy == COUNT_Y - 1, 8 + CY, YE)
    left = jnp.where(iz == 0, 2 * CZ, 2 * CZ - LANES)
    right = jnp.where(iz == COUNT_Z - 1, CZ, CZ + LANES)
    return low_y, high_y, left, right


def chebyshev_kernel(info, n_in, k_in, zup, zdn, field, perm, extra, resid, kap, da, db, acc):
    ix, iy, iz = info[0], info[1], info[2]
    lane = lax.broadcasted_iota(jnp.int32, (YE, CZ), 1)
    for x in range(NPL):
        resid[x, :, 0:CZ] = n_in[x]
        resid[x, :, CZ:] = z_halo(0, x, zup, zdn, lane)
    for x in range(KPL):
        kap[x, :, 0:CZ] = k_in[x] + 6.0
        kap[x, :, CZ:] = z_halo(groups(NPL), x, zup, zdn, lane) + 6.0
    row = lax.broadcasted_iota(jnp.int32, (YE, 2 * CZ), 0)
    wide = lax.broadcasted_iota(jnp.int32, (YE, 2 * CZ), 1)
    low_y, high_y, left, right = inside_bounds(iy, iz)
    inside = (row >= low_y) & (row < high_y) & ((wide < right) | (wide >= left))
    mask = jnp.where(inside, 1.0, 0.0).astype(F32)

    def first(x, _):
        da[x] = resid[x] / THETA
        return 0

    for x in range(NPL):
        first(x, 0)
    for x in range(CX):
        acc[x] = da[NH + x]
    old, new = da, db
    for k, (a, b) in enumerate(sweep_weights(SWEEPS)[: SWEEPS - 1], 1):
        def plane(x, _, old=old, new=new, a=a, b=b):
            d = old[x]
            beside = old[x + 1] + old[x - 1]
            beside = beside + (pltpu.roll(d, YE - 1, 0) + pltpu.roll(d, 1, 0))
            beside = beside + (pltpu.roll(d, 2 * CZ - 1, 1) + pltpu.roll(d, 1, 1))
            r = resid[x] - (kap[x - 1] * d - beside)
            resid[x] = r
            at = ix * CX - NH + x
            scale = jnp.where((at >= 0) & (at < CX * COUNT_X), b, 0.0).astype(F32)
            new[x] = a * d + (scale * mask) * r
            return 0

        for x in range(k, NPL - k):
            plane(x, 0)
        for x in range(CX):
            acc[x] += new[NH + x]
        old, new = new, old
    for x in range(CX):
        value = acc[x, 8 : 8 + CY, 0:CZ]
        field[x] = value
        perm[x] = jnp.exp(LOG_GAIN * value)
    half = jnp.where(ix == LATE_EXTRA[0], CX // 2, 0)
    for r in range(CX // 2):
        extra[r] = perm[half + r]


ACROSS = [(4, 0), (5, 1), (8, 4), (9, 5), (12, 8), (3, 7), (6, 10), (7, 11), (10, 14), (11, 15)]
EARLY_EXTRA, LATE_EXTRA = (6, 3), (9, 12)


def window(info, tile):
    first = info[CUTS_AT]
    return first + cut(info, tile) - DEPTH, first + cut(info, tile + 1) + DEPTH - 1


def ring_plane(info, tile, device, r):
    low, high = window(info, tile)
    above = (device + RING) * CX + r <= high
    below = (device - RING) * CX + r >= low
    return above, below


def ring_kernel(info, own, moved, *outs):
    ix = info[0]
    place = lax.rem(ix, RING)
    for s, out in enumerate(outs, 1):
        tile = ix - place + lax.rem(place + s, RING)
        for r in range(CX):
            above, below = ring_plane(info, tile, ix, r)
            out[r] = jnp.where(above | below, moved[r], own[r])


def join_tile_kernel(info, own, moved, extra, ring1, ring2, ring3, press, source, up, dn, across, far2, near2, w_out, p_out, s_out, yup, ydn):
    ix = info[0]
    place = lax.rem(ix, RING)
    here = cut(info, ix)
    w_out[...] = jnp.ones_like(w_out)
    p_out[...] = jnp.zeros_like(p_out)
    s_out[...] = jnp.zeros_like(s_out)
    for s, ring in enumerate((own, ring1, ring2, ring3)):
        device = ix - place + lax.rem(place + RING - s, RING)
        direct_above = (ix == EARLY_EXTRA[1]) & (device + RING == EARLY_EXTRA[0])
        direct_below = (ix == LATE_EXTRA[1]) & (device - RING == LATE_EXTRA[0])
        for r in range(CX):
            above, below = ring_plane(info, ix, device, r)
            value = ring[r]
            if s == 0:
                value = jnp.where(above | below, moved[r], value)
            direct = (above & direct_above) | (below & direct_below)
            value = jnp.where(direct, extra[r % (CX // 2)], value)
            at = device + jnp.where(above, RING, jnp.where(below, -RING, 0))
            g = at * CX + r - info[CUTS_AT]
            q = g - here + DEPTH
            good = (g >= 0) & (g < INSET) & (q >= 0) & (q < WIN)
            w_out[jnp.where(good, q, WIN)] = value

    def put(out, tile, row, value):
        known = (tile >= 0) & (tile < COUNT_X)
        safe = clamp(tile, 0, COUNT_X - 1)
        begin, end = cut(info, safe), cut(info, safe + 1)
        at = begin + row - here + DEPTH
        good = known & (begin + row < end) & (at >= 0) & (at < WIN)
        out[jnp.where(good, at, WIN)] = value

    def skipped(tile, kept):
        safe = clamp(tile, 0, COUNT_X - 1)
        return jnp.maximum(cut(info, safe + 1) - cut(info, safe) - kept, 0)

    for k in range(MOST):
        put(p_out, ix, k, press[k])
        put(s_out, ix, k, source[k])
    def put_all(part, tile, ends, rows_p, rows_s):
        for k in range(rows_p):
            put(p_out, tile, jnp.where(ends, skipped(tile, rows_p), 0) + k, part[k])
        for k in range(rows_s):
            put(s_out, tile, jnp.where(ends, skipped(tile, rows_s), 0) + k, part[rows_p + k])

    first, final, late = place == 0, place == RING - 1, place >= RING // 2
    put_all(up, jnp.where(first, -1, ix - 1), True, 8, 7)
    put_all(dn, jnp.where(final, -1, ix + 1), False, 8, 7)
    put_all(across, jnp.where(first, ix - 1, jnp.where(final, ix + 1, -1)), first, 8, 7)
    put_all(far2, jnp.where(late, ix + 2, ix - 2), jnp.logical_not(late), 8, 7)
    put_all(near2, jnp.where(late, ix - 2, ix + 2), late, 6, 5)
    side_rows(((w_out, WIN), (p_out, WIN), (s_out, WIN)), yup, ydn)


def harmonic(own, other):
    return 2.0 * own * other / (own + other)


def jacobi_kernel(info, w_in, p_in, s_in, zup, zdn, out, perm, pa, pb, sc, cxm, cxp, cym, cyp, czm, czp):
    ix, iy, iz = info[0], info[1], info[2]
    here = cut(info, ix)
    count = cut(info, ix + 1) - here
    lane = lax.broadcasted_iota(jnp.int32, (YE, CZ), 1)
    for part, (src, dst) in enumerate(((w_in, perm), (p_in, pa), (s_in, sc))):
        for x in range(WIN):
            dst[x, :, 0:CZ] = src[x]
            dst[x, :, CZ:] = z_halo(part * groups(WIN), x, zup, zdn, lane)

    row = lax.broadcasted_iota(jnp.int32, (YE, 2 * CZ), 0)
    wide = lax.broadcasted_iota(jnp.int32, (YE, 2 * CZ), 1)
    low_y, high_y, left, right = inside_bounds(iy, iz)
    inside = (row >= low_y) & (row < high_y) & ((wide < right) | (wide >= left))
    has_ym = row != low_y
    has_yp = row != high_y - 1
    has_zm = wide != jnp.where(iz == 0, 0, 2 * CZ - LANES)
    has_zp = wide != right - 1

    def couple(q, _):
        g = here + q - DEPTH
        own = perm[q]
        live = inside & (g >= 0) & (g < INSET)
        txm = jnp.where(g > 0, harmonic(own, perm[q - 1]), own)
        txp = jnp.where(g < INSET - 1, harmonic(own, perm[q + 1]), own)
        ty = harmonic(own, pltpu.roll(own, 1, 0))
        tz = harmonic(own, pltpu.roll(own, 1, 1))
        tym = jnp.where(has_ym, ty, own)
        typ = jnp.where(has_yp, pltpu.roll(ty, YE - 1, 0), own)
        tzm = jnp.where(has_zm, tz, own)
        tzp = jnp.where(has_zp, pltpu.roll(tz, 2 * CZ - 1, 1), own)
        total = txm + txp + tym + typ + tzm + tzp

        def share(has, part):
            return jnp.where(live & has, part / total, 0.0)

        cxm[q] = share(g > 0, txm)
        cxp[q] = share(g < INSET - 1, txp)
        cym[q] = share(has_ym, tym)
        cyp[q] = share(has_yp, typ)
        czm[q] = share(has_zm, tzm)
        czp[q] = share(has_zp, tzp)
        sc[q] = share(True, sc[q])
        return 0

    for q in range(1, WIN - 1):
        couple(q, 0)

    old, new = pa, pb
    for sweep in range(1, JACOBI + 1):
        def plane(q, _, old=old, new=new):
            p = old[q]
            total = sc[q] + cxm[q] * old[q - 1] + cxp[q] * old[q + 1]
            total = total + cym[q] * pltpu.roll(p, 1, 0) + cyp[q] * pltpu.roll(p, YE - 1, 0)
            total = total + czm[q] * pltpu.roll(p, 1, 1) + czp[q] * pltpu.roll(p, 2 * CZ - 1, 1)
            new[q] = total
            return 0

        for q in range(sweep, WIN - sweep):
            plane(q, 0)
        old, new = new, old
    for r in range(MOST):
        out[r] = jnp.where(r < count, old[DEPTH + r, 8 : 8 + CY, 0:CZ], 0.0)


def call(kernel, args, outs, scratch=(), scalars=1, cost=1 << 20):
    smem = pl.BlockSpec(memory_space=pltpu.SMEM)
    vmem = pl.BlockSpec(memory_space=pltpu.VMEM)
    return pl.pallas_call(
        kernel,
        out_shape=[pltpu.VMEM(shape, F32) for shape in outs],
        in_specs=[smem] * scalars + [vmem] * (len(args) - scalars),
        out_specs=[vmem] * len(outs),
        scratch_shapes=[pltpu.VMEM(shape, F32) for shape in scratch],
        compiler_params=pltpu.CompilerParams(vmem_limit_bytes=56 << 20),
        cost_estimate=pl.CostEstimate(flops=64 * cost, transcendentals=0, bytes_accessed=cost),
    )(*args[:scalars], *[pltpu.with_memory_space_constraint(arg, pltpu.VMEM) for arg in args[scalars:]])


def shifted(value, axis, count, by):
    return lax.ppermute(value, axis, [(i, i + by) for i in range(count) if 0 <= i + by < count])


def ringed(value, s):
    return lax.ppermute(value, "gx", [(i, i - i % RING + (i + s) % RING) for i in range(COUNT_X)])


def join_y(plane_counts, parts, yup, ydn, beside=()):
    yup, ydn = shifted(yup, "gy", COUNT_Y, 1), shifted(ydn, "gy", COUNT_Y, -1)
    packed = (sum(groups(planes) for planes in plane_counts) * YE, CZ)

    def join_rows(*refs):
        join_y_kernel(plane_counts, *refs)

    *parts, zup, zdn = call(
        join_rows,
        (*parts, yup, ydn),
        [(planes, YE, CZ) for planes in plane_counts] + [packed, packed],
        scalars=0,
    )
    return beside, (*parts, shifted(zup, "gz", COUNT_Z, 1), shifted(zdn, "gz", COUNT_Z, -1))


def local(noise, kappa_sq, cuts, pressure_init, source):
    spots = jnp.stack([lax.axis_index("gx"), lax.axis_index("gy"), lax.axis_index("gz")]).astype(jnp.int32)
    info = jnp.concatenate([spots, cuts])
    plane = (CY, CZ)
    inner = [(i, i + 1) for i in range(COUNT_X) if (i + 1) % RING]
    outer = [(i, i + 1) for i in range(COUNT_X - 1) if (i + 1) % RING == 0]
    inner_dn, outer_dn = [(j, i) for i, j in inner], [(j, i) for i, j in outer]
    carry, up, dn = call(pick_slab_kernel, (spots, noise, kappa_sq), [(PN, *plane)] * 3)
    press, charge, carry, up, dn = lax.optimization_barrier((pressure_init, source, carry, up, dn))
    halo = (15, *plane)
    t_up, t_dn, far, near2 = call(pick_tile_kernel, (info, press, charge), [halo] * 3 + [(11, *plane)])
    carry = lax.ppermute(carry, "gx", outer + outer_dn)
    up, dn = lax.ppermute(up, "gx", inner), lax.ppermute(dn, "gx", inner_dn)
    t_up, t_dn = lax.ppermute(t_up, "gx", inner), lax.ppermute(t_dn, "gx", inner_dn)
    far = lax.ppermute(far, "gx", [(i, i + (3, 1, -1, -3)[i % RING]) for i in range(COUNT_X)])
    steps = [(i, i + (RING, RING, -RING, -RING)[i % RING]) for i in range(COUNT_X)]
    across = lax.ppermute(far, "gx", [(i, to) for i, to in steps if 0 <= to < COUNT_X])
    near2 = ringed(near2, 2)
    carry, near2 = lax.optimization_barrier((carry, near2))
    n, k, yup, ydn = call(
        join_slab_kernel,
        (spots, noise, kappa_sq, carry, up, dn),
        [(NPL, *plane), (KPL, *plane), (NPL + KPL, 8, CZ), (NPL + KPL, 8, CZ)],
    )
    across, (n, k, zup, zdn) = join_y((NPL, KPL), (n, k), yup, ydn, across)
    big = (NPL, YE, 2 * CZ)
    field, perm, extra = call(
        chebyshev_kernel,
        (info, n, k, zup, zdn),
        [(CX, *plane), (CX, *plane), (CX // 2, *plane)],
        [big, (KPL, YE, 2 * CZ), big, big, (CX, YE, 2 * CZ)],
        cost=40 << 20,
    )
    moved = lax.ppermute(perm, "gx", ACROSS)
    extra = lax.ppermute(extra, "gx", [EARLY_EXTRA, LATE_EXTRA])
    moved, extra, across = lax.optimization_barrier((moved, extra, across))
    far2 = lax.ppermute(across, "gx", [(i, i ^ 1) for i in range(COUNT_X)])
    rings = call(ring_kernel, (info, perm, moved), [(CX, *plane)] * (RING - 1))
    rings = [ringed(value, s) for s, value in enumerate(rings, 1)]
    rows = (3 * WIN, 8, CZ)
    w, p, s, yup, ydn = call(
        join_tile_kernel,
        (info, perm, moved, extra, *rings, pressure_init, source, t_up, t_dn, across, far2, near2),
        [(WIN + 1, *plane)] * 3 + [rows, rows],
    )
    _, (w, p, s, zup, zdn) = join_y((WIN, WIN, WIN), (w, p, s), yup, ydn)
    room = (WIN + 1, YE, 2 * CZ)
    (pressure,) = call(jacobi_kernel, (info, w, p, s, zup, zdn), [(MOST, *plane)], [room] * 10)
    return (field, pressure)


def solution(mesh):
    placed = (P("gx", "gy", "gz"), P("gx", "gy", "gz"), P(), P("gx", "gy", "gz"), P("gx", "gy", "gz"))
    return jax.shard_map(
        local,
        mesh=mesh,
        in_specs=placed,
        out_specs=(P("gx", "gy", "gz"), P("gx", "gy", "gz")),
        check_vma=False,
    )
```

```python
import jax
import jax.numpy as jnp
from jax import lax
from jax.experimental import pallas as pl
from jax.experimental.pallas import tpu as pltpu
from jax.sharding import PartitionSpec as P

SWEEPS = 8
JACOBI = 8
THETA = 7.125
DELTA = 6.875
LOG_GAIN = 2.0

COUNT_X = 16
COUNT_Y = 8
COUNT_Z = 4
CX, CY, CZ = 8, 32, 128
INSET = 96
MOST = 10
DEPTH = 8
WIN = MOST + 2 * DEPTH
NH = SWEEPS - 1
NPL = CX + 2 * NH
KPL = NPL - 2
YE = CY + 16
RING = 4

F32 = jnp.float32


def sweep_weights(count):
    ratio_base = THETA / DELTA
    ratio_now = 1.0 / ratio_base
    weights = []
    for index in range(count):
        ratio_next = 1.0 / (2.0 * ratio_base - ratio_now)
        weights.append((ratio_next * ratio_now, 2.0 * ratio_next / DELTA))
        ratio_now = ratio_next
    return weights


CUTS_AT = 3


def cut(info, tile):
    return info[CUTS_AT + 1 + tile]


def clamp(value, low, high):
    return jnp.minimum(jnp.maximum(value, low), high)


def turn(value, shift, axis):
    shift %= value.shape[axis]
    return value if shift == 0 else pltpu.roll(value, shift, axis)


PN = 2 * NH - 1


def pick_slab_kernel(spots, noise, kappa, carry, up, dn):
    at = jnp.where(lax.rem(spots[0], RING) == RING - 1, 1, 0)
    up[0:NH] = noise[CX - NH :]
    dn[0:NH] = noise[:NH]
    up[NH:] = kappa[CX - NH + 1 :]
    dn[NH:] = kappa[: NH - 1]
    for k in range(NH):
        carry[k] = noise[k + (CX - NH) * at]
    for k in range(NH - 1):
        carry[NH + k] = kappa[k + (CX - NH + 1) * at]


def pick_tile_kernel(info, press, source, up, dn, far, near2):
    ix = info[0]
    width = cut(info, ix + 1) - cut(info, ix)
    late = lax.rem(ix, RING) >= RING // 2
    for k in range(8):
        last = clamp(width - 8, 0, 2)
        up[k] = press[last + k]
        dn[k] = press[k]
        far[k] = press[jnp.where(late, last, 0) + k]
    for k in range(7):
        last = clamp(width - 7, 0, 3)
        up[8 + k] = source[last + k]
        dn[8 + k] = source[k]
        far[8 + k] = source[jnp.where(late, last, 0) + k]
    for k in range(6):
        near2[k] = press[jnp.where(late, 0, clamp(width - 6, 0, 4)) + k]
    for k in range(5):
        near2[6 + k] = source[jnp.where(late, 0, clamp(width - 5, 0, 5)) + k]


def side_rows(parts, yup, ydn):
    at = 0
    for part, planes in parts:
        for x in range(planes):
            yup[at] = part[x, CY - 8 :]
            ydn[at] = part[x, 0:8]
            at += 1


def join_slab_kernel(spots, noise, kappa, carry, up, dn, n_out, k_out, yup, ydn):
    place = lax.rem(spots[0], RING)
    h = NH - 1
    n_out[NH : NH + CX] = noise[...]
    k_out[h : h + CX] = kappa[...]
    for at_n, at_k, end, inner in ((0, 0, 0, up), (NH + CX, h + CX, RING - 1, dn)):
        @pl.when(place == end)
        def _(at_n=at_n, at_k=at_k):
            n_out[at_n : at_n + NH] = carry[0:NH]
            k_out[at_k : at_k + h] = carry[NH:]

        @pl.when(place != end)
        def _(at_n=at_n, at_k=at_k, inner=inner):
            n_out[at_n : at_n + NH] = inner[0:NH]
            k_out[at_k : at_k + h] = inner[NH:]

    side_rows(((n_out, NPL), (k_out, KPL)), yup, ydn)


LANES = 8
EACH = CZ // LANES


def groups(planes):
    return -(-planes // EACH)


def join_y_kernel(plane_counts, *refs):
    count = len(plane_counts)
    sources, (yup, ydn), outs, (zup, zdn) = refs[:count], refs[count : count + 2], refs[count + 2 : -2], refs[-2:]
    lane = lax.broadcasted_iota(jnp.int32, (YE, CZ), 1)
    at, begin = 0, 0
    for source, out, planes in zip(sources, outs, plane_counts):
        for x in range(planes):
            out[x, 0:8] = yup[at]
            out[x, 8 : 8 + CY] = source[x]
            out[x, 8 + CY :] = ydn[at]
            at += 1
        for g in range(groups(planes)):
            up = jnp.zeros((YE, CZ), F32)
            dn = jnp.zeros((YE, CZ), F32)
            for k in range(min(EACH, planes - g * EACH)):
                value = out[g * EACH + k]
                here = (lane >= LANES * k) & (lane < LANES * (k + 1))
                up = jnp.where(here, turn(value, LANES * (k + 1), 1), up)
                dn = jnp.where(here, turn(value, LANES * k, 1), dn)
            zup[begin : begin + YE] = up
            zdn[begin : begin + YE] = dn
            begin += YE


def z_halo(start, x, zup, zdn, lane):
    begin = (start + x // EACH) * YE
    k = x % EACH
    above = turn(zdn[begin : begin + YE], -LANES * k, 1)
    below = turn(zup[begin : begin + YE], -LANES * (k + 1), 1)
    return jnp.where(lane < LANES, above, jnp.where(lane >= CZ - LANES, below, 0.0))


def inside_bounds(iy, iz):
    low_y = jnp.where(iy == 0, 8, 0)
    high_y = jnp.where(iy == COUNT_Y - 1, 8 + CY, YE)
    left = jnp.where(iz == 0, 2 * CZ, 2 * CZ - LANES)
    right = jnp.where(iz == COUNT_Z - 1, CZ, CZ + LANES)
    return low_y, high_y, left, right


def chebyshev_kernel(info, n_in, k_in, zup, zdn, field, perm, extra, resid, kap, da, db, acc):
    ix, iy, iz = info[0], info[1], info[2]
    lane = lax.broadcasted_iota(jnp.int32, (YE, CZ), 1)
    for x in range(NPL):
        resid[x, :, 0:CZ] = n_in[x]
        resid[x, :, CZ:] = z_halo(0, x, zup, zdn, lane)
    for x in range(KPL):
        kap[x, :, 0:CZ] = k_in[x] + 6.0
        kap[x, :, CZ:] = z_halo(groups(NPL), x, zup, zdn, lane) + 6.0
    row = lax.broadcasted_iota(jnp.int32, (YE, 2 * CZ), 0)
    wide = lax.broadcasted_iota(jnp.int32, (YE, 2 * CZ), 1)
    low_y, high_y, left, right = inside_bounds(iy, iz)
    inside = (row >= low_y) & (row < high_y) & ((wide < right) | (wide >= left))
    mask = jnp.where(inside, 1.0, 0.0).astype(F32)

    def first(x, _):
        da[x] = resid[x] / THETA
        return 0

    for x in range(NPL):
        first(x, 0)
    for x in range(CX):
        acc[x] = da[NH + x]
    old, new = da, db
    for k, (a, b) in enumerate(sweep_weights(SWEEPS)[: SWEEPS - 1], 1):
        def plane(x, _, old=old, new=new, a=a, b=b):
            d = old[x]
            beside = old[x + 1] + old[x - 1]
            beside = beside + (pltpu.roll(d, YE - 1, 0) + pltpu.roll(d, 1, 0))
            beside = beside + (pltpu.roll(d, 2 * CZ - 1, 1) + pltpu.roll(d, 1, 1))
            r = resid[x] - (kap[x - 1] * d - beside)
            resid[x] = r
            at = ix * CX - NH + x
            scale = jnp.where((at >= 0) & (at < CX * COUNT_X), b, 0.0).astype(F32)
            new[x] = a * d + (scale * mask) * r
            return 0

        for x in range(k, NPL - k):
            plane(x, 0)
        for x in range(CX):
            acc[x] += new[NH + x]
        old, new = new, old
    for x in range(CX):
        value = acc[x, 8 : 8 + CY, 0:CZ]
        field[x] = value
        perm[x] = jnp.exp(LOG_GAIN * value)
    half = jnp.where(ix == LATE_EXTRA[0], CX // 2, 0)
    for r in range(CX // 2):
        extra[r] = perm[half + r]


ACROSS = [(4, 0), (5, 1), (8, 4), (9, 5), (12, 8), (3, 7), (6, 10), (7, 11), (10, 14), (11, 15)]
EARLY_EXTRA, LATE_EXTRA = (6, 3), (9, 12)


def window(info, tile):
    first = info[CUTS_AT]
    return first + cut(info, tile) - DEPTH, first + cut(info, tile + 1) + DEPTH - 1


def ring_plane(info, tile, device, r):
    low, high = window(info, tile)
    above = (device + RING) * CX + r <= high
    below = (device - RING) * CX + r >= low
    return above, below


def ring_kernel(info, own, moved, *outs):
    ix = info[0]
    place = lax.rem(ix, RING)
    for s, out in enumerate(outs, 1):
        tile = ix - place + lax.rem(place + s, RING)
        for r in range(CX):
            above, below = ring_plane(info, tile, ix, r)
            out[r] = jnp.where(above | below, moved[r], own[r])


def join_tile_kernel(info, own, moved, extra, ring1, ring2, ring3, press, source, up, dn, across, far2, near2, w_out, p_out, s_out, yup, ydn):
    ix = info[0]
    place = lax.rem(ix, RING)
    here = cut(info, ix)
    w_out[...] = jnp.ones_like(w_out)
    p_out[...] = jnp.zeros_like(p_out)
    s_out[...] = jnp.zeros_like(s_out)
    for s, ring in enumerate((own, ring1, ring2, ring3)):
        device = ix - place + lax.rem(place + RING - s, RING)
        direct_above = (ix == EARLY_EXTRA[1]) & (device + RING == EARLY_EXTRA[0])
        direct_below = (ix == LATE_EXTRA[1]) & (device - RING == LATE_EXTRA[0])
        for r in range(CX):
            above, below = ring_plane(info, ix, device, r)
            value = ring[r]
            if s == 0:
                value = jnp.where(above | below, moved[r], value)
            direct = (above & direct_above) | (below & direct_below)
            value = jnp.where(direct, extra[r % (CX // 2)], value)
            at = device + jnp.where(above, RING, jnp.where(below, -RING, 0))
            g = at * CX + r - info[CUTS_AT]
            q = g - here + DEPTH
            good = (g >= 0) & (g < INSET) & (q >= 0) & (q < WIN)
            w_out[jnp.where(good, q, WIN)] = value

    def put(out, tile, row, value):
        known = (tile >= 0) & (tile < COUNT_X)
        safe = clamp(tile, 0, COUNT_X - 1)
        begin, end = cut(info, safe), cut(info, safe + 1)
        at = begin + row - here + DEPTH
        good = known & (begin + row < end) & (at >= 0) & (at < WIN)
        out[jnp.where(good, at, WIN)] = value

    def skipped(tile, kept):
        safe = clamp(tile, 0, COUNT_X - 1)
        return jnp.maximum(cut(info, safe + 1) - cut(info, safe) - kept, 0)

    for k in range(MOST):
        put(p_out, ix, k, press[k])
        put(s_out, ix, k, source[k])
    def put_all(part, tile, ends, rows_p, rows_s):
        for k in range(rows_p):
            put(p_out, tile, jnp.where(ends, skipped(tile, rows_p), 0) + k, part[k])
        for k in range(rows_s):
            put(s_out, tile, jnp.where(ends, skipped(tile, rows_s), 0) + k, part[rows_p + k])

    first, final, late = place == 0, place == RING - 1, place >= RING // 2
    put_all(up, jnp.where(first, -1, ix - 1), True, 8, 7)
    put_all(dn, jnp.where(final, -1, ix + 1), False, 8, 7)
    put_all(across, jnp.where(first, ix - 1, jnp.where(final, ix + 1, -1)), first, 8, 7)
    put_all(far2, jnp.where(late, ix + 2, ix - 2), jnp.logical_not(late), 8, 7)
    put_all(near2, jnp.where(late, ix - 2, ix + 2), late, 6, 5)
    side_rows(((w_out, WIN), (p_out, WIN), (s_out, WIN)), yup, ydn)


def harmonic(own, other):
    return 2.0 * own * other / (own + other)


def jacobi_kernel(info, w_in, p_in, s_in, zup, zdn, out, perm, pa, pb, sc, cxm, cxp, cym, cyp, czm, czp):
    ix, iy, iz = info[0], info[1], info[2]
    here = cut(info, ix)
    count = cut(info, ix + 1) - here
    lane = lax.broadcasted_iota(jnp.int32, (YE, CZ), 1)
    for part, (src, dst) in enumerate(((w_in, perm), (p_in, pa), (s_in, sc))):
        for x in range(WIN):
            dst[x, :, 0:CZ] = src[x]
            dst[x, :, CZ:] = z_halo(part * groups(WIN), x, zup, zdn, lane)

    row = lax.broadcasted_iota(jnp.int32, (YE, 2 * CZ), 0)
    wide = lax.broadcasted_iota(jnp.int32, (YE, 2 * CZ), 1)
    low_y, high_y, left, right = inside_bounds(iy, iz)
    inside = (row >= low_y) & (row < high_y) & ((wide < right) | (wide >= left))
    has_ym = row != low_y
    has_yp = row != high_y - 1
    has_zm = wide != jnp.where(iz == 0, 0, 2 * CZ - LANES)
    has_zp = wide != right - 1

    def couple(q, _):
        g = here + q - DEPTH
        own = perm[q]
        live = inside & (g >= 0) & (g < INSET)
        txm = jnp.where(g > 0, harmonic(own, perm[q - 1]), own)
        txp = jnp.where(g < INSET - 1, harmonic(own, perm[q + 1]), own)
        ty = harmonic(own, pltpu.roll(own, 1, 0))
        tz = harmonic(own, pltpu.roll(own, 1, 1))
        tym = jnp.where(has_ym, ty, own)
        typ = jnp.where(has_yp, pltpu.roll(ty, YE - 1, 0), own)
        tzm = jnp.where(has_zm, tz, own)
        tzp = jnp.where(has_zp, pltpu.roll(tz, 2 * CZ - 1, 1), own)
        total = txm + txp + tym + typ + tzm + tzp

        def share(has, part):
            return jnp.where(live & has, part / total, 0.0)

        cxm[q] = share(g > 0, txm)
        cxp[q] = share(g < INSET - 1, txp)
        cym[q] = share(has_ym, tym)
        cyp[q] = share(has_yp, typ)
        czm[q] = share(has_zm, tzm)
        czp[q] = share(has_zp, tzp)
        sc[q] = share(True, sc[q])
        return 0

    for q in range(1, WIN - 1):
        couple(q, 0)

    old, new = pa, pb
    for sweep in range(1, JACOBI + 1):
        def plane(q, _, old=old, new=new):
            p = old[q]
            total = sc[q] + cxm[q] * old[q - 1] + cxp[q] * old[q + 1]
            total = total + cym[q] * pltpu.roll(p, 1, 0) + cyp[q] * pltpu.roll(p, YE - 1, 0)
            total = total + czm[q] * pltpu.roll(p, 1, 1) + czp[q] * pltpu.roll(p, 2 * CZ - 1, 1)
            new[q] = total
            return 0

        for q in range(sweep, WIN - sweep):
            plane(q, 0)
        old, new = new, old
    for r in range(MOST):
        out[r] = jnp.where(r < count, old[DEPTH + r, 8 : 8 + CY, 0:CZ], 0.0)


def call(kernel, args, outs, scratch=(), scalars=1, cost=1 << 20):
    smem = pl.BlockSpec(memory_space=pltpu.SMEM)
    vmem = pl.BlockSpec(memory_space=pltpu.VMEM)
    return pl.pallas_call(
        kernel,
        out_shape=[pltpu.VMEM(shape, F32) for shape in outs],
        in_specs=[smem] * scalars + [vmem] * (len(args) - scalars),
        out_specs=[vmem] * len(outs),
        scratch_shapes=[pltpu.VMEM(shape, F32) for shape in scratch],
        compiler_params=pltpu.CompilerParams(vmem_limit_bytes=56 << 20),
        cost_estimate=pl.CostEstimate(flops=64 * cost, transcendentals=0, bytes_accessed=cost),
    )(*args[:scalars], *[pltpu.with_memory_space_constraint(arg, pltpu.VMEM) for arg in args[scalars:]])


def shifted(value, axis, count, by):
    return lax.ppermute(value, axis, [(i, i + by) for i in range(count) if 0 <= i + by < count])


def ringed(value, s):
    return lax.ppermute(value, "gx", [(i, i - i % RING + (i + s) % RING) for i in range(COUNT_X)])


def join_y(plane_counts, parts, yup, ydn, beside=()):
    yup, ydn = shifted(yup, "gy", COUNT_Y, 1), shifted(ydn, "gy", COUNT_Y, -1)
    yup, ydn, beside = lax.optimization_barrier((yup, ydn, beside))
    packed = (sum(groups(planes) for planes in plane_counts) * YE, CZ)

    def join_rows(*refs):
        join_y_kernel(plane_counts, *refs)

    *parts, zup, zdn = call(
        join_rows,
        (*parts, yup, ydn),
        [(planes, YE, CZ) for planes in plane_counts] + [packed, packed],
        scalars=0,
    )
    return beside, (*parts, shifted(zup, "gz", COUNT_Z, 1), shifted(zdn, "gz", COUNT_Z, -1))


def local(noise, kappa_sq, cuts, pressure_init, source):
    spots = jnp.stack([lax.axis_index("gx"), lax.axis_index("gy"), lax.axis_index("gz")]).astype(jnp.int32)
    info = jnp.concatenate([spots, cuts])
    plane = (CY, CZ)
    inner = [(i, i + 1) for i in range(COUNT_X) if (i + 1) % RING]
    outer = [(i, i + 1) for i in range(COUNT_X - 1) if (i + 1) % RING == 0]
    inner_dn, outer_dn = [(j, i) for i, j in inner], [(j, i) for i, j in outer]
    carry, up, dn = call(pick_slab_kernel, (spots, noise, kappa_sq), [(PN, *plane)] * 3)
    press, charge, carry, up, dn = lax.optimization_barrier((pressure_init, source, carry, up, dn))
    halo = (15, *plane)
    t_up, t_dn, far, near2 = call(pick_tile_kernel, (info, press, charge), [halo] * 3 + [(11, *plane)])
    carry = lax.ppermute(carry, "gx", outer + outer_dn)
    up, dn = lax.ppermute(up, "gx", inner), lax.ppermute(dn, "gx", inner_dn)
    t_up, t_dn = lax.ppermute(t_up, "gx", inner), lax.ppermute(t_dn, "gx", inner_dn)
    far = lax.ppermute(far, "gx", [(i, i + (3, 1, -1, -3)[i % RING]) for i in range(COUNT_X)])
    steps = [(i, i + (RING, RING, -RING, -RING)[i % RING]) for i in range(COUNT_X)]
    across = lax.ppermute(far, "gx", [(i, to) for i, to in steps if 0 <= to < COUNT_X])
    near2 = ringed(near2, 2)
    carry, near2 = lax.optimization_barrier((carry, near2))
    n, k, yup, ydn = call(
        join_slab_kernel,
        (spots, noise, kappa_sq, carry, up, dn),
        [(NPL, *plane), (KPL, *plane), (NPL + KPL, 8, CZ), (NPL + KPL, 8, CZ)],
    )
    (t_up, t_dn), (n, k, zup, zdn) = join_y((NPL, KPL), (n, k), yup, ydn, (t_up, t_dn))
    big = (NPL, YE, 2 * CZ)
    field, perm, extra = call(
        chebyshev_kernel,
        (info, n, k, zup, zdn),
        [(CX, *plane), (CX, *plane), (CX // 2, *plane)],
        [big, (KPL, YE, 2 * CZ), big, big, (CX, YE, 2 * CZ)],
        cost=1 << 20,
    )
    moved = lax.ppermute(perm, "gx", ACROSS)
    extra = lax.ppermute(extra, "gx", [EARLY_EXTRA, LATE_EXTRA])
    moved, extra, across = lax.optimization_barrier((moved, extra, across))
    far2 = lax.ppermute(across, "gx", [(i, i ^ 1) for i in range(COUNT_X)])
    rings = call(ring_kernel, (info, perm, moved), [(CX, *plane)] * (RING - 1))
    rings = [ringed(value, s) for s, value in enumerate(rings, 1)]
    rows = (3 * WIN, 8, CZ)
    w, p, s, yup, ydn = call(
        join_tile_kernel,
        (info, perm, moved, extra, *rings, pressure_init, source, t_up, t_dn, across, far2, near2),
        [(WIN + 1, *plane)] * 3 + [rows, rows],
    )
    _, (w, p, s, zup, zdn) = join_y((WIN, WIN, WIN), (w, p, s), yup, ydn)
    room = (WIN + 1, YE, 2 * CZ)
    (pressure,) = call(jacobi_kernel, (info, w, p, s, zup, zdn), [(MOST, *plane)], [room] * 10)
    return (field, pressure)


def solution(mesh):
    placed = (P("gx", "gy", "gz"), P("gx", "gy", "gz"), P(), P("gx", "gy", "gz"), P("gx", "gy", "gz"))
    return jax.shard_map(
        local,
        mesh=mesh,
        in_specs=placed,
        out_specs=(P("gx", "gy", "gz"), P("gx", "gy", "gz")),
        check_vma=False,
    )
```

```python
import jax
import jax.numpy as jnp
from jax import lax
from jax.experimental import pallas as pl
from jax.experimental.pallas import tpu as pltpu
from jax.sharding import PartitionSpec as P

SWEEPS = 8
JACOBI = 8
THETA = 7.125
DELTA = 6.875
LOG_GAIN = 2.0

COUNT_X = 16
COUNT_Y = 8
COUNT_Z = 4
CX, CY, CZ = 8, 32, 128
INSET = 96
MOST = 10
DEPTH = 8
WIN = MOST + 2 * DEPTH
NH = SWEEPS - 1
NPL = CX + 2 * NH
KPL = NPL - 2
YE = CY + 16
RING = 4

F32 = jnp.float32


def sweep_weights(count):
    ratio_base = THETA / DELTA
    ratio_now = 1.0 / ratio_base
    weights = []
    for index in range(count):
        ratio_next = 1.0 / (2.0 * ratio_base - ratio_now)
        weights.append((ratio_next * ratio_now, 2.0 * ratio_next / DELTA))
        ratio_now = ratio_next
    return weights


CUTS_AT = 3


def cut(info, tile):
    return info[CUTS_AT + 1 + tile]


def clamp(value, low, high):
    return jnp.minimum(jnp.maximum(value, low), high)


def turn(value, shift, axis):
    shift %= value.shape[axis]
    return value if shift == 0 else pltpu.roll(value, shift, axis)


PN = 2 * NH - 1


def pick_slab_kernel(spots, noise, kappa, carry, up, dn):
    at = jnp.where(lax.rem(spots[0], RING) == RING - 1, 1, 0)
    up[0:NH] = noise[CX - NH :]
    dn[0:NH] = noise[:NH]
    up[NH:] = kappa[CX - NH + 1 :]
    dn[NH:] = kappa[: NH - 1]
    for k in range(NH):
        carry[k] = noise[k + (CX - NH) * at]
    for k in range(NH - 1):
        carry[NH + k] = kappa[k + (CX - NH + 1) * at]


def pick_tile_kernel(info, press, source, up, dn, far, near2):
    ix = info[0]
    width = cut(info, ix + 1) - cut(info, ix)
    late = lax.rem(ix, RING) >= RING // 2
    for k in range(8):
        last = clamp(width - 8, 0, 2)
        up[k] = press[last + k]
        dn[k] = press[k]
        far[k] = press[jnp.where(late, last, 0) + k]
    for k in range(7):
        last = clamp(width - 7, 0, 3)
        up[8 + k] = source[last + k]
        dn[8 + k] = source[k]
        far[8 + k] = source[jnp.where(late, last, 0) + k]
    for k in range(6):
        near2[k] = press[jnp.where(late, 0, clamp(width - 6, 0, 4)) + k]
    for k in range(5):
        near2[6 + k] = source[jnp.where(late, 0, clamp(width - 5, 0, 5)) + k]


def side_rows(parts, yup, ydn):
    at = 0
    for part, planes in parts:
        for x in range(planes):
            yup[at] = part[x, CY - 8 :]
            ydn[at] = part[x, 0:8]
            at += 1


def join_slab_kernel(spots, noise, kappa, carry, up, dn, n_out, k_out, yup, ydn):
    place = lax.rem(spots[0], RING)
    h = NH - 1
    n_out[NH : NH + CX] = noise[...]
    k_out[h : h + CX] = kappa[...]
    for at_n, at_k, end, inner in ((0, 0, 0, up), (NH + CX, h + CX, RING - 1, dn)):
        @pl.when(place == end)
        def _(at_n=at_n, at_k=at_k):
            n_out[at_n : at_n + NH] = carry[0:NH]
            k_out[at_k : at_k + h] = carry[NH:]

        @pl.when(place != end)
        def _(at_n=at_n, at_k=at_k, inner=inner):
            n_out[at_n : at_n + NH] = inner[0:NH]
            k_out[at_k : at_k + h] = inner[NH:]

    side_rows(((n_out, NPL), (k_out, KPL)), yup, ydn)


LANES = 8
EACH = CZ // LANES


def groups(planes):
    return -(-planes // EACH)


def join_y_kernel(plane_counts, *refs):
    count = len(plane_counts)
    sources, (yup, ydn), outs, (zup, zdn) = refs[:count], refs[count : count + 2], refs[count + 2 : -2], refs[-2:]
    lane = lax.broadcasted_iota(jnp.int32, (YE, CZ), 1)
    at, begin = 0, 0
    for source, out, planes in zip(sources, outs, plane_counts):
        for x in range(planes):
            out[x, 0:8] = yup[at]
            out[x, 8 : 8 + CY] = source[x]
            out[x, 8 + CY :] = ydn[at]
            at += 1
        for g in range(groups(planes)):
            up = jnp.zeros((YE, CZ), F32)
            dn = jnp.zeros((YE, CZ), F32)
            for k in range(min(EACH, planes - g * EACH)):
                value = out[g * EACH + k]
                here = (lane >= LANES * k) & (lane < LANES * (k + 1))
                up = jnp.where(here, turn(value, LANES * (k + 1), 1), up)
                dn = jnp.where(here, turn(value, LANES * k, 1), dn)
            zup[begin : begin + YE] = up
            zdn[begin : begin + YE] = dn
            begin += YE


def z_halo(start, x, zup, zdn, lane):
    begin = (start + x // EACH) * YE
    k = x % EACH
    above = turn(zdn[begin : begin + YE], -LANES * k, 1)
    below = turn(zup[begin : begin + YE], -LANES * (k + 1), 1)
    return jnp.where(lane < LANES, above, jnp.where(lane >= CZ - LANES, below, 0.0))


def inside_bounds(iy, iz):
    low_y = jnp.where(iy == 0, 8, 0)
    high_y = jnp.where(iy == COUNT_Y - 1, 8 + CY, YE)
    left = jnp.where(iz == 0, 2 * CZ, 2 * CZ - LANES)
    right = jnp.where(iz == COUNT_Z - 1, CZ, CZ + LANES)
    return low_y, high_y, left, right


def chebyshev_kernel(info, n_in, k_in, zup, zdn, field, perm, extra, resid, kap, da, db, acc):
    ix, iy, iz = info[0], info[1], info[2]
    lane = lax.broadcasted_iota(jnp.int32, (YE, CZ), 1)
    for x in range(NPL):
        resid[x, :, 0:CZ] = n_in[x]
        resid[x, :, CZ:] = z_halo(0, x, zup, zdn, lane)
    for x in range(KPL):
        kap[x, :, 0:CZ] = k_in[x] + 6.0
        kap[x, :, CZ:] = z_halo(groups(NPL), x, zup, zdn, lane) + 6.0
    row = lax.broadcasted_iota(jnp.int32, (YE, 2 * CZ), 0)
    wide = lax.broadcasted_iota(jnp.int32, (YE, 2 * CZ), 1)
    low_y, high_y, left, right = inside_bounds(iy, iz)
    inside = (row >= low_y) & (row < high_y) & ((wide < right) | (wide >= left))
    mask = jnp.where(inside, 1.0, 0.0).astype(F32)

    def first(x, _):
        da[x] = resid[x] / THETA
        return 0

    for x in range(NPL):
        first(x, 0)
    for x in range(CX):
        acc[x] = da[NH + x]
    old, new = da, db
    for k, (a, b) in enumerate(sweep_weights(SWEEPS)[: SWEEPS - 1], 1):
        def plane(x, _, old=old, new=new, a=a, b=b):
            d = old[x]
            beside = old[x + 1] + old[x - 1]
            beside = beside + (pltpu.roll(d, YE - 1, 0) + pltpu.roll(d, 1, 0))
            beside = beside + (pltpu.roll(d, 2 * CZ - 1, 1) + pltpu.roll(d, 1, 1))
            r = resid[x] - (kap[x - 1] * d - beside)
            resid[x] = r
            at = ix * CX - NH + x
            scale = jnp.where((at >= 0) & (at < CX * COUNT_X), b, 0.0).astype(F32)
            new[x] = a * d + (scale * mask) * r
            return 0

        for x in range(k, NPL - k):
            plane(x, 0)
        for x in range(CX):
            acc[x] += new[NH + x]
        old, new = new, old
    for x in range(CX):
        value = acc[x, 8 : 8 + CY, 0:CZ]
        field[x] = value
        perm[x] = jnp.exp(LOG_GAIN * value)
    half = jnp.where(ix == LATE_EXTRA[0], CX // 2, 0)
    for r in range(CX // 2):
        extra[r] = perm[half + r]


ACROSS = [(4, 0), (5, 1), (8, 4), (9, 5), (12, 8), (3, 7), (6, 10), (7, 11), (10, 14), (11, 15)]
EARLY_EXTRA, LATE_EXTRA = (6, 3), (9, 12)


def window(info, tile):
    first = info[CUTS_AT]
    return first + cut(info, tile) - DEPTH, first + cut(info, tile + 1) + DEPTH - 1


def ring_plane(info, tile, device, r):
    low, high = window(info, tile)
    above = (device + RING) * CX + r <= high
    below = (device - RING) * CX + r >= low
    return above, below


def ring_kernel(info, own, moved, *outs):
    ix = info[0]
    place = lax.rem(ix, RING)
    for s, out in enumerate(outs, 1):
        tile = ix - place + lax.rem(place + s, RING)
        for r in range(CX):
            above, below = ring_plane(info, tile, ix, r)
            out[r] = jnp.where(above | below, moved[r], own[r])


def join_tile_kernel(info, own, moved, extra, ring1, ring2, ring3, press, source, up, dn, across, far2, near2, w_out, p_out, s_out, yup, ydn):
    ix = info[0]
    place = lax.rem(ix, RING)
    here = cut(info, ix)
    w_out[...] = jnp.ones_like(w_out)
    p_out[...] = jnp.zeros_like(p_out)
    s_out[...] = jnp.zeros_like(s_out)
    for s, ring in enumerate((own, ring1, ring2, ring3)):
        device = ix - place + lax.rem(place + RING - s, RING)
        direct_above = (ix == EARLY_EXTRA[1]) & (device + RING == EARLY_EXTRA[0])
        direct_below = (ix == LATE_EXTRA[1]) & (device - RING == LATE_EXTRA[0])
        for r in range(CX):
            above, below = ring_plane(info, ix, device, r)
            value = ring[r]
            if s == 0:
                value = jnp.where(above | below, moved[r], value)
            direct = (above & direct_above) | (below & direct_below)
            value = jnp.where(direct, extra[r % (CX // 2)], value)
            at = device + jnp.where(above, RING, jnp.where(below, -RING, 0))
            g = at * CX + r - info[CUTS_AT]
            q = g - here + DEPTH
            good = (g >= 0) & (g < INSET) & (q >= 0) & (q < WIN)
            w_out[jnp.where(good, q, WIN)] = value

    def put(out, tile, row, value):
        known = (tile >= 0) & (tile < COUNT_X)
        safe = clamp(tile, 0, COUNT_X - 1)
        begin, end = cut(info, safe), cut(info, safe + 1)
        at = begin + row - here + DEPTH
        good = known & (begin + row < end) & (at >= 0) & (at < WIN)
        out[jnp.where(good, at, WIN)] = value

    def skipped(tile, kept):
        safe = clamp(tile, 0, COUNT_X - 1)
        return jnp.maximum(cut(info, safe + 1) - cut(info, safe) - kept, 0)

    for k in range(MOST):
        put(p_out, ix, k, press[k])
        put(s_out, ix, k, source[k])
    def put_all(part, tile, ends, rows_p, rows_s):
        for k in range(rows_p):
            put(p_out, tile, jnp.where(ends, skipped(tile, rows_p), 0) + k, part[k])
        for k in range(rows_s):
            put(s_out, tile, jnp.where(ends, skipped(tile, rows_s), 0) + k, part[rows_p + k])

    first, final, late = place == 0, place == RING - 1, place >= RING // 2
    put_all(up, jnp.where(first, -1, ix - 1), True, 8, 7)
    put_all(dn, jnp.where(final, -1, ix + 1), False, 8, 7)
    put_all(across, jnp.where(first, ix - 1, jnp.where(final, ix + 1, -1)), first, 8, 7)
    put_all(far2, jnp.where(late, ix + 2, ix - 2), jnp.logical_not(late), 8, 7)
    put_all(near2, jnp.where(late, ix - 2, ix + 2), late, 6, 5)
    side_rows(((w_out, WIN), (p_out, WIN), (s_out, WIN)), yup, ydn)


def harmonic(own, other):
    return 2.0 * own * other / (own + other)


def jacobi_kernel(info, w_in, p_in, s_in, zup, zdn, out, perm, pa, pb, sc, cxm, cxp, cym, cyp, czm, czp):
    ix, iy, iz = info[0], info[1], info[2]
    here = cut(info, ix)
    count = cut(info, ix + 1) - here
    lane = lax.broadcasted_iota(jnp.int32, (YE, CZ), 1)
    for part, (src, dst) in enumerate(((w_in, perm), (p_in, pa), (s_in, sc))):
        for x in range(WIN):
            dst[x, :, 0:CZ] = src[x]
            dst[x, :, CZ:] = z_halo(part * groups(WIN), x, zup, zdn, lane)

    row = lax.broadcasted_iota(jnp.int32, (YE, 2 * CZ), 0)
    wide = lax.broadcasted_iota(jnp.int32, (YE, 2 * CZ), 1)
    low_y, high_y, left, right = inside_bounds(iy, iz)
    inside = (row >= low_y) & (row < high_y) & ((wide < right) | (wide >= left))
    has_ym = row != low_y
    has_yp = row != high_y - 1
    has_zm = wide != jnp.where(iz == 0, 0, 2 * CZ - LANES)
    has_zp = wide != right - 1

    def couple(q, _):
        g = here + q - DEPTH
        own = perm[q]
        live = inside & (g >= 0) & (g < INSET)
        txm = jnp.where(g > 0, harmonic(own, perm[q - 1]), own)
        txp = jnp.where(g < INSET - 1, harmonic(own, perm[q + 1]), own)
        ty = harmonic(own, pltpu.roll(own, 1, 0))
        tz = harmonic(own, pltpu.roll(own, 1, 1))
        tym = jnp.where(has_ym, ty, own)
        typ = jnp.where(has_yp, pltpu.roll(ty, YE - 1, 0), own)
        tzm = jnp.where(has_zm, tz, own)
        tzp = jnp.where(has_zp, pltpu.roll(tz, 2 * CZ - 1, 1), own)
        total = txm + txp + tym + typ + tzm + tzp

        def share(has, part):
            return jnp.where(live & has, part / total, 0.0)

        cxm[q] = share(g > 0, txm)
        cxp[q] = share(g < INSET - 1, txp)
        cym[q] = share(has_ym, tym)
        cyp[q] = share(has_yp, typ)
        czm[q] = share(has_zm, tzm)
        czp[q] = share(has_zp, tzp)
        sc[q] = share(True, sc[q])
        return 0

    for q in range(1, WIN - 1):
        couple(q, 0)

    old, new = pa, pb
    for sweep in range(1, JACOBI + 1):
        def plane(q, _, old=old, new=new):
            p = old[q]
            total = sc[q] + cxm[q] * old[q - 1] + cxp[q] * old[q + 1]
            total = total + cym[q] * pltpu.roll(p, 1, 0) + cyp[q] * pltpu.roll(p, YE - 1, 0)
            total = total + czm[q] * pltpu.roll(p, 1, 1) + czp[q] * pltpu.roll(p, 2 * CZ - 1, 1)
            new[q] = total
            return 0

        for q in range(sweep, WIN - sweep):
            plane(q, 0)
        old, new = new, old
    for r in range(MOST):
        out[r] = jnp.where(r < count, old[DEPTH + r, 8 : 8 + CY, 0:CZ], 0.0)


def call(kernel, args, outs, scratch=(), scalars=1, cost=1 << 20):
    smem = pl.BlockSpec(memory_space=pltpu.SMEM)
    vmem = pl.BlockSpec(memory_space=pltpu.VMEM)
    return pl.pallas_call(
        kernel,
        out_shape=[pltpu.VMEM(shape, F32) for shape in outs],
        in_specs=[smem] * scalars + [vmem] * (len(args) - scalars),
        out_specs=[vmem] * len(outs),
        scratch_shapes=[pltpu.VMEM(shape, F32) for shape in scratch],
        compiler_params=pltpu.CompilerParams(vmem_limit_bytes=56 << 20),
        cost_estimate=pl.CostEstimate(flops=64 * cost, transcendentals=0, bytes_accessed=cost),
    )(*args[:scalars], *[pltpu.with_memory_space_constraint(arg, pltpu.VMEM) for arg in args[scalars:]])


def shifted(value, axis, count, by):
    return lax.ppermute(value, axis, [(i, i + by) for i in range(count) if 0 <= i + by < count])


def ringed(value, s):
    return lax.ppermute(value, "gx", [(i, i - i % RING + (i + s) % RING) for i in range(COUNT_X)])


def join_y(plane_counts, parts, yup, ydn, beside=()):
    yup, ydn = shifted(yup, "gy", COUNT_Y, 1), shifted(ydn, "gy", COUNT_Y, -1)
    yup, ydn, beside = lax.optimization_barrier((yup, ydn, beside))
    packed = (sum(groups(planes) for planes in plane_counts) * YE, CZ)

    def join_rows(*refs):
        join_y_kernel(plane_counts, *refs)

    *parts, zup, zdn = call(
        join_rows,
        (*parts, yup, ydn),
        [(planes, YE, CZ) for planes in plane_counts] + [packed, packed],
        scalars=0,
    )
    return beside, (*parts, shifted(zup, "gz", COUNT_Z, 1), shifted(zdn, "gz", COUNT_Z, -1))


def local(noise, kappa_sq, cuts, pressure_init, source):
    spots = jnp.stack([lax.axis_index("gx"), lax.axis_index("gy"), lax.axis_index("gz")]).astype(jnp.int32)
    info = jnp.concatenate([spots, cuts])
    plane = (CY, CZ)
    inner = [(i, i + 1) for i in range(COUNT_X) if (i + 1) % RING]
    outer = [(i, i + 1) for i in range(COUNT_X - 1) if (i + 1) % RING == 0]
    inner_dn, outer_dn = [(j, i) for i, j in inner], [(j, i) for i, j in outer]
    carry, up, dn = call(pick_slab_kernel, (spots, noise, kappa_sq), [(PN, *plane)] * 3)
    press, charge, carry, up, dn = lax.optimization_barrier((pressure_init, source, carry, up, dn))
    halo = (15, *plane)
    t_up, t_dn, far, near2 = call(pick_tile_kernel, (info, press, charge), [halo] * 3 + [(11, *plane)])
    carry = lax.ppermute(carry, "gx", outer + outer_dn)
    up, dn = lax.ppermute(up, "gx", inner), lax.ppermute(dn, "gx", inner_dn)
    t_up, t_dn = lax.ppermute(t_up, "gx", inner), lax.ppermute(t_dn, "gx", inner_dn)
    far = lax.ppermute(far, "gx", [(i, i + (3, 1, -1, -3)[i % RING]) for i in range(COUNT_X)])
    steps = [(i, i + (RING, RING, -RING, -RING)[i % RING]) for i in range(COUNT_X)]
    across = lax.ppermute(far, "gx", [(i, to) for i, to in steps if 0 <= to < COUNT_X])
    near2 = ringed(near2, 2)
    carry, near2 = lax.optimization_barrier((carry, near2))
    n, k, yup, ydn = call(
        join_slab_kernel,
        (spots, noise, kappa_sq, carry, up, dn),
        [(NPL, *plane), (KPL, *plane), (NPL + KPL, 8, CZ), (NPL + KPL, 8, CZ)],
    )
    (t_up, t_dn), (n, k, zup, zdn) = join_y((NPL, KPL), (n, k), yup, ydn, (t_up, t_dn))
    big = (NPL, YE, 2 * CZ)
    field, perm, extra = call(
        chebyshev_kernel,
        (info, n, k, zup, zdn),
        [(CX, *plane), (CX, *plane), (CX // 2, *plane)],
        [big, (KPL, YE, 2 * CZ), big, big, (CX, YE, 2 * CZ)],
        cost=1 << 20,
    )
    moved = lax.ppermute(perm, "gx", ACROSS)
    extra = lax.ppermute(extra, "gx", [EARLY_EXTRA, LATE_EXTRA])
    extra, across = lax.optimization_barrier((extra, across))
    far2 = lax.ppermute(across, "gx", [(i, i ^ 1) for i in range(COUNT_X)])
    rings = call(ring_kernel, (info, perm, moved), [(CX, *plane)] * (RING - 1))
    rings = [ringed(value, s) for s, value in enumerate(rings, 1)]
    rows = (3 * WIN, 8, CZ)
    w, p, s, yup, ydn = call(
        join_tile_kernel,
        (info, perm, moved, extra, *rings, pressure_init, source, t_up, t_dn, across, far2, near2),
        [(WIN + 1, *plane)] * 3 + [rows, rows],
    )
    _, (w, p, s, zup, zdn) = join_y((WIN, WIN, WIN), (w, p, s), yup, ydn)
    room = (WIN + 1, YE, 2 * CZ)
    (pressure,) = call(jacobi_kernel, (info, w, p, s, zup, zdn), [(MOST, *plane)], [room] * 10)
    return (field, pressure)


def solution(mesh):
    placed = (P("gx", "gy", "gz"), P("gx", "gy", "gz"), P(), P("gx", "gy", "gz"), P("gx", "gy", "gz"))
    return jax.shard_map(
        local,
        mesh=mesh,
        in_specs=placed,
        out_specs=(P("gx", "gy", "gz"), P("gx", "gy", "gz")),
        check_vma=False,
    )
```

```python
import jax
import jax.numpy as jnp
from jax import lax
from jax.experimental import pallas as pl
from jax.experimental.pallas import tpu as pltpu
from jax.sharding import PartitionSpec as P

SWEEPS = 8
JACOBI = 8
THETA = 7.125
DELTA = 6.875
LOG_GAIN = 2.0

COUNT_X = 16
COUNT_Y = 8
COUNT_Z = 4
CX, CY, CZ = 8, 32, 128
INSET = 96
MOST = 10
DEPTH = 8
WIN = MOST + 2 * DEPTH
NH = SWEEPS - 1
NPL = CX + 2 * NH
KPL = NPL - 2
YE = CY + 16
RING = 4

F32 = jnp.float32


def sweep_weights(count):
    ratio_base = THETA / DELTA
    ratio_now = 1.0 / ratio_base
    weights = []
    for index in range(count):
        ratio_next = 1.0 / (2.0 * ratio_base - ratio_now)
        weights.append((ratio_next * ratio_now, 2.0 * ratio_next / DELTA))
        ratio_now = ratio_next
    return weights


CUTS_AT = 3


def cut(info, tile):
    return info[CUTS_AT + 1 + tile]


def clamp(value, low, high):
    return jnp.minimum(jnp.maximum(value, low), high)


def turn(value, shift, axis):
    shift %= value.shape[axis]
    return value if shift == 0 else pltpu.roll(value, shift, axis)


PN = 2 * NH - 1


def pick_carry_kernel(spots, noise, kappa, carry, sems):
    at = jnp.where(lax.rem(spots[0], RING) == RING - 1, 1, 0)
    from_noise = pltpu.make_async_copy(noise.at[pl.ds((CX - NH) * at, NH)], carry.at[0:NH], sems.at[0])
    from_kappa = pltpu.make_async_copy(kappa.at[pl.ds((CX - NH + 1) * at, NH - 1)], carry.at[NH:PN], sems.at[1])
    from_noise.start()
    from_kappa.start()
    from_noise.wait()
    from_kappa.wait()


def pick_slab_kernel(noise, kappa, up, dn):
    up[0:NH] = noise[CX - NH :]
    dn[0:NH] = noise[:NH]
    up[NH:] = kappa[CX - NH + 1 :]
    dn[NH:] = kappa[: NH - 1]


def pick_tile_kernel(info, press, source, up, dn, far, near2):
    ix = info[0]
    width = cut(info, ix + 1) - cut(info, ix)
    late = lax.rem(ix, RING) >= RING // 2
    for k in range(8):
        last = clamp(width - 8, 0, 2)
        up[k] = press[last + k]
        dn[k] = press[k]
        far[k] = press[jnp.where(late, last, 0) + k]
    for k in range(7):
        last = clamp(width - 7, 0, 3)
        up[8 + k] = source[last + k]
        dn[8 + k] = source[k]
        far[8 + k] = source[jnp.where(late, last, 0) + k]
    for k in range(6):
        near2[k] = press[jnp.where(late, 0, clamp(width - 6, 0, 4)) + k]
    for k in range(5):
        near2[6 + k] = source[jnp.where(late, 0, clamp(width - 5, 0, 5)) + k]


def side_rows(parts, yup, ydn):
    at = 0
    for part, planes in parts:
        for x in range(planes):
            yup[at] = part[x, CY - 8 :]
            ydn[at] = part[x, 0:8]
            at += 1


def join_slab_kernel(spots, noise, kappa, carry, up, dn, n_out, k_out, yup, ydn):
    place = lax.rem(spots[0], RING)
    h = NH - 1
    n_out[NH : NH + CX] = noise[...]
    k_out[h : h + CX] = kappa[...]
    for at_n, at_k, end, inner in ((0, 0, 0, up), (NH + CX, h + CX, RING - 1, dn)):
        @pl.when(place == end)
        def _(at_n=at_n, at_k=at_k):
            n_out[at_n : at_n + NH] = carry[0:NH]
            k_out[at_k : at_k + h] = carry[NH:]

        @pl.when(place != end)
        def _(at_n=at_n, at_k=at_k, inner=inner):
            n_out[at_n : at_n + NH] = inner[0:NH]
            k_out[at_k : at_k + h] = inner[NH:]

    side_rows(((n_out, NPL), (k_out, KPL)), yup, ydn)


LANES = 8
EACH = CZ // LANES


def groups(planes):
    return -(-planes // EACH)


def join_y_kernel(plane_counts, *refs):
    count = len(plane_counts)
    sources, (yup, ydn), outs, (zup, zdn) = refs[:count], refs[count : count + 2], refs[count + 2 : -2], refs[-2:]
    lane = lax.broadcasted_iota(jnp.int32, (YE, CZ), 1)
    at, begin = 0, 0
    for source, out, planes in zip(sources, outs, plane_counts):
        for x in range(planes):
            out[x, 0:8] = yup[at]
            out[x, 8 : 8 + CY] = source[x]
            out[x, 8 + CY :] = ydn[at]
            at += 1
        for g in range(groups(planes)):
            up = jnp.zeros((YE, CZ), F32)
            dn = jnp.zeros((YE, CZ), F32)
            for k in range(min(EACH, planes - g * EACH)):
                value = out[g * EACH + k]
                here = (lane >= LANES * k) & (lane < LANES * (k + 1))
                up = jnp.where(here, turn(value, LANES * (k + 1), 1), up)
                dn = jnp.where(here, turn(value, LANES * k, 1), dn)
            zup[begin : begin + YE] = up
            zdn[begin : begin + YE] = dn
            begin += YE


def z_halo(start, x, zup, zdn, lane):
    begin = (start + x // EACH) * YE
    k = x % EACH
    above = turn(zdn[begin : begin + YE], -LANES * k, 1)
    below = turn(zup[begin : begin + YE], -LANES * (k + 1), 1)
    return jnp.where(lane < LANES, above, jnp.where(lane >= CZ - LANES, below, 0.0))


def inside_bounds(iy, iz):
    low_y = jnp.where(iy == 0, 8, 0)
    high_y = jnp.where(iy == COUNT_Y - 1, 8 + CY, YE)
    left = jnp.where(iz == 0, 2 * CZ, 2 * CZ - LANES)
    right = jnp.where(iz == COUNT_Z - 1, CZ, CZ + LANES)
    return low_y, high_y, left, right


def chebyshev_kernel(info, n_in, k_in, zup, zdn, field, perm, extra, resid, kap, da, db, acc):
    ix, iy, iz = info[0], info[1], info[2]
    lane = lax.broadcasted_iota(jnp.int32, (YE, CZ), 1)
    for x in range(NPL):
        resid[x, :, 0:CZ] = n_in[x]
        resid[x, :, CZ:] = z_halo(0, x, zup, zdn, lane)
    for x in range(KPL):
        kap[x, :, 0:CZ] = k_in[x] + 6.0
        kap[x, :, CZ:] = z_halo(groups(NPL), x, zup, zdn, lane) + 6.0
    row = lax.broadcasted_iota(jnp.int32, (YE, 2 * CZ), 0)
    wide = lax.broadcasted_iota(jnp.int32, (YE, 2 * CZ), 1)
    low_y, high_y, left, right = inside_bounds(iy, iz)
    inside = (row >= low_y) & (row < high_y) & ((wide < right) | (wide >= left))
    mask = jnp.where(inside, 1.0, 0.0).astype(F32)

    def first(x, _):
        da[x] = resid[x] / THETA
        return 0

    for x in range(NPL):
        first(x, 0)
    own = (slice(8, 8 + CY), slice(0, CZ))
    for x in range(CX):
        acc[x] = da[NH + x, *own]
    old, new = da, db
    for k, (a, b) in enumerate(sweep_weights(SWEEPS)[: SWEEPS - 1], 1):
        last = k == SWEEPS - 1
        ys, zs = own if last else (slice(None), slice(None))
        for x in range(k, NPL - k):
            d = old[x]
            beside = old[x + 1, ys, zs] + old[x - 1, ys, zs]
            beside = beside + (pltpu.roll(d, YE - 1, 0)[ys, zs] + pltpu.roll(d, 1, 0)[ys, zs])
            beside = beside + (pltpu.roll(d, 2 * CZ - 1, 1)[ys, zs] + pltpu.roll(d, 1, 1)[ys, zs])
            d = d[ys, zs]
            r = resid[x, ys, zs] - (kap[x - 1, ys, zs] * d - beside)
            if last:
                acc[x - NH] += a * d + b * r
                continue
            resid[x] = r
            at = ix * CX - NH + x
            scale = jnp.where((at >= 0) & (at < CX * COUNT_X), b, 0.0).astype(F32)
            new[x] = a * d + (scale * mask) * r
        if not last:
            for x in range(CX):
                acc[x] += new[NH + x, *own]
        old, new = new, old
    for x in range(CX):
        value = acc[x]
        field[x] = value
        perm[x] = jnp.exp(LOG_GAIN * value)
    half = jnp.where(ix == LATE_EXTRA[0], CX // 2, 0)
    for r in range(CX // 2):
        extra[r] = perm[half + r]


ACROSS = [(4, 0), (5, 1), (8, 4), (9, 5), (12, 8), (3, 7), (6, 10), (7, 11), (10, 14), (11, 15)]
EARLY_EXTRA, LATE_EXTRA = (6, 3), (9, 12)


def window(info, tile):
    first = info[CUTS_AT]
    return first + cut(info, tile) - DEPTH, first + cut(info, tile + 1) + DEPTH - 1


def ring_plane(info, tile, device, r):
    low, high = window(info, tile)
    above = (device + RING) * CX + r <= high
    below = (device - RING) * CX + r >= low
    return above, below


def ring_kernel(info, own, moved, *outs):
    ix = info[0]
    place = lax.rem(ix, RING)
    for s, out in enumerate(outs, 1):
        tile = ix - place + lax.rem(place + s, RING)
        for r in range(CX):
            above, below = ring_plane(info, tile, ix, r)
            out[r] = jnp.where(above | below, moved[r], own[r])


def join_tile_kernel(info, own, moved, extra, ring1, ring2, ring3, press, source, up, dn, across, far2, near2, w_out, p_out, s_out, yup, ydn):
    ix = info[0]
    place = lax.rem(ix, RING)
    here = cut(info, ix)
    w_out[...] = jnp.ones_like(w_out)
    p_out[...] = jnp.zeros_like(p_out)
    s_out[...] = jnp.zeros_like(s_out)
    for s, ring in enumerate((own, ring1, ring2, ring3)):
        device = ix - place + lax.rem(place + RING - s, RING)
        direct_above = (ix == EARLY_EXTRA[1]) & (device + RING == EARLY_EXTRA[0])
        direct_below = (ix == LATE_EXTRA[1]) & (device - RING == LATE_EXTRA[0])
        for r in range(CX):
            above, below = ring_plane(info, ix, device, r)
            value = ring[r]
            if s == 0:
                value = jnp.where(above | below, moved[r], value)
            direct = (above & direct_above) | (below & direct_below)
            value = jnp.where(direct, extra[r % (CX // 2)], value)
            at = device + jnp.where(above, RING, jnp.where(below, -RING, 0))
            g = at * CX + r - info[CUTS_AT]
            q = g - here + DEPTH
            good = (g >= 0) & (g < INSET) & (q >= 0) & (q < WIN)
            w_out[jnp.where(good, q, WIN)] = value

    def put(out, tile, row, value):
        known = (tile >= 0) & (tile < COUNT_X)
        safe = clamp(tile, 0, COUNT_X - 1)
        begin, end = cut(info, safe), cut(info, safe + 1)
        at = begin + row - here + DEPTH
        good = known & (begin + row < end) & (at >= 0) & (at < WIN)
        out[jnp.where(good, at, WIN)] = value

    def skipped(tile, kept):
        safe = clamp(tile, 0, COUNT_X - 1)
        return jnp.maximum(cut(info, safe + 1) - cut(info, safe) - kept, 0)

    for k in range(MOST):
        put(p_out, ix, k, press[k])
        put(s_out, ix, k, source[k])
    def put_all(part, tile, ends, rows_p, rows_s):
        for k in range(rows_p):
            put(p_out, tile, jnp.where(ends, skipped(tile, rows_p), 0) + k, part[k])
        for k in range(rows_s):
            put(s_out, tile, jnp.where(ends, skipped(tile, rows_s), 0) + k, part[rows_p + k])

    first, final, late = place == 0, place == RING - 1, place >= RING // 2
    put_all(up, jnp.where(first, -1, ix - 1), True, 8, 7)
    put_all(dn, jnp.where(final, -1, ix + 1), False, 8, 7)
    put_all(across, jnp.where(first, ix - 1, jnp.where(final, ix + 1, -1)), first, 8, 7)
    put_all(far2, jnp.where(late, ix + 2, ix - 2), jnp.logical_not(late), 8, 7)
    put_all(near2, jnp.where(late, ix - 2, ix + 2), late, 6, 5)
    side_rows(((w_out, WIN), (p_out, WIN), (s_out, WIN)), yup, ydn)


def harmonic(own, other):
    return 2.0 * own * other / (own + other)


def jacobi_kernel(info, w_in, p_in, s_in, zup, zdn, out, perm, pa, pb, sc, cxm, cxp, cym, cyp, czm, czp):
    ix, iy, iz = info[0], info[1], info[2]
    here = cut(info, ix)
    count = cut(info, ix + 1) - here
    lane = lax.broadcasted_iota(jnp.int32, (YE, CZ), 1)
    for part, (src, dst) in enumerate(((w_in, perm), (p_in, pa), (s_in, sc))):
        for x in range(WIN):
            dst[x, :, 0:CZ] = src[x]
            dst[x, :, CZ:] = z_halo(part * groups(WIN), x, zup, zdn, lane)

    row = lax.broadcasted_iota(jnp.int32, (YE, 2 * CZ), 0)
    wide = lax.broadcasted_iota(jnp.int32, (YE, 2 * CZ), 1)
    low_y, high_y, left, right = inside_bounds(iy, iz)
    inside = (row >= low_y) & (row < high_y) & ((wide < right) | (wide >= left))
    has_ym = row != low_y
    has_yp = row != high_y - 1
    has_zm = wide != jnp.where(iz == 0, 0, 2 * CZ - LANES)
    has_zp = wide != right - 1

    def couple(q, _):
        g = here + q - DEPTH
        own = perm[q]
        live = inside & (g >= 0) & (g < INSET)
        txm = jnp.where(g > 0, harmonic(own, perm[q - 1]), own)
        txp = jnp.where(g < INSET - 1, harmonic(own, perm[q + 1]), own)
        ty = harmonic(own, pltpu.roll(own, 1, 0))
        tz = harmonic(own, pltpu.roll(own, 1, 1))
        tym = jnp.where(has_ym, ty, own)
        typ = jnp.where(has_yp, pltpu.roll(ty, YE - 1, 0), own)
        tzm = jnp.where(has_zm, tz, own)
        tzp = jnp.where(has_zp, pltpu.roll(tz, 2 * CZ - 1, 1), own)
        total = txm + txp + tym + typ + tzm + tzp

        inv = 1.0 / total

        def share(has, part):
            return jnp.where(live & has, part * inv, 0.0)

        cxm[q] = share(g > 0, txm)
        cxp[q] = share(g < INSET - 1, txp)
        cym[q] = share(has_ym, tym)
        cyp[q] = share(has_yp, typ)
        czm[q] = share(has_zm, tzm)
        czp[q] = share(has_zp, tzp)
        sc[q] = share(True, sc[q])
        return 0

    for q in range(1, WIN - 1):
        couple(q, 0)

    old, new = pa, pb
    for sweep in range(1, JACOBI + 1):
        last = sweep == JACOBI
        ys, zs = (slice(8, 8 + CY), slice(0, CZ)) if last else (slice(None), slice(None))
        for q in range(sweep, WIN - sweep):
            p = old[q]
            total = sc[q, ys, zs] + cxm[q, ys, zs] * old[q - 1, ys, zs] + cxp[q, ys, zs] * old[q + 1, ys, zs]
            total = total + cym[q, ys, zs] * pltpu.roll(p, 1, 0)[ys, zs] + cyp[q, ys, zs] * pltpu.roll(p, YE - 1, 0)[ys, zs]
            total = total + czm[q, ys, zs] * pltpu.roll(p, 1, 1)[ys, zs] + czp[q, ys, zs] * pltpu.roll(p, 2 * CZ - 1, 1)[ys, zs]
            if last:
                out[q - DEPTH] = jnp.where(q - DEPTH < count, total, 0.0)
            else:
                new[q] = total
        old, new = new, old


def call(kernel, args, outs, scratch=(), scalars=1, cost=1 << 20):
    smem = pl.BlockSpec(memory_space=pltpu.SMEM)
    vmem = pl.BlockSpec(memory_space=pltpu.VMEM)
    return pl.pallas_call(
        kernel,
        out_shape=[pltpu.VMEM(shape, F32) for shape in outs],
        in_specs=[smem] * scalars + [vmem] * (len(args) - scalars),
        out_specs=[vmem] * len(outs),
        scratch_shapes=[pltpu.VMEM(shape, F32) for shape in scratch],
        compiler_params=pltpu.CompilerParams(vmem_limit_bytes=56 << 20),
        cost_estimate=pl.CostEstimate(flops=64 * cost, transcendentals=0, bytes_accessed=cost),
    )(*args[:scalars], *[pltpu.with_memory_space_constraint(arg, pltpu.VMEM) for arg in args[scalars:]])


def shifted(value, axis, count, by):
    return lax.ppermute(value, axis, [(i, i + by) for i in range(count) if 0 <= i + by < count])


def ringed(value, s):
    return lax.ppermute(value, "gx", [(i, i - i % RING + (i + s) % RING) for i in range(COUNT_X)])


def join_y(plane_counts, parts, yup, ydn, beside=()):
    yup, ydn = shifted(yup, "gy", COUNT_Y, 1), shifted(ydn, "gy", COUNT_Y, -1)
    yup, ydn, beside = lax.optimization_barrier((yup, ydn, beside))
    packed = (sum(groups(planes) for planes in plane_counts) * YE, CZ)

    def join_rows(*refs):
        join_y_kernel(plane_counts, *refs)

    *parts, zup, zdn = call(
        join_rows,
        (*parts, yup, ydn),
        [(planes, YE, CZ) for planes in plane_counts] + [packed, packed],
        scalars=0,
    )
    return beside, (*parts, shifted(zup, "gz", COUNT_Z, 1), shifted(zdn, "gz", COUNT_Z, -1))


def local(noise, kappa_sq, cuts, pressure_init, source):
    spots = jnp.stack([lax.axis_index("gx"), lax.axis_index("gy"), lax.axis_index("gz")]).astype(jnp.int32)
    info = jnp.concatenate([spots, cuts])
    plane = (CY, CZ)
    inner = [(i, i + 1) for i in range(COUNT_X) if (i + 1) % RING]
    outer = [(i, i + 1) for i in range(COUNT_X - 1) if (i + 1) % RING == 0]
    inner_dn, outer_dn = [(j, i) for i, j in inner], [(j, i) for i, j in outer]
    carry = pl.pallas_call(
        pick_carry_kernel,
        out_shape=pltpu.VMEM((PN, *plane), F32),
        in_specs=[pl.BlockSpec(memory_space=pltpu.SMEM)] + [pl.BlockSpec(memory_space=pl.ANY)] * 2,
        out_specs=pl.BlockSpec(memory_space=pltpu.VMEM),
        scratch_shapes=[pltpu.SemaphoreType.DMA((2,))],
    )(spots, noise, kappa_sq)
    slab_noise, slab_kappa, carry = lax.optimization_barrier((noise, kappa_sq, carry))
    up, dn = call(pick_slab_kernel, (slab_noise, slab_kappa), [(PN, *plane)] * 2, scalars=0)
    press, charge, carry, up, dn = lax.optimization_barrier((pressure_init, source, carry, up, dn))
    halo = (15, *plane)
    t_up, t_dn, far, near2 = call(pick_tile_kernel, (info, press, charge), [halo] * 3 + [(11, *plane)])
    carry = lax.ppermute(carry, "gx", outer + outer_dn)
    up, dn = lax.ppermute(up, "gx", inner), lax.ppermute(dn, "gx", inner_dn)
    t_up, t_dn = lax.ppermute(t_up, "gx", inner), lax.ppermute(t_dn, "gx", inner_dn)
    far = lax.ppermute(far, "gx", [(i, i + (3, 1, -1, -3)[i % RING]) for i in range(COUNT_X)])
    steps = [(i, i + (RING, RING, -RING, -RING)[i % RING]) for i in range(COUNT_X)]
    across = lax.ppermute(far, "gx", [(i, to) for i, to in steps if 0 <= to < COUNT_X])
    near2 = ringed(near2, 2)
    carry, near2 = lax.optimization_barrier((carry, near2))
    n, k, yup, ydn = call(
        join_slab_kernel,
        (spots, noise, kappa_sq, carry, up, dn),
        [(NPL, *plane), (KPL, *plane), (NPL + KPL, 8, CZ), (NPL + KPL, 8, CZ)],
    )
    (t_up, t_dn), (n, k, zup, zdn) = join_y((NPL, KPL), (n, k), yup, ydn, (t_up, t_dn))
    big = (NPL, YE, 2 * CZ)
    field, perm, extra = call(
        chebyshev_kernel,
        (info, n, k, zup, zdn),
        [(CX, *plane), (CX, *plane), (CX // 2, *plane)],
        [big, (KPL, YE, 2 * CZ), big, big, (CX, *plane)],
        cost=1 << 20,
    )
    moved = lax.ppermute(perm, "gx", ACROSS)
    extra = lax.ppermute(extra, "gx", [EARLY_EXTRA, LATE_EXTRA])
    extra, across = lax.optimization_barrier((extra, across))
    far2 = lax.ppermute(across, "gx", [(i, i ^ 1) for i in range(COUNT_X)])
    rings = call(ring_kernel, (info, perm, moved), [(CX, *plane)] * (RING - 1))
    rings = [ringed(value, s) for s, value in enumerate(rings, 1)]
    rows = (3 * WIN, 8, CZ)
    w, p, s, yup, ydn = call(
        join_tile_kernel,
        (info, perm, moved, extra, *rings, pressure_init, source, t_up, t_dn, across, far2, near2),
        [(WIN + 1, *plane)] * 3 + [rows, rows],
    )
    _, (w, p, s, zup, zdn) = join_y((WIN, WIN, WIN), (w, p, s), yup, ydn)
    room = (WIN + 1, YE, 2 * CZ)
    (pressure,) = call(jacobi_kernel, (info, w, p, s, zup, zdn), [(MOST, *plane)], [room] * 10)
    return (field, pressure)


def solution(mesh):
    placed = (P("gx", "gy", "gz"), P("gx", "gy", "gz"), P(), P("gx", "gy", "gz"), P("gx", "gy", "gz"))
    return jax.shard_map(
        local,
        mesh=mesh,
        in_specs=placed,
        out_specs=(P("gx", "gy", "gz"), P("gx", "gy", "gz")),
        check_vma=False,
    )
```

```python
import jax
import jax.numpy as jnp
from jax import lax
from jax.experimental import pallas as pl
from jax.experimental.pallas import tpu as pltpu
from jax.sharding import PartitionSpec as P

SWEEPS = 8
JACOBI = 8
THETA = 7.125
DELTA = 6.875
LOG_GAIN = 2.0

COUNT_X = 16
COUNT_Y = 8
COUNT_Z = 4
CX, CY, CZ = 8, 32, 128
INSET = 96
MOST = 10
DEPTH = 8
WIN = MOST + 2 * DEPTH
NH = SWEEPS - 1
NPL = CX + 2 * NH
KPL = NPL - 2
YE = CY + 16
RING = 4

F32 = jnp.float32


def sweep_weights(count):
    ratio_base = THETA / DELTA
    ratio_now = 1.0 / ratio_base
    weights = []
    for index in range(count):
        ratio_next = 1.0 / (2.0 * ratio_base - ratio_now)
        weights.append((ratio_next * ratio_now, 2.0 * ratio_next / DELTA))
        ratio_now = ratio_next
    return weights


CUTS_AT = 3


def cut(info, tile):
    return info[CUTS_AT + 1 + tile]


def clamp(value, low, high):
    return jnp.minimum(jnp.maximum(value, low), high)


def turn(value, shift, axis):
    shift %= value.shape[axis]
    return value if shift == 0 else pltpu.roll(value, shift, axis)


PN = 2 * NH - 1


def pick_carry_kernel(spots, noise, kappa, carry, sems):
    at = jnp.where(lax.rem(spots[0], RING) == RING - 1, 1, 0)
    from_noise = pltpu.make_async_copy(noise.at[pl.ds((CX - NH) * at, NH)], carry.at[0:NH], sems.at[0])
    from_kappa = pltpu.make_async_copy(kappa.at[pl.ds((CX - NH + 1) * at, NH - 1)], carry.at[NH:PN], sems.at[1])
    from_noise.start()
    from_kappa.start()
    from_noise.wait()
    from_kappa.wait()


def pick_slab_kernel(noise, kappa, up, dn):
    up[0:NH] = noise[CX - NH :]
    dn[0:NH] = noise[:NH]
    up[NH:] = kappa[CX - NH + 1 :]
    dn[NH:] = kappa[: NH - 1]


def pick_tile_kernel(info, press, source, up, dn, far, near2):
    ix = info[0]
    width = cut(info, ix + 1) - cut(info, ix)
    late = lax.rem(ix, RING) >= RING // 2
    for k in range(8):
        last = clamp(width - 8, 0, 2)
        up[k] = press[last + k]
        dn[k] = press[k]
        far[k] = press[jnp.where(late, last, 0) + k]
    for k in range(7):
        last = clamp(width - 7, 0, 3)
        up[8 + k] = source[last + k]
        dn[8 + k] = source[k]
        far[8 + k] = source[jnp.where(late, last, 0) + k]
    for k in range(6):
        near2[k] = press[jnp.where(late, 0, clamp(width - 6, 0, 4)) + k]
    for k in range(5):
        near2[6 + k] = source[jnp.where(late, 0, clamp(width - 5, 0, 5)) + k]


def side_rows(parts, yup, ydn):
    at = 0
    for part, planes in parts:
        for x in range(planes):
            yup[at] = part[x, CY - 8 :]
            ydn[at] = part[x, 0:8]
            at += 1


def join_slab_kernel(spots, noise, kappa, carry, up, dn, n_out, k_out, yup, ydn):
    place = lax.rem(spots[0], RING)
    h = NH - 1
    n_out[NH : NH + CX] = noise[...]
    k_out[h : h + CX] = kappa[...]
    for at_n, at_k, end, inner in ((0, 0, 0, up), (NH + CX, h + CX, RING - 1, dn)):
        @pl.when(place == end)
        def _(at_n=at_n, at_k=at_k):
            n_out[at_n : at_n + NH] = carry[0:NH]
            k_out[at_k : at_k + h] = carry[NH:]

        @pl.when(place != end)
        def _(at_n=at_n, at_k=at_k, inner=inner):
            n_out[at_n : at_n + NH] = inner[0:NH]
            k_out[at_k : at_k + h] = inner[NH:]

    side_rows(((n_out, NPL), (k_out, KPL)), yup, ydn)


LANES = 8
EACH = CZ // LANES


def groups(planes):
    return -(-planes // EACH)


def join_y_kernel(plane_counts, *refs):
    count = len(plane_counts)
    sources, (yup, ydn), outs, (zup, zdn) = refs[:count], refs[count : count + 2], refs[count + 2 : -2], refs[-2:]
    lane = lax.broadcasted_iota(jnp.int32, (YE, CZ), 1)
    at, begin = 0, 0
    for source, out, planes in zip(sources, outs, plane_counts):
        for x in range(planes):
            out[x, 0:8] = yup[at]
            out[x, 8 : 8 + CY] = source[x]
            out[x, 8 + CY :] = ydn[at]
            at += 1
        for g in range(groups(planes)):
            up = jnp.zeros((YE, CZ), F32)
            dn = jnp.zeros((YE, CZ), F32)
            for k in range(min(EACH, planes - g * EACH)):
                value = out[g * EACH + k]
                here = (lane >= LANES * k) & (lane < LANES * (k + 1))
                up = jnp.where(here, turn(value, LANES * (k + 1), 1), up)
                dn = jnp.where(here, turn(value, LANES * k, 1), dn)
            zup[begin : begin + YE] = up
            zdn[begin : begin + YE] = dn
            begin += YE


def z_halo(start, x, zup, zdn, lane):
    begin = (start + x // EACH) * YE
    k = x % EACH
    above = turn(zdn[begin : begin + YE], -LANES * k, 1)
    below = turn(zup[begin : begin + YE], -LANES * (k + 1), 1)
    return jnp.where(lane < LANES, above, jnp.where(lane >= CZ - LANES, below, 0.0))


def inside_bounds(iy, iz):
    low_y = jnp.where(iy == 0, 8, 0)
    high_y = jnp.where(iy == COUNT_Y - 1, 8 + CY, YE)
    left = jnp.where(iz == 0, 2 * CZ, 2 * CZ - LANES)
    right = jnp.where(iz == COUNT_Z - 1, CZ, CZ + LANES)
    return low_y, high_y, left, right


def chebyshev_kernel(info, n_in, k_in, zup, zdn, field, perm, extra, resid, kap, da, db, acc):
    ix, iy, iz = info[0], info[1], info[2]
    lane = lax.broadcasted_iota(jnp.int32, (YE, CZ), 1)
    for x in range(NPL):
        resid[x, :, 0:CZ] = n_in[x]
        resid[x, :, CZ:] = z_halo(0, x, zup, zdn, lane)
    for x in range(KPL):
        kap[x, :, 0:CZ] = k_in[x] + 6.0
        kap[x, :, CZ:] = z_halo(groups(NPL), x, zup, zdn, lane) + 6.0
    row = lax.broadcasted_iota(jnp.int32, (YE, 2 * CZ), 0)
    wide = lax.broadcasted_iota(jnp.int32, (YE, 2 * CZ), 1)
    low_y, high_y, left, right = inside_bounds(iy, iz)
    inside = (row >= low_y) & (row < high_y) & ((wide < right) | (wide >= left))
    mask = jnp.where(inside, 1.0, 0.0).astype(F32)

    def first(x, _):
        da[x] = resid[x] / THETA
        return 0

    for x in range(NPL):
        first(x, 0)
    own = (slice(8, 8 + CY), slice(0, CZ))
    for x in range(CX):
        acc[x] = da[NH + x, *own]
    old, new = da, db
    for k, (a, b) in enumerate(sweep_weights(SWEEPS)[: SWEEPS - 1], 1):
        last = k == SWEEPS - 1
        ys, zs = own if last else (slice(None), slice(None))
        for x in range(k, NPL - k):
            d = old[x]
            beside = old[x + 1, ys, zs] + old[x - 1, ys, zs]
            beside = beside + (pltpu.roll(d, YE - 1, 0)[ys, zs] + pltpu.roll(d, 1, 0)[ys, zs])
            beside = beside + (pltpu.roll(d, 2 * CZ - 1, 1)[ys, zs] + pltpu.roll(d, 1, 1)[ys, zs])
            d = d[ys, zs]
            r = resid[x, ys, zs] - (kap[x - 1, ys, zs] * d - beside)
            if last:
                acc[x - NH] += a * d + b * r
                continue
            resid[x] = r
            at = ix * CX - NH + x
            scale = jnp.where((at >= 0) & (at < CX * COUNT_X), b, 0.0).astype(F32)
            new[x] = a * d + (scale * mask) * r
        if not last:
            for x in range(CX):
                acc[x] += new[NH + x, *own]
        old, new = new, old
    for x in range(CX):
        value = acc[x]
        field[x] = value
        perm[x] = jnp.exp(LOG_GAIN * value)
    half = jnp.where(ix == LATE_EXTRA[0], CX // 2, 0)
    for r in range(CX // 2):
        extra[r] = perm[half + r]


ACROSS = [(4, 0), (5, 1), (8, 4), (9, 5), (12, 8), (3, 7), (6, 10), (7, 11), (10, 14), (11, 15)]
EARLY_EXTRA, LATE_EXTRA = (6, 3), (9, 12)


def window(info, tile):
    first = info[CUTS_AT]
    return first + cut(info, tile) - DEPTH, first + cut(info, tile + 1) + DEPTH - 1


def ring_plane(info, tile, device, r):
    low, high = window(info, tile)
    above = (device + RING) * CX + r <= high
    below = (device - RING) * CX + r >= low
    return above, below


def ring_kernel(info, own, moved, *outs):
    ix = info[0]
    place = lax.rem(ix, RING)
    for s, out in enumerate(outs, 1):
        tile = ix - place + lax.rem(place + s, RING)
        for r in range(CX):
            above, below = ring_plane(info, tile, ix, r)
            out[r] = jnp.where(above | below, moved[r], own[r])


def join_tile_kernel(info, own, moved, extra, ring2, ring1, ring3, press, source, up, dn, across, far2, near2, w_out, p_out, s_out, yup, ydn):
    ix = info[0]
    place = lax.rem(ix, RING)
    here = cut(info, ix)
    w_out[...] = jnp.ones_like(w_out)
    p_out[...] = jnp.zeros_like(p_out)
    s_out[...] = jnp.zeros_like(s_out)
    for s, ring in enumerate((own, ring1, ring2, ring3)):
        device = ix - place + lax.rem(place + RING - s, RING)
        direct_above = (ix == EARLY_EXTRA[1]) & (device + RING == EARLY_EXTRA[0])
        direct_below = (ix == LATE_EXTRA[1]) & (device - RING == LATE_EXTRA[0])
        for r in range(CX):
            above, below = ring_plane(info, ix, device, r)
            value = ring[r]
            if s == 0:
                value = jnp.where(above | below, moved[r], value)
            direct = (above & direct_above) | (below & direct_below)
            value = jnp.where(direct, extra[r % (CX // 2)], value)
            at = device + jnp.where(above, RING, jnp.where(below, -RING, 0))
            g = at * CX + r - info[CUTS_AT]
            q = g - here + DEPTH
            good = (g >= 0) & (g < INSET) & (q >= 0) & (q < WIN)
            w_out[jnp.where(good, q, WIN)] = value

    def put(out, tile, row, value):
        known = (tile >= 0) & (tile < COUNT_X)
        safe = clamp(tile, 0, COUNT_X - 1)
        begin, end = cut(info, safe), cut(info, safe + 1)
        at = begin + row - here + DEPTH
        good = known & (begin + row < end) & (at >= 0) & (at < WIN)
        out[jnp.where(good, at, WIN)] = value

    def skipped(tile, kept):
        safe = clamp(tile, 0, COUNT_X - 1)
        return jnp.maximum(cut(info, safe + 1) - cut(info, safe) - kept, 0)

    for k in range(MOST):
        put(p_out, ix, k, press[k])
        put(s_out, ix, k, source[k])
    def put_all(part, tile, ends, rows_p, rows_s):
        for k in range(rows_p):
            put(p_out, tile, jnp.where(ends, skipped(tile, rows_p), 0) + k, part[k])
        for k in range(rows_s):
            put(s_out, tile, jnp.where(ends, skipped(tile, rows_s), 0) + k, part[rows_p + k])

    first, final, late = place == 0, place == RING - 1, place >= RING // 2
    put_all(up, jnp.where(first, -1, ix - 1), True, 8, 7)
    put_all(dn, jnp.where(final, -1, ix + 1), False, 8, 7)
    put_all(across, jnp.where(first, ix - 1, jnp.where(final, ix + 1, -1)), first, 8, 7)
    put_all(far2, jnp.where(late, ix + 2, ix - 2), jnp.logical_not(late), 8, 7)
    put_all(near2, jnp.where(late, ix - 2, ix + 2), late, 6, 5)
    side_rows(((w_out, WIN), (p_out, WIN), (s_out, WIN)), yup, ydn)


def harmonic(own, other):
    return 2.0 * own * other / (own + other)


def jacobi_kernel(info, w_in, p_in, s_in, zup, zdn, out, perm, pa, pb, sc, cxm, cxp, cym, cyp, czm, czp):
    ix, iy, iz = info[0], info[1], info[2]
    here = cut(info, ix)
    count = cut(info, ix + 1) - here
    lane = lax.broadcasted_iota(jnp.int32, (YE, CZ), 1)
    for part, (src, dst) in enumerate(((w_in, perm), (p_in, pa), (s_in, sc))):
        for x in range(WIN):
            dst[x, :, 0:CZ] = src[x]
            dst[x, :, CZ:] = z_halo(part * groups(WIN), x, zup, zdn, lane)

    row = lax.broadcasted_iota(jnp.int32, (YE, 2 * CZ), 0)
    wide = lax.broadcasted_iota(jnp.int32, (YE, 2 * CZ), 1)
    low_y, high_y, left, right = inside_bounds(iy, iz)
    inside = (row >= low_y) & (row < high_y) & ((wide < right) | (wide >= left))
    has_ym = row != low_y
    has_yp = row != high_y - 1
    has_zm = wide != jnp.where(iz == 0, 0, 2 * CZ - LANES)
    has_zp = wide != right - 1

    def couple(q, _):
        g = here + q - DEPTH
        own = perm[q]
        live = inside & (g >= 0) & (g < INSET)
        txm = jnp.where(g > 0, harmonic(own, perm[q - 1]), own)
        txp = jnp.where(g < INSET - 1, harmonic(own, perm[q + 1]), own)
        ty = harmonic(own, pltpu.roll(own, 1, 0))
        tz = harmonic(own, pltpu.roll(own, 1, 1))
        tym = jnp.where(has_ym, ty, own)
        typ = jnp.where(has_yp, pltpu.roll(ty, YE - 1, 0), own)
        tzm = jnp.where(has_zm, tz, own)
        tzp = jnp.where(has_zp, pltpu.roll(tz, 2 * CZ - 1, 1), own)
        total = txm + txp + tym + typ + tzm + tzp

        inv = 1.0 / total

        def share(has, part):
            return jnp.where(live & has, part * inv, 0.0)

        cxm[q] = share(g > 0, txm)
        cxp[q] = share(g < INSET - 1, txp)
        cym[q] = share(has_ym, tym)
        cyp[q] = share(has_yp, typ)
        czm[q] = share(has_zm, tzm)
        czp[q] = share(has_zp, tzp)
        sc[q] = share(True, sc[q])
        return 0

    for q in range(1, WIN - 1):
        couple(q, 0)

    old, new = pa, pb
    for sweep in range(1, JACOBI + 1):
        last = sweep == JACOBI
        ys, zs = (slice(8, 8 + CY), slice(0, CZ)) if last else (slice(None), slice(None))
        for q in range(sweep, WIN - sweep):
            p = old[q]
            total = sc[q, ys, zs] + cxm[q, ys, zs] * old[q - 1, ys, zs] + cxp[q, ys, zs] * old[q + 1, ys, zs]
            total = total + cym[q, ys, zs] * pltpu.roll(p, 1, 0)[ys, zs] + cyp[q, ys, zs] * pltpu.roll(p, YE - 1, 0)[ys, zs]
            total = total + czm[q, ys, zs] * pltpu.roll(p, 1, 1)[ys, zs] + czp[q, ys, zs] * pltpu.roll(p, 2 * CZ - 1, 1)[ys, zs]
            if last:
                out[q - DEPTH] = jnp.where(q - DEPTH < count, total, 0.0)
            else:
                new[q] = total
        old, new = new, old


def call(kernel, args, outs, scratch=(), scalars=1, cost=1 << 20):
    smem = pl.BlockSpec(memory_space=pltpu.SMEM)
    vmem = pl.BlockSpec(memory_space=pltpu.VMEM)
    return pl.pallas_call(
        kernel,
        out_shape=[pltpu.VMEM(shape, F32) for shape in outs],
        in_specs=[smem] * scalars + [vmem] * (len(args) - scalars),
        out_specs=[vmem] * len(outs),
        scratch_shapes=[pltpu.VMEM(shape, F32) for shape in scratch],
        compiler_params=pltpu.CompilerParams(vmem_limit_bytes=56 << 20),
        cost_estimate=pl.CostEstimate(flops=64 * cost, transcendentals=0, bytes_accessed=cost),
    )(*args[:scalars], *[pltpu.with_memory_space_constraint(arg, pltpu.VMEM) for arg in args[scalars:]])


def shifted(value, axis, count, by):
    return lax.ppermute(value, axis, [(i, i + by) for i in range(count) if 0 <= i + by < count])


def ringed(value, s):
    return lax.ppermute(value, "gx", [(i, i - i % RING + (i + s) % RING) for i in range(COUNT_X)])


def join_y(plane_counts, parts, yup, ydn, beside=()):
    yup, ydn = shifted(yup, "gy", COUNT_Y, 1), shifted(ydn, "gy", COUNT_Y, -1)
    yup, ydn, beside = lax.optimization_barrier((yup, ydn, beside))
    packed = (sum(groups(planes) for planes in plane_counts) * YE, CZ)

    def join_rows(*refs):
        join_y_kernel(plane_counts, *refs)

    *parts, zup, zdn = call(
        join_rows,
        (*parts, yup, ydn),
        [(planes, YE, CZ) for planes in plane_counts] + [packed, packed],
        scalars=0,
    )
    return beside, (*parts, shifted(zup, "gz", COUNT_Z, 1), shifted(zdn, "gz", COUNT_Z, -1))


def local(noise, kappa_sq, cuts, pressure_init, source):
    spots = jnp.stack([lax.axis_index("gx"), lax.axis_index("gy"), lax.axis_index("gz")]).astype(jnp.int32)
    info = jnp.concatenate([spots, cuts])
    plane = (CY, CZ)
    inner = [(i, i + 1) for i in range(COUNT_X) if (i + 1) % RING]
    outer = [(i, i + 1) for i in range(COUNT_X - 1) if (i + 1) % RING == 0]
    inner_dn, outer_dn = [(j, i) for i, j in inner], [(j, i) for i, j in outer]
    carry = pl.pallas_call(
        pick_carry_kernel,
        out_shape=pltpu.VMEM((PN, *plane), F32),
        in_specs=[pl.BlockSpec(memory_space=pltpu.SMEM)] + [pl.BlockSpec(memory_space=pl.ANY)] * 2,
        out_specs=pl.BlockSpec(memory_space=pltpu.VMEM),
        scratch_shapes=[pltpu.SemaphoreType.DMA((2,))],
    )(spots, noise, kappa_sq)
    slab_noise, slab_kappa, carry = lax.optimization_barrier((noise, kappa_sq, carry))
    up, dn = call(pick_slab_kernel, (slab_noise, slab_kappa), [(PN, *plane)] * 2, scalars=0)
    press, charge, carry, up, dn = lax.optimization_barrier((pressure_init, source, carry, up, dn))
    halo = (15, *plane)
    t_up, t_dn, far, near2 = call(pick_tile_kernel, (info, press, charge), [halo] * 3 + [(11, *plane)])
    carry = lax.ppermute(carry, "gx", outer + outer_dn)
    up, dn = lax.ppermute(up, "gx", inner), lax.ppermute(dn, "gx", inner_dn)
    t_up, t_dn = lax.ppermute(t_up, "gx", inner), lax.ppermute(t_dn, "gx", inner_dn)
    far = lax.ppermute(far, "gx", [(i, i + (3, 1, -1, -3)[i % RING]) for i in range(COUNT_X)])
    steps = [(i, i + (RING, RING, -RING, -RING)[i % RING]) for i in range(COUNT_X)]
    across = lax.ppermute(far, "gx", [(i, to) for i, to in steps if 0 <= to < COUNT_X])
    near2 = ringed(near2, 2)
    carry, near2 = lax.optimization_barrier((carry, near2))
    n, k, yup, ydn = call(
        join_slab_kernel,
        (spots, noise, kappa_sq, carry, up, dn),
        [(NPL, *plane), (KPL, *plane), (NPL + KPL, 8, CZ), (NPL + KPL, 8, CZ)],
    )
    (t_up, t_dn), (n, k, zup, zdn) = join_y((NPL, KPL), (n, k), yup, ydn, (t_up, t_dn))
    big = (NPL, YE, 2 * CZ)
    field, perm, extra = call(
        chebyshev_kernel,
        (info, n, k, zup, zdn),
        [(CX, *plane), (CX, *plane), (CX // 2, *plane)],
        [big, (KPL, YE, 2 * CZ), big, big, (CX, *plane)],
        cost=1 << 20,
    )
    moved = lax.ppermute(perm, "gx", ACROSS)
    extra = lax.ppermute(extra, "gx", [EARLY_EXTRA, LATE_EXTRA])
    extra, across = lax.optimization_barrier((extra, across))
    far2 = lax.ppermute(across, "gx", [(i, i ^ 1) for i in range(COUNT_X)])
    rings = call(ring_kernel, (info, perm, moved), [(CX, *plane)] * (RING - 1))
    ring2 = ringed(rings[1], 2)
    rings = [ring2, ringed(rings[0], 1), ringed(rings[2], 3)]
    rows = (3 * WIN, 8, CZ)
    w, p, s, yup, ydn = call(
        join_tile_kernel,
        (info, perm, moved, extra, *rings, pressure_init, source, t_up, t_dn, across, far2, near2),
        [(WIN + 1, *plane)] * 3 + [rows, rows],
    )
    _, (w, p, s, zup, zdn) = join_y((WIN, WIN, WIN), (w, p, s), yup, ydn)
    room = (WIN + 1, YE, 2 * CZ)
    (pressure,) = call(jacobi_kernel, (info, w, p, s, zup, zdn), [(MOST, *plane)], [room] * 10)
    return (field, pressure)


def solution(mesh):
    placed = (P("gx", "gy", "gz"), P("gx", "gy", "gz"), P(), P("gx", "gy", "gz"), P("gx", "gy", "gz"))
    return jax.shard_map(
        local,
        mesh=mesh,
        in_specs=placed,
        out_specs=(P("gx", "gy", "gz"), P("gx", "gy", "gz")),
        check_vma=False,
    )
```
